32 devices in a mesh: stream: 16 (over z, y, x), cross: 2 (over core).
Axes of the slice: x: 2, y: 2, z: 4, core: 2. Of those that a mesh axis runs over, the one named last changes fastest.
Arguments:
- source: float32 [128, 16, 128], P('stream', 'cross'), may hold values from -6 to 6
- metric: float32 [16, 2, 16], P('stream', 'cross'), may hold values from 0.5 to 4
- base_velocity: float32 [3, 128, 16, 128], P(None, 'stream', 'cross'), may hold values from -6 to 6
- drop_elem: int32 [16, 2, 5, 128], P('stream', 'cross'), may hold values from 0 to 511, as said below
- drop_coord: float32 [16, 2, 5, 3, 128], P('stream', 'cross'), may hold values from -1 to 1
- drop_vel: float32 [16, 2, 5, 3, 128], P('stream', 'cross'), may hold values from -6 to 6
- drop_prop: float32 [16, 2, 5, 2, 128], P('stream', 'cross'), may hold values from 0.5 to 4
- drop_counts: int32 [16, 2, 5], P('stream', 'cross'), may hold values from 0 to 128, as said below
Outputs:
- pressure: float32 [128, 16, 128], P('stream', 'cross')
- momentum_source: float32 [3, 128, 16, 128], P(None, 'stream', 'cross')
- drop_accel: float32 [16, 2, 5, 3, 128], P('stream', 'cross')
The draws below stay inside these ranges and needn't reach their ends.
Inputs may be any that keep to these rules, and one draw needn't show every extreme that they name: `drop_elem`: elements are numbered (ex * 2 + ey) * 16 + ez. The owner element of every slot of block b of holder (s, c) lies in slab s + b - 2 (streamwise element index from (s + b - 2) * 1 to that plus 1 - 1) and column c (element index from c * 1 to c + 1 - 1); this holds for slots that are not live as well, for blocks whose slab lies in the grid. `drop_counts`: A block whose owner slab s + b - 2 lies outside 0 to 15 has count 0. In every draw some slab of some column receives 128 live droplets from each of its 5 holder slabs.
All inputs are finite; a program needn't handle non-finite values.
Results may differ from the reference program's by a relative error of at most 0.0003.
Values sent between devices are 32-bit elements; how exact they have to be, the bound alone decides.
No kernel may reach another device: no remote copies, remote signals or barrier semaphores. Data moves between devices by JAX's collectives and lax.ppermute only.
A program may use at most 64 MiB of HBM per device.

```python
import math
import jax
import jax.numpy as jnp
import numpy as np
from jax import lax

EX = 1
EY = 1
EZ = 16
CAP = 128
SWEEPS = 3
DRIFT = 2
REACH = 5
SLABS = 16
COLS = 2
EXT = 16
EYT = 2
XT = 128
YT = 16
ZT = 128


def draw_drop_elem(key, part):
    slab_index = jnp.arange(SLABS, dtype=jnp.int32)
    offsets = jnp.arange(REACH, dtype=jnp.int32) - DRIFT
    target = jnp.clip(slab_index[:, None] + offsets[None, :], 0, SLABS - 1)
    shape_all = (SLABS, COLS, REACH, CAP)
    pick_x = jax.random.randint(jax.random.fold_in(key, 11), shape_all, 0, EX)
    pick_y = jax.random.randint(jax.random.fold_in(key, 12), shape_all, 0, EY)
    pick_z = jax.random.randint(jax.random.fold_in(key, 13), shape_all, 0, EZ)
    elem_x = target[:, None, :, None] * EX + pick_x
    col_index = jnp.arange(COLS, dtype=jnp.int32)
    elem_y = col_index[None, :, None, None] * EY + pick_y
    return ((elem_x * EYT + elem_y) * EZ + pick_z).astype(jnp.int32)


def draw_drop_counts(key, part):
    base_counts = jax.random.randint(jax.random.fold_in(key, 21), (SLABS, COLS, REACH), CAP // 3, CAP + 1)
    slab_index = jnp.arange(SLABS, dtype=jnp.int32)
    offsets = jnp.arange(REACH, dtype=jnp.int32) - DRIFT
    owner_slab = slab_index[:, None] + offsets[None, :]
    inside = (owner_slab >= 0) & (owner_slab < SLABS)
    full_slab = jax.random.randint(jax.random.fold_in(key, 22), (), DRIFT, SLABS - DRIFT)
    full_col = jax.random.randint(jax.random.fold_in(key, 23), (), 0, COLS)
    col_index = jnp.arange(COLS, dtype=jnp.int32)
    hit_slab = owner_slab == full_slab
    hit = hit_slab[:, None, :] & (col_index == full_col)[None, :, None]
    counts = jnp.where(hit, CAP, base_counts)
    return jnp.where(inside[:, None, :], counts, 0).astype(jnp.int32)


def steps_of(own_key, dims, shards, low, high):
    def one(position, parts):
        draws = jax.random.uniform(jax.random.fold_in(jax.random.fold_in(own_key, 6), position), (parts,), jnp.float32, low / len(shards), high / len(shards))
        return jnp.repeat(jnp.exp(draws), dims[position] // parts).reshape((-1,) + (1,) * (len(dims) - position - 1))

    factor_of = one(*shards[0])
    for cut in shards[1:]:
        factor_of = factor_of * one(*cut)
    return factor_of


def bell_draw(key, extent, scale, most, split=(), kind=jnp.bfloat16):
    entries = scale * jax.random.normal(key, extent, jnp.float32)
    if split:
        entries = entries * steps_of(key, extent, split, -0.22, 0.18)
    return jnp.clip(entries, -most, most).astype(kind)


def setup_inputs(seed: int = 0) -> dict:
    arg_keys = jax.random.split(jax.random.key(seed), 9)
    source = bell_draw(arg_keys[0], (XT, YT, ZT), 1.0, 6.0, ((0, 16), (1, 2)), jnp.float32)
    metric = jnp.clip(jnp.exp(math.log(4.0) - 2.0794415 * jax.random.uniform(arg_keys[1], (EXT, EYT, EZ), jnp.float32) ** steps_of(arg_keys[1], (EXT, EYT, EZ), ((0, 16), (1, 2)), -0.2, 0.2)), 0.5, 4.0)
    base_velocity = bell_draw(arg_keys[2], (3, XT, YT, ZT), 1.0, 6.0, ((1, 16), (2, 2)), jnp.float32)
    drop_elem = draw_drop_elem(jax.random.fold_in(arg_keys[8], 71), 0)
    drop_coord = jnp.clip(jax.random.uniform(arg_keys[4], (SLABS, COLS, REACH, 3, CAP), jnp.float32, -1.0, 1.0) * steps_of(arg_keys[4], (SLABS, COLS, REACH, 3, CAP), ((0, 16), (1, 2)), -0.4, 0.0), -1.0, 1.0)
    drop_vel = bell_draw(arg_keys[5], (SLABS, COLS, REACH, 3, CAP), 1.0, 6.0, ((0, 16), (1, 2)), jnp.float32)
    drop_prop = jnp.clip(jnp.exp(math.log(4.0) - 2.0794415 * jax.random.uniform(arg_keys[6], (SLABS, COLS, REACH, 2, CAP), jnp.float32) ** steps_of(arg_keys[6], (SLABS, COLS, REACH, 2, CAP), ((0, 16), (1, 2)), -0.2, 0.2)), 0.5, 4.0)
    drop_counts = draw_drop_counts(jax.random.fold_in(arg_keys[8], 71), 0)
    return dict(source=source, metric=metric, base_velocity=base_velocity, drop_elem=drop_elem, drop_coord=drop_coord, drop_vel=drop_vel, drop_prop=drop_prop, drop_counts=drop_counts)


HIGHEST_PREC = lax.Precision.HIGHEST
MASS_SHIFT = 1.0
UPPER_BOUND = 2.5
LOWER_BOUND = UPPER_BOUND / 30.0
GLL_POINTS = [-1.0, -0.8717401485096066, -0.5917001814331423, -0.2092992179024789,
              0.2092992179024789, 0.5917001814331423, 0.8717401485096066, 1.0]


def legendre_seven(points):
    before = points * 0.0 + 1.0
    current = points
    for order in range(1, 7):
        following = ((2.0 * order + 1.0) * points * current - order * before) / (order + 1.0)
        before = current
        current = following
    return current


def outer_three(first, second, third):
    return first[:, None, None] * second[None, :, None] * third[None, None, :]


def gll_tables():
    gll_nodes = np.array(GLL_POINTS)
    values = legendre_seven(gll_nodes)
    weights = 2.0 / (56.0 * values * values)
    deriv_mat = np.zeros((8, 8))
    for row_idx in range(8):
        for col_idx in range(8):
            if row_idx != col_idx:
                deriv_mat[row_idx, col_idx] = values[row_idx] / (values[col_idx] * (gll_nodes[row_idx] - gll_nodes[col_idx]))
    deriv_mat[0, 0] = -14.0
    deriv_mat[7, 7] = 14.0
    return gll_nodes, weights, deriv_mat


def weight_cube():
    gll_nodes, weights, deriv_mat = gll_tables()
    cube_table = outer_three(weights, weights, weights)
    return jnp.asarray(cube_table.reshape(1, 8, 1, 8, 1, 8), jnp.float32)


def split_cells(grid_field):
    size_x, size_y, size_z = grid_field.shape[-3:]
    return grid_field.reshape(grid_field.shape[:-3] + (size_x // 8, 8, size_y // 8, 8, size_z // 8, 8))


def scale_of(metric):
    return metric[:, None, :, None, :, None]


def derivatives(cells):
    gll_nodes, weights, deriv_mat = gll_tables()
    dmat = jnp.asarray(deriv_mat, jnp.float32)
    grad_x = jnp.einsum("ia,xaybzc->xiybzc", dmat, cells, precision=HIGHEST_PREC)
    grad_y = jnp.einsum("jb,xaybzc->xayjzc", dmat, cells, precision=HIGHEST_PREC)
    grad_z = jnp.einsum("kc,xaybzc->xaybzk", dmat, cells, precision=HIGHEST_PREC)
    return grad_x, grad_y, grad_z


def operator_local(grid_field, metric):
    gll_nodes, weights, deriv_mat = gll_tables()
    dmat = jnp.asarray(deriv_mat, jnp.float32)
    cells = split_cells(grid_field)
    wcube = weight_cube()
    grad_x, grad_y, grad_z = derivatives(cells)
    back_x = jnp.einsum("ai,xaybzc->xiybzc", dmat, wcube * grad_x, precision=HIGHEST_PREC)
    back_y = jnp.einsum("bj,xaybzc->xayjzc", dmat, wcube * grad_y, precision=HIGHEST_PREC)
    back_z = jnp.einsum("ck,xaybzc->xaybzk", dmat, wcube * grad_z, precision=HIGHEST_PREC)
    result = scale_of(metric) * (back_x + back_y + back_z) + MASS_SHIFT * wcube * cells
    return result.reshape(grid_field.shape)


def diagonal_local(metric, field_shape):
    gll_nodes, weights, deriv_mat = gll_tables()
    stiff_diag = (deriv_mat * deriv_mat * weights[:, None]).sum(0)
    cube_table = (outer_three(stiff_diag, weights, weights)
                  + outer_three(weights, stiff_diag, weights)
                  + outer_three(weights, weights, stiff_diag))
    stiff_cube = jnp.asarray(cube_table.reshape(1, 8, 1, 8, 1, 8), jnp.float32)
    result = scale_of(metric) * stiff_cube + MASS_SHIFT * weight_cube()
    return result.reshape(field_shape)


def pair_sum(padded, along):
    length = padded.shape[along] - 2
    count = length // 8
    interior = lax.slice_in_dim(padded, 1, length + 1, axis=along)
    before_rows = lax.slice_in_dim(padded, 0, length, 8, along)
    after_rows = lax.slice_in_dim(padded, 9, length + 2, 8, along)
    split_shape = interior.shape[:along] + (count, 8) + interior.shape[along + 1:]
    blocks = interior.reshape(split_shape)
    first_row = lax.slice_in_dim(blocks, 0, 1, axis=along + 1) + jnp.expand_dims(before_rows, along + 1)
    middle = lax.slice_in_dim(blocks, 1, 7, axis=along + 1)
    last_row = lax.slice_in_dim(blocks, 7, 8, axis=along + 1) + jnp.expand_dims(after_rows, along + 1)
    return jnp.concatenate([first_row, middle, last_row], along + 1).reshape(interior.shape)


def assemble(padded):
    first_axis = padded.ndim - 3
    summed = pair_sum(padded, first_axis)
    summed = pair_sum(summed, first_axis + 1)
    pad_width = [(0, 0)] * (summed.ndim - 1) + [(1, 1)]
    return pair_sum(jnp.pad(summed, pad_width), first_axis + 2)


def zero_rim(grid_field):
    pad_width = [(0, 0)] * (grid_field.ndim - 3) + [(1, 1), (1, 1), (0, 0)]
    return jnp.pad(grid_field, pad_width)


def chebyshev(source, metric, summer):
    center = (UPPER_BOUND + LOWER_BOUND) / 2.0
    half_width = (UPPER_BOUND - LOWER_BOUND) / 2.0
    ratio_bound = center / half_width
    cheb_rho = 1.0 / ratio_bound
    cells = split_cells(source)
    right_side = summer((weight_cube() * cells).reshape(source.shape))
    diagonal = summer(diagonal_local(metric, source.shape))
    inv_diag = 1.0 / diagonal
    residual = right_side
    update = inv_diag * residual / center
    iterate = jnp.zeros_like(source)
    for sweep in range(SWEEPS):
        iterate = iterate + update
        residual = residual - summer(operator_local(update, metric))
        rho_next = 1.0 / (2.0 * ratio_bound - cheb_rho)
        update = (rho_next * cheb_rho) * update + (2.0 * rho_next / half_width) * (inv_diag * residual)
        cheb_rho = rho_next
    return iterate + update


def velocity_table(pressure, base_velocity, metric):
    cells = split_cells(pressure)
    grad_x, grad_y, grad_z = derivatives(cells)
    scale_cube = scale_of(metric)
    gradient = jnp.stack([scale_cube * grad_x, scale_cube * grad_y, scale_cube * grad_z], 0)
    velocity = split_cells(base_velocity) - gradient
    velocity = velocity.transpose(1, 3, 5, 0, 2, 4, 6)
    return velocity.reshape(metric.shape[0] * metric.shape[1] * metric.shape[2], 1536)


def table_to_field(source_table, metric):
    elem_x, elem_y, elem_z = metric.shape
    cube = source_table.reshape(elem_x, elem_y, elem_z, 3, 8, 8, 8).transpose(3, 0, 4, 1, 5, 2, 6)
    return cube.reshape(3, 8 * elem_x, 8 * elem_y, 8 * elem_z)


def lagrange(coords):
    gll_nodes, weights, deriv_mat = gll_tables()
    factors = []
    for node_idx in range(8):
        factor = jnp.ones_like(coords)
        for other_idx in range(8):
            if other_idx != node_idx:
                factor = factor * (coords - float(gll_nodes[other_idx])) / float(gll_nodes[node_idx] - gll_nodes[other_idx])
        factors.append(factor)
    return jnp.stack(factors, 0)


def droplet_terms(gathered, drop_state, is_live):
    slot_count = gathered.shape[0]
    basis_r = lagrange(drop_state[0])
    basis_s = lagrange(drop_state[1])
    basis_t = lagrange(drop_state[2])
    partial_value = jnp.einsum("ncijk,kn->ncij", gathered, basis_t, precision=HIGHEST_PREC)
    partial_value = jnp.einsum("ncij,jn->nci", partial_value, basis_s, precision=HIGHEST_PREC)
    fluid_vel = jnp.einsum("nci,in->cn", partial_value, basis_r, precision=HIGHEST_PREC)
    drag_accel = jnp.where(is_live[None, :], drop_state[6][None, :] * (fluid_vel - drop_state[3:6]), 0.0)
    drag_force = -drop_state[7][None, :] * drag_accel
    spread = jnp.einsum("cn,in,jn,kn->ncijk", drag_force, basis_r, basis_s, basis_t, precision=HIGHEST_PREC)
    return drag_accel, spread.reshape(slot_count, 1536)


def reference(source, metric, base_velocity, drop_elem, drop_coord, drop_vel, drop_prop, drop_counts):
    pressure = chebyshev(source, metric, lambda grid_field: assemble(zero_rim(grid_field)))
    vel_table = velocity_table(pressure, base_velocity, metric)
    holders = SLABS * COLS
    slot_total = REACH * CAP
    drop_state = jnp.concatenate([drop_coord, drop_vel, drop_prop], axis=3)
    drop_state = drop_state.reshape(holders, REACH, 8, CAP).transpose(0, 2, 1, 3).reshape(holders, 8, slot_total)
    owner_ids = drop_elem.reshape(holders, slot_total).astype(jnp.int32)
    slot_index = jnp.arange(CAP, dtype=jnp.int32)
    is_live = (slot_index[None, None, :] < drop_counts.reshape(holders, REACH)[:, :, None]).reshape(holders, slot_total)

    def per_holder(running, inputs):
        holder_ids, holder_state, holder_live = inputs
        gathered = jnp.take(vel_table, holder_ids, axis=0).reshape(slot_total, 3, 8, 8, 8)
        drag_accel, spread = droplet_terms(gathered, holder_state, holder_live)
        running = running.at[holder_ids].add(spread)
        return running, drag_accel

    empty_table = jnp.zeros((EXT * EYT * EZ, 1536), jnp.float32)
    source_table, accels = lax.scan(per_holder, empty_table, (owner_ids, drop_state, is_live))
    drop_accel = accels.reshape(holders, 3, REACH, CAP).transpose(0, 2, 1, 3).reshape(SLABS, COLS, REACH, 3, CAP)
    momentum_source = assemble(zero_rim(table_to_field(source_table, metric)))
    return pressure, momentum_source, drop_accel
```

```python
import jax
import jax.numpy as jnp
import numpy as np
from jax import lax
from jax.experimental import pallas as pl
from jax.experimental.pallas import tpu as pltpu
from jax.sharding import PartitionSpec as P

SWEEPS = 3
DEPTH = SWEEPS + 1
NODES = 8
STATE = 9
MASS_SHIFT = 1.0
UPPER_BOUND = 2.5
LOWER_BOUND = UPPER_BOUND / 30.0
GLL_POINTS = [
    -1.0,
    -0.8717401485096066,
    -0.5917001814331423,
    -0.2092992179024789,
    0.2092992179024789,
    0.5917001814331423,
    0.8717401485096066,
    1.0,
]
F32 = jnp.float32
BF16 = jnp.bfloat16
ROUTES = ((1, 0), (1, 1), (2, 0), (2, 1))


def legendre_seven(points):
    before = points * 0.0 + 1.0
    current = points
    for order in range(1, 7):
        following = ((2.0 * order + 1.0) * points * current - order * before) / (order + 1.0)
        before = current
        current = following
    return current


def gll_tables():
    gll_nodes = np.array(GLL_POINTS)
    values = legendre_seven(gll_nodes)
    weights = 2.0 / (56.0 * values * values)
    deriv_mat = np.zeros((8, 8))
    for row_idx in range(8):
        for col_idx in range(8):
            if row_idx != col_idx:
                deriv_mat[row_idx, col_idx] = values[row_idx] / (
                    values[col_idx] * (gll_nodes[row_idx] - gll_nodes[col_idx])
                )
    deriv_mat[0, 0] = -14.0
    deriv_mat[7, 7] = 14.0
    return (gll_nodes, weights, deriv_mat)


NODE_POS, WEIGHTS, DERIV = gll_tables()
STIFF = DERIV.T @ (WEIGHTS[:, None] * DERIV)
STIFF_DIAG = np.diag(STIFF)


def split_pair(table):
    high = table.astype(np.float32).astype(jnp.bfloat16)
    low = (table - high.astype(np.float64)).astype(np.float32).astype(jnp.bfloat16)
    return high, low


def lane_weights(matrix, lanes):
    full = np.kron(np.eye(lanes // NODES), matrix.T)
    high, low = split_pair(full)
    zero = np.zeros_like(np.asarray(low))
    return np.concatenate(
        [np.concatenate([high, low], 1), np.concatenate([high, zero], 1)], 0
    ).astype(jnp.bfloat16)


T_KY, T_DY = 0, 8
T_WJ, T_QJ, T_WK, T_QK, T_Z7, T_Z0, T_Y7, T_Y0 = range(16, 24)
T_NODE = 24
T_INV = 31
T_COUNT = 32


def table_tiles(lanes):
    tiles = np.zeros((T_COUNT, NODES, lanes))
    for turn in range(NODES):
        for row in range(NODES):
            tiles[T_KY + turn, row, :] = STIFF[row, (row - turn) % NODES]
            tiles[T_DY + turn, row, :] = DERIV[row, (row - turn) % NODES]
    reps = lanes // NODES
    tiles[T_WJ] = WEIGHTS[:, None]
    tiles[T_QJ] = STIFF_DIAG[:, None]
    tiles[T_WK] = np.tile(WEIGHTS, reps)[None, :]
    tiles[T_QK] = np.tile(STIFF_DIAG, reps)[None, :]
    place = np.arange(lanes)
    tiles[T_Z7] = ((place % NODES == NODES - 1) & (place < lanes - 1))[None, :]
    tiles[T_Z0] = ((place % NODES == 0) & (place > 0))[None, :]
    tiles[T_Y7, NODES - 1] = 1.0
    tiles[T_Y0, 0] = 1.0
    for row in range(NODES):
        others = [m for m in range(NODES) if m != row]
        scale = 1.0
        for slot, other in enumerate(others):
            tiles[T_NODE + slot, row, :] = NODE_POS[other]
            scale *= NODE_POS[row] - NODE_POS[other]
        tiles[T_INV, row, :] = 1.0 / scale
    return tiles.astype(np.float32)


def bit_pairs(count, bit):
    return [(i, i ^ bit) for i in range(count)]


def neighbour_pairs(count, distance, odd):
    pairs = []
    for low in range(count - distance):
        if (low // distance) % 2 == odd:
            pairs += [(low, low + distance), (low + distance, low)]
    return pairs


def route_block(position, route, reach):
    distance, odd = route
    upward = (position // distance) % 2 == odd
    middle = (reach - 1) // 2
    return jnp.where(upward, middle + distance, middle - distance)


def split_value(value):
    high = value.astype(BF16)
    low = (value - high.astype(F32)).astype(BF16)
    return high, low


def pack_kernel(lanes, slabs, cols, reach, spread_ref, source, metric, elem, coord, vel, prop, counts, *outs):
    packed, own, routed = outs[0], outs[1], outs[2:6]
    state = outs[6]
    position = lax.axis_index("stream")
    column = lax.axis_index("cross")
    elem_z = metric.shape[-1]
    packed[0:NODES] = source[...]
    row = jnp.broadcast_to(metric[0, 0][None, :], (NODES, elem_z))
    packed[NODES] = jnp.dot(row, spread_ref[...], precision=lax.Precision.HIGHEST, preferred_element_type=F32)
    capacity = elem.shape[-1]
    middle = (reach - 1) // 2
    slot = lax.broadcasted_iota(jnp.int32, (1, capacity), 1)
    for block in range(reach):
        base = ((position + (block - middle)) * cols + column) * elem_z
        local = elem[0, 0, block : block + 1, :] - base + 1
        live = slot < counts[0, 0, block]
        ids = jnp.where(live, local, 0).astype(F32)
        state[block, 0:3, :] = coord[0, 0, block]
        state[block, 3:6, :] = vel[0, 0, block]
        state[block, 6:8, :] = prop[0, 0, block]
        state[block, 8:16, :] = jnp.broadcast_to(ids, (8, capacity))
    own[...] = state[middle]
    for route, out in zip(ROUTES, routed):
        out[...] = state[route_block(position, route, reach)]


def z_assembled(block, tiles):
    lanes = block.shape[-1]
    axis = block.ndim - 1
    after = pltpu.roll(block, lanes - 1, axis)
    before = pltpu.roll(block, 1, axis)
    return block + tiles[T_Z7] * after + tiles[T_Z0] * before


def y_assembled(blocks, tiles):
    axis = blocks[0].ndim - 2
    out = []
    for j, block in enumerate(blocks):
        total = block
        if j + 1 < len(blocks):
            total = total + tiles[T_Y7] * pltpu.roll(blocks[j + 1], NODES - 1, axis)
        if j > 0:
            total = total + tiles[T_Y0] * pltpu.roll(blocks[j - 1], 1, axis)
        out.append(total)
    return out


def x_product(planes, matrix):
    out = []
    for row in range(NODES):
        total = None
        for col in range(NODES):
            term = planes[col] * float(matrix[row, col])
            total = term if total is None else total + term
        out.append(total)
    return out


def y_product(block, tiles, start):
    total = block * tiles[start]
    for turn in range(1, NODES):
        total = total + pltpu.roll(block, turn, block.ndim - 2) * tiles[start + turn]
    return total


def z_product(rows, weights):
    lanes = rows.shape[-1]
    high, low = split_value(rows)
    both = jnp.concatenate([high, low], axis=1)
    wide = jnp.dot(both, weights, preferred_element_type=F32)
    return wide[:, :lanes] + wide[:, lanes:]


def lagrange(row, tiles):
    capacity = row.shape[-1]
    coords = jnp.broadcast_to(row, (NODES, capacity))
    factor = tiles[T_INV]
    for slot in range(NODES - 1):
        factor = factor * (coords - tiles[T_NODE + slot])
    return factor


def main_kernel(slabs, cols, *refs):
    tiles, stiff_w, deriv_w = refs[0:3]
    pieces = refs[3 : 3 + 3 * cols]
    base_velocity, own = refs[3 + 3 * cols : 5 + 3 * cols]
    routed = refs[5 + 3 * cols : 9 + 3 * cols]
    (pressure, momentum, face_even, face_odd, acc_own, acc_e1, acc_o1, acc_e2, acc_o2,
     loads, scales, resid, update, inv, work, zed) = refs[9 + 3 * cols :]
    lanes = tiles.shape[-1]
    position = lax.axis_index("stream")
    column = lax.axis_index("cross")
    span = 2 * DEPTH - 1
    middle = DEPTH - 1

    group_even = (position // DEPTH) % 2 == 0
    rank = position % DEPTH
    wjk = tiles[T_WJ] * tiles[T_WK]
    for slot_c in range(cols):
        col = column ^ slot_c
        for kind in range(3):
            if kind == 0:
                shift = 0
            elif kind == 1:
                shift = jnp.where(group_even, DEPTH, -DEPTH)
            else:
                shift = jnp.where(group_even, -DEPTH, DEPTH)
            piece = pieces[3 * slot_c + kind]
            for slot in range(DEPTH):
                at = (rank ^ slot) - rank + shift + (2 * DEPTH - 1)
                for i in range(NODES):
                    loads[at, col, i] = piece[slot, i] * (wjk * float(WEIGHTS[i]))
                scales[at, col] = piece[slot, NODES]
    wide_mid = 2 * DEPTH - 1

    def present(offset):
        where = position + offset
        return jnp.where((where >= 0) & (where < slabs), 1.0, 0.0).astype(F32)

    def sides(offset):
        at = wide_mid + offset
        stacks, diags = [], []
        for j in range(cols):
            stacks.append(z_assembled(loads[at, j], tiles))
        stacks = y_assembled(stacks, tiles)
        pres = present(offset)
        for j in range(cols):
            scale = scales[at, j]
            alpha = z_assembled(scale * tiles[T_WK], tiles)
            beta = z_assembled(scale * tiles[T_QK] + (MASS_SHIFT * pres) * tiles[T_WK], tiles)
            rows = []
            for i in range(NODES):
                first = tiles[T_WJ] * float(STIFF_DIAG[i]) + tiles[T_QJ] * float(WEIGHTS[i])
                rows.append(alpha * first + beta * (tiles[T_WJ] * float(WEIGHTS[i])))
            diags.append(jnp.stack(rows, 0))
        diags = y_assembled(diags, tiles)
        return stacks, diags

    def sides_body(step, carry):
        offset = step - DEPTH
        stacks, diags = sides(offset)
        for j in range(cols):
            work[step, j] = stacks[j]
            zed[step, j] = diags[j]
        return carry

    lax.fori_loop(0, 2 * DEPTH + 1, sides_body, 0)

    center = (UPPER_BOUND + LOWER_BOUND) / 2.0
    half_width = (UPPER_BOUND - LOWER_BOUND) / 2.0
    ratio_bound = center / half_width
    cheb_rho = 1.0 / ratio_bound

    def start_body(step, carry):
        gap = 1.0 - present(step - middle)
        for j in range(cols):
            for i in range(NODES):
                side = work[step + 1, j, i]
                diag = zed[step + 1, j, i]
                if i == 0:
                    side = side + work[step, j, NODES - 1]
                    diag = diag + zed[step, j, NODES - 1]
                if i == NODES - 1:
                    side = side + work[step + 2, j, 0]
                    diag = diag + zed[step + 2, j, 0]
                inverse = 1.0 / (diag + gap)
                inv[step, j, i] = inverse
                resid[step, j, i] = side
                update[step, j, i] = side * inverse * (1.0 / center)
        return carry

    lax.fori_loop(0, span, start_body, 0)

    iterate = update[middle, column]
    for sweep in range(SWEEPS):
        radius = SWEEPS - sweep
        first = middle - radius
        count = 2 * radius + 1
        rows = update[first : first + count].reshape(count * cols * NODES * NODES, lanes)
        zed[0:count] = z_product(rows, stiff_w[...]).reshape(count, cols, NODES, NODES, lanes)

        def operator_body(step, carry, first=first):
            offset = step + first - middle
            pres = present(offset)
            outs = []
            for j in range(cols):
                scale = scales[wide_mid + offset, j]
                scaled = scale * tiles[T_WK]
                value = update[first + step, j]
                planes = [value[i] for i in range(NODES)]
                from_x = x_product(planes, STIFF)
                mass = (MASS_SHIFT * pres) * wjk
                scale_x = scaled * tiles[T_WJ]
                scale_z = scale * tiles[T_WJ]
                local = []
                for i in range(NODES):
                    weight = float(WEIGHTS[i])
                    from_y = y_product(planes[i], tiles, T_KY)
                    rest = scaled * from_y + scale_z * zed[step, j, i] + mass * planes[i]
                    local.append(scale_x * from_x[i] + rest * weight)
                outs.append(z_assembled(jnp.stack(local, 0), tiles))
            outs = y_assembled(outs, tiles)
            for j in range(cols):
                work[step, j] = outs[j]
            return carry

        lax.fori_loop(0, count, operator_body, 0)
        rho_next = 1.0 / (2.0 * ratio_bound - cheb_rho)

        def update_body(step, carry, first=first, rho_next=rho_next, cheb_rho=cheb_rho):
            at = first + 1 + step
            for j in range(cols):
                for i in range(NODES):
                    total = work[step + 1, j, i]
                    if i == 0:
                        total = total + work[step, j, NODES - 1]
                    if i == NODES - 1:
                        total = total + work[step + 2, j, 0]
                    left = resid[at, j, i] - total
                    resid[at, j, i] = left
                    update[at, j, i] = (rho_next * cheb_rho) * update[at, j, i] + (
                        2.0 * rho_next / half_width
                    ) * (inv[at, j, i] * left)
            return carry

        lax.fori_loop(0, count - 2, update_body, 0)
        cheb_rho = rho_next
        iterate = iterate + update[middle, column]
    pressure[...] = iterate

    scale = scales[wide_mid, column]
    planes = [iterate[i] for i in range(NODES)]
    grad_x = x_product(planes, DERIV)
    grad_z = z_product(iterate.reshape(NODES * NODES, lanes), deriv_w[...]).reshape(NODES, NODES, lanes)
    velocity = []
    for i in range(NODES):
        velocity.append(base_velocity[0, i] - scale * grad_x[i])
    for i in range(NODES):
        velocity.append(base_velocity[1, i] - scale * y_product(planes[i], tiles, T_DY))
    for i in range(NODES):
        velocity.append(base_velocity[2, i] - scale * grad_z[i])
    velocity = jnp.concatenate(velocity, 0)

    groups = (own,) + tuple(routed)
    pick, bases = [], []
    for group in groups:
        basis = [lagrange(group[axis : axis + 1, :], tiles) for axis in range(3)]
        ids = group[8:16, :]
        pick.append(jnp.concatenate(
            [jnp.where(ids == float(e + 1), basis[2], 0.0) for e in range(lanes // NODES)], 0))
        bases.append(basis)
    pick = jnp.concatenate(pick, 1)
    pick_high, pick_low = split_value(pick)
    vel_high, vel_low = split_value(velocity)
    partial = jnp.dot(
        jnp.concatenate([vel_high, vel_low, vel_high], 1),
        jnp.concatenate([pick_high, pick_high, pick_low], 0),
        preferred_element_type=F32,
    )
    capacity = own.shape[-1]
    spread = []
    for g, (group, basis) in enumerate(zip(groups, bases)):
        ids = group[8:9, :]
        cells = [basis[1] * basis[0][i : i + 1, :] for i in range(NODES)]
        accel_rows, parts = [], []
        for comp in range(3):
            total = None
            for i in range(NODES):
                row = (comp * NODES + i) * NODES
                term = partial[row : row + NODES, g * capacity : (g + 1) * capacity] * cells[i]
                total = term if total is None else total + term
            fluid = jnp.sum(total, axis=0, keepdims=True)
            accel = jnp.where(ids > 0.5, group[6:7, :] * (fluid - group[3 + comp : 4 + comp, :]), 0.0)
            accel_rows.append(accel)
            force = -group[7:8, :] * accel
            parts += [cells[i] * force for i in range(NODES)]
        accel_rows.append(jnp.zeros((NODES - 3, capacity), F32))
        (acc_own, acc_e1, acc_o1, acc_e2, acc_o2)[g][...] = jnp.concatenate(accel_rows, 0)
        spread.append(jnp.concatenate(parts, 0))
    spread = jnp.concatenate(spread, 1)
    spread_high, spread_low = split_value(spread)
    added = lax.dot_general(
        jnp.concatenate([spread_high, spread_low, spread_high], 1),
        jnp.concatenate([pick_high, pick_high, pick_low], 1),
        (((1,), (1,)), ((), ())),
        preferred_element_type=F32,
    )
    added = z_assembled(added.reshape(3, NODES, NODES, lanes), tiles)
    momentum[...] = added
    low_row = added[:, :, 0, :]
    high_row = added[:, :, NODES - 1, :]
    even = column % 2 == 0
    face_even[...] = jnp.where(even, high_row, low_row)
    face_odd[...] = jnp.where(even, low_row, high_row)


def middle_kernel(cols, momentum, face_even, face_odd, acc_e1, acc_o1, out, send_e1, send_o1):
    position = lax.axis_index("stream")
    column = lax.axis_index("cross")
    even = column % 2 == 0
    high = jnp.where(even, face_even[...], face_odd[...]) if cols > 2 else jnp.where(even, face_even[...], 0.0)
    low = jnp.where(even, face_odd[...], face_even[...]) if cols > 2 else jnp.where(even, 0.0, face_even[...])
    out[...] = momentum[...]
    out[:, :, 0, :] = momentum[:, :, 0, :] + low
    out[:, :, NODES - 1, :] = momentum[:, :, NODES - 1, :] + high
    lower = position % 2 == 0
    top = jnp.where(lower, NODES - 1, 0)
    bottom = NODES - 1 - top
    for comp in range(3):
        send_e1[comp] = out[comp, top]
        send_o1[comp] = out[comp, bottom]
    send_e1[3] = acc_e1[...]
    send_o1[3] = acc_o1[...]


def last_kernel(reach, momentum, got_e1, got_o1, acc_own, got_e2, got_o2, out, accel):
    position = lax.axis_index("stream")
    lower = position % 2 == 0
    top = jnp.where(lower, NODES - 1, 0)
    bottom = NODES - 1 - top
    out[...] = momentum[...]
    for comp in range(3):
        out[comp, top] = momentum[comp, top] + got_e1[comp]
        out[comp, bottom] = momentum[comp, bottom] + got_o1[comp]
    accel[0, 0, (reach - 1) // 2] = acc_own[0:3]
    arrived = (got_e1[3], got_o1[3], got_e2[...], got_o2[...])
    for route, value in zip(ROUTES, arrived):
        accel[0, 0, route_block(position, route, reach)] = value[0:3]


def f32(*shape):
    return jax.ShapeDtypeStruct(shape, F32)


def on_device(
    source, metric, base_velocity, drop_elem, drop_coord, drop_vel, drop_prop, drop_counts
):
    slabs = lax.axis_size("stream")
    cols = lax.axis_size("cross")
    lanes = source.shape[-1]
    reach, capacity = drop_elem.shape[2:]
    elem_z = metric.shape[-1]
    vmem = pl.BlockSpec(memory_space=pltpu.VMEM)
    smem = pl.BlockSpec(memory_space=pltpu.SMEM)
    tiles = jnp.asarray(table_tiles(lanes))
    stiff_w = jnp.asarray(lane_weights(STIFF, lanes))
    deriv_w = jnp.asarray(lane_weights(DERIV, lanes))
    to_lanes = jnp.asarray(np.kron(np.eye(elem_z), np.ones((1, NODES))), F32)

    packed, own, *routed = pl.pallas_call(
        lambda *refs: pack_kernel(lanes, slabs, cols, reach, *refs),
        out_shape=[f32(NODES + 1, NODES, lanes)] + [f32(16, capacity)] * 5,
        in_specs=[vmem] * 7 + [smem],
        out_specs=[vmem] * 6,
        scratch_shapes=[pltpu.VMEM((reach, 16, capacity), F32)],
        name="pack",
    )(to_lanes, source, metric, drop_elem, drop_coord, drop_vel, drop_prop, drop_counts)

    def permuted(value, axis, pairs):
        return lax.ppermute(value, axis, pairs)

    got = [
        permuted(value, "stream", neighbour_pairs(slabs, *route))
        for value, route in zip(routed, ROUTES)
    ]
    gathered = packed[None]
    bit = 1
    while bit < DEPTH:
        gathered = jnp.concatenate(
            [gathered, permuted(gathered, "stream", bit_pairs(slabs, bit))], 0
        )
        bit *= 2
    pieces = [gathered] + [
        permuted(gathered, "stream", neighbour_pairs(slabs, DEPTH, odd)) for odd in (0, 1)
    ]
    columns = [pieces]
    bit = 1
    while bit < cols:
        columns = columns + [
            [permuted(piece, "cross", bit_pairs(cols, bit)) for piece in group] for group in columns
        ]
        bit *= 2
    flat = [piece for group in columns for piece in group]

    span = 2 * DEPTH - 1
    field = (cols, NODES, NODES, lanes)
    pressure, momentum, face_even, face_odd, *accels = pl.pallas_call(
        lambda *refs: main_kernel(slabs, cols, *refs),
        out_shape=[f32(NODES, NODES, lanes), f32(3, NODES, NODES, lanes)]
        + [f32(3, NODES, lanes)] * 2
        + [f32(NODES, capacity)] * 5,
        in_specs=[vmem] * (9 + 3 * cols),
        out_specs=[vmem] * 9,
        scratch_shapes=[
            pltpu.VMEM((4 * DEPTH - 1,) + field, F32),
            pltpu.VMEM((4 * DEPTH - 1, cols, NODES, lanes), F32),
            pltpu.VMEM((span,) + field, F32),
            pltpu.VMEM((span,) + field, F32),
            pltpu.VMEM((span,) + field, F32),
            pltpu.VMEM((span + 2,) + field, F32),
            pltpu.VMEM((span + 2,) + field, F32),
        ],
        name="sweeps_and_droplets",
    )(tiles, stiff_w, deriv_w, *flat, base_velocity, own, *got)
    acc_own, acc_e1, acc_o1, acc_e2, acc_o2 = accels

    got_e2, got_o2 = [
        permuted(value, "stream", neighbour_pairs(slabs, *route))
        for value, route in zip((acc_e2, acc_o2), ROUTES[2:])
    ]
    face_even = permuted(face_even, "cross", neighbour_pairs(cols, 1, 0))
    if cols > 2:
        face_odd = permuted(face_odd, "cross", neighbour_pairs(cols, 1, 1))
    momentum, send_e1, send_o1 = pl.pallas_call(
        lambda *refs: middle_kernel(cols, *refs),
        out_shape=[f32(3, NODES, NODES, lanes)] + [f32(4, NODES, lanes)] * 2,
        in_specs=[vmem] * 5,
        out_specs=[vmem] * 3,
        name="cross_faces",
    )(momentum, face_even, face_odd, acc_e1, acc_o1)
    got_e1, got_o1 = [
        permuted(value, "stream", neighbour_pairs(slabs, *route))
        for value, route in zip((send_e1, send_o1), ROUTES[:2])
    ]
    momentum, accel = pl.pallas_call(
        lambda *refs: last_kernel(reach, *refs),
        out_shape=[f32(3, NODES, NODES, lanes), f32(1, 1, reach, 3, capacity)],
        in_specs=[vmem] * 6,
        out_specs=[vmem] * 2,
        name="stream_faces",
    )(momentum, got_e1, got_o1, acc_own, got_e2, got_o2)
    return (pressure, momentum, accel)


def solution(mesh):
    in_specs = (
        P("stream", "cross", None),
        P("stream", "cross", None),
        P(None, "stream", "cross", None),
        P("stream", "cross", None, None),
        P("stream", "cross", None, None, None),
        P("stream", "cross", None, None, None),
        P("stream", "cross", None, None, None),
        P("stream", "cross", None),
    )
    out_specs = (
        P("stream", "cross", None),
        P(None, "stream", "cross", None),
        P("stream", "cross", None, None, None),
    )
    return jax.shard_map(
        on_device, mesh=mesh, in_specs=in_specs, out_specs=out_specs, check_vma=False
    )
```

```python
import jax
import jax.numpy as jnp
import numpy as np
from jax import lax
from jax.experimental import pallas as pl
from jax.experimental.pallas import tpu as pltpu
from jax.sharding import PartitionSpec as P


SWEEPS = 3
DEPTH = SWEEPS + 1
NODES = 8
MASS_SHIFT = 1.0
UPPER_BOUND = 2.5
LOWER_BOUND = UPPER_BOUND / 30.0
GLL_POINTS = [
    -1.0,
    -0.8717401485096066,
    -0.5917001814331423,
    -0.2092992179024789,
    0.2092992179024789,
    0.5917001814331423,
    0.8717401485096066,
    1.0,
]
F32 = jnp.float32
BF16 = jnp.bfloat16
ROUTES = ((1, 0), (1, 1), (2, 0), (2, 1))


def legendre_seven(points):
    before = points * 0.0 + 1.0
    current = points
    for order in range(1, 7):
        following = ((2.0 * order + 1.0) * points * current - order * before) / (order + 1.0)
        before = current
        current = following
    return current


def gll_tables():
    gll_nodes = np.array(GLL_POINTS)
    values = legendre_seven(gll_nodes)
    weights = 2.0 / (56.0 * values * values)
    deriv_mat = np.zeros((8, 8))
    for row_idx in range(8):
        for col_idx in range(8):
            if row_idx != col_idx:
                deriv_mat[row_idx, col_idx] = values[row_idx] / (
                    values[col_idx] * (gll_nodes[row_idx] - gll_nodes[col_idx])
                )
    deriv_mat[0, 0] = -14.0
    deriv_mat[7, 7] = 14.0
    return (gll_nodes, weights, deriv_mat)


NODE_POS, WEIGHTS, DERIV = gll_tables()
STIFF = DERIV.T @ (WEIGHTS[:, None] * DERIV)
STIFF_DIAG = np.diag(STIFF)


def split_pair(table):
    high = table.astype(np.float32).astype(jnp.bfloat16)
    low = (table - high.astype(np.float64)).astype(np.float32).astype(jnp.bfloat16)
    return high, low


def lane_weights(matrix, lanes):
    full = np.kron(np.eye(lanes // NODES), matrix.T)
    high, low = split_pair(full)
    zero = np.zeros_like(np.asarray(low))
    return np.concatenate(
        [np.concatenate([high, low], 1), np.concatenate([high, zero], 1)], 0
    ).astype(jnp.bfloat16)


T_KY, T_DY = 0, 8
T_WJ, T_QJ, T_WK, T_QK, T_Z7, T_Z0, T_Y7, T_Y0 = range(16, 24)
T_NODE = 24
T_INV = 31
T_COUNT = 32


def table_tiles(lanes):
    tiles = np.zeros((T_COUNT, NODES, lanes))
    for turn in range(NODES):
        for row in range(NODES):
            tiles[T_KY + turn, row, :] = STIFF[row, (row - turn) % NODES]
            tiles[T_DY + turn, row, :] = DERIV[row, (row - turn) % NODES]
    reps = lanes // NODES
    tiles[T_WJ] = WEIGHTS[:, None]
    tiles[T_QJ] = STIFF_DIAG[:, None]
    tiles[T_WK] = np.tile(WEIGHTS, reps)[None, :]
    tiles[T_QK] = np.tile(STIFF_DIAG, reps)[None, :]
    place = np.arange(lanes)
    tiles[T_Z7] = ((place % NODES == NODES - 1) & (place < lanes - 1))[None, :]
    tiles[T_Z0] = ((place % NODES == 0) & (place > 0))[None, :]
    tiles[T_Y7, NODES - 1] = 1.0
    tiles[T_Y0, 0] = 1.0
    for row in range(NODES):
        others = [m for m in range(NODES) if m != row]
        scale = 1.0
        for slot, other in enumerate(others):
            tiles[T_NODE + slot, row, :] = NODE_POS[other]
            scale *= NODE_POS[row] - NODE_POS[other]
        tiles[T_INV, row, :] = 1.0 / scale
    return tiles.astype(np.float32)


def bit_pairs(count, bit):
    return [(i, i ^ bit) for i in range(count)]


def neighbour_pairs(count, distance, odd):
    pairs = []
    for low in range(count - distance):
        if (low // distance) % 2 == odd:
            pairs += [(low, low + distance), (low + distance, low)]
    return pairs


def route_block(position, route, reach):
    distance, odd = route
    upward = (position // distance) % 2 == odd
    middle = (reach - 1) // 2
    return jnp.where(upward, middle + distance, middle - distance)


def split_value(value):
    high = value.astype(BF16)
    low = (value - high.astype(F32)).astype(BF16)
    return high, low


def pack_kernel(cols, reach, spread_ref, source, metric, elem, coord, vel, prop, counts, *outs):
    packed, own, routed = outs[0], outs[1], outs[2:6]
    state = outs[6]
    position = lax.axis_index("stream")
    column = lax.axis_index("cross")
    elem_z = metric.shape[-1]
    packed[0:NODES] = source[...]
    row = jnp.broadcast_to(metric[0, 0][None, :], (NODES, elem_z))
    packed[NODES] = jnp.dot(row, spread_ref[...], precision=lax.Precision.HIGHEST, preferred_element_type=F32)
    capacity = elem.shape[-1]
    middle = (reach - 1) // 2
    slot = lax.broadcasted_iota(jnp.int32, (1, capacity), 1)
    for block in range(reach):
        base = ((position + (block - middle)) * cols + column) * elem_z
        local = elem[block] - base + 1
        live = slot < counts[0, 0, block]
        ids = jnp.where(live, local, 0).astype(F32)
        for axis in range(3):
            state[block, axis : axis + 1, :] = coord[3 * block + axis]
            state[block, 3 + axis : 4 + axis, :] = vel[3 * block + axis]
        state[block, 6:8, :] = prop[0, 0, block]
        state[block, 8:16, :] = jnp.broadcast_to(ids, (8, capacity))
    own[...] = state[middle]
    for route, out in zip(ROUTES, routed):
        out[...] = state[route_block(position, route, reach)]


def z_assembled(block, tiles):
    lanes = block.shape[-1]
    axis = block.ndim - 1
    after = pltpu.roll(block, lanes - 1, axis)
    before = pltpu.roll(block, 1, axis)
    return block + tiles[T_Z7] * after + tiles[T_Z0] * before


def y_assembled(blocks, tiles):
    axis = blocks[0].ndim - 2
    out = []
    for j, block in enumerate(blocks):
        total = block
        if j + 1 < len(blocks):
            total = total + tiles[T_Y7] * pltpu.roll(blocks[j + 1], NODES - 1, axis)
        if j > 0:
            total = total + tiles[T_Y0] * pltpu.roll(blocks[j - 1], 1, axis)
        out.append(total)
    return out


def x_product(planes, matrix):
    out = []
    for row in range(NODES):
        total = None
        for col in range(NODES):
            term = planes[col] * float(matrix[row, col])
            total = term if total is None else total + term
        out.append(total)
    return out


def y_product(block, tiles, start):
    total = block * tiles[start]
    for turn in range(1, NODES):
        total = total + pltpu.roll(block, turn, block.ndim - 2) * tiles[start + turn]
    return total


def z_product(rows, weights):
    lanes = rows.shape[-1]
    high, low = split_value(rows)
    both = jnp.concatenate([high, low], axis=1)
    wide = jnp.dot(both, weights, preferred_element_type=F32)
    return wide[:, :lanes] + wide[:, lanes:]


def lagrange(row, tiles):
    capacity = row.shape[-1]
    coords = jnp.broadcast_to(row, (NODES, capacity))
    factor = tiles[T_INV]
    for slot in range(NODES - 1):
        factor = factor * (coords - tiles[T_NODE + slot])
    return factor


def main_kernel(slabs, cols, *refs):
    tiles, stiff_w, deriv_w = refs[0:3]
    pieces = refs[3 : 3 + 3 * cols]
    base_velocity, own = refs[3 + 3 * cols : 5 + 3 * cols]
    routed = refs[5 + 3 * cols : 9 + 3 * cols]
    (pressure, momentum, face_even, face_odd, acc_own, acc_e1, acc_o1, acc_e2, acc_o2,
     loads, scales, resid, update, inv, work, zed) = refs[9 + 3 * cols :]
    lanes = tiles.shape[-1]
    position = lax.axis_index("stream")
    column = lax.axis_index("cross")
    span = 2 * DEPTH - 1
    middle = DEPTH - 1

    group_even = (position // DEPTH) % 2 == 0
    rank = position % DEPTH
    wjk = tiles[T_WJ] * tiles[T_WK]
    for slot_c in range(cols):
        col = column ^ slot_c
        for kind in range(3):
            if kind == 0:
                shift = 0
            elif kind == 1:
                shift = jnp.where(group_even, DEPTH, -DEPTH)
            else:
                shift = jnp.where(group_even, -DEPTH, DEPTH)
            piece = pieces[3 * slot_c + kind]
            for slot in range(DEPTH):
                at = (rank ^ slot) - rank + shift + (2 * DEPTH - 1)
                for i in range(NODES):
                    loads[at, col, i] = piece[slot, i] * (wjk * float(WEIGHTS[i]))
                scales[at, col] = piece[slot, NODES]
    wide_mid = 2 * DEPTH - 1

    def present(offset):
        where = position + offset
        return jnp.where((where >= 0) & (where < slabs), 1.0, 0.0).astype(F32)

    def sides(offset):
        at = wide_mid + offset
        stacks, diags = [], []
        for j in range(cols):
            stacks.append(z_assembled(loads[at, j], tiles))
        stacks = y_assembled(stacks, tiles)
        pres = present(offset)
        for j in range(cols):
            scale = scales[at, j]
            alpha = z_assembled(scale * tiles[T_WK], tiles)
            beta = z_assembled(scale * tiles[T_QK] + (MASS_SHIFT * pres) * tiles[T_WK], tiles)
            rows = []
            for i in range(NODES):
                first = tiles[T_WJ] * float(STIFF_DIAG[i]) + tiles[T_QJ] * float(WEIGHTS[i])
                rows.append(alpha * first + beta * (tiles[T_WJ] * float(WEIGHTS[i])))
            diags.append(jnp.stack(rows, 0))
        diags = y_assembled(diags, tiles)
        return stacks, diags

    def sides_body(step, carry):
        offset = step - DEPTH
        stacks, diags = sides(offset)
        for j in range(cols):
            work[step, j] = stacks[j]
            zed[step, j] = diags[j]
        return carry

    lax.fori_loop(0, 2 * DEPTH + 1, sides_body, 0)

    center = (UPPER_BOUND + LOWER_BOUND) / 2.0
    half_width = (UPPER_BOUND - LOWER_BOUND) / 2.0
    ratio_bound = center / half_width
    cheb_rho = 1.0 / ratio_bound

    def start_body(step, carry):
        gap = 1.0 - present(step - middle)
        for j in range(cols):
            for i in range(NODES):
                side = work[step + 1, j, i]
                diag = zed[step + 1, j, i]
                if i == 0:
                    side = side + work[step, j, NODES - 1]
                    diag = diag + zed[step, j, NODES - 1]
                if i == NODES - 1:
                    side = side + work[step + 2, j, 0]
                    diag = diag + zed[step + 2, j, 0]
                inverse = 1.0 / (diag + gap)
                inv[step, j, i] = inverse
                resid[step, j, i] = side
                update[step, j, i] = side * inverse * (1.0 / center)
        return carry

    lax.fori_loop(0, span, start_body, 0)

    iterate = update[middle, column]
    for sweep in range(SWEEPS):
        radius = SWEEPS - sweep
        first = middle - radius
        count = 2 * radius + 1
        rows = update[first : first + count].reshape(count * cols * NODES * NODES, lanes)
        zed[0:count] = z_product(rows, stiff_w[...]).reshape(count, cols, NODES, NODES, lanes)

        def operator_body(step, carry, first=first):
            offset = step + first - middle
            pres = present(offset)
            outs = []
            for j in range(cols):
                scale = scales[wide_mid + offset, j]
                scaled = scale * tiles[T_WK]
                value = update[first + step, j]
                planes = [value[i] for i in range(NODES)]
                from_x = x_product(planes, STIFF)
                mass = (MASS_SHIFT * pres) * wjk
                scale_x = scaled * tiles[T_WJ]
                scale_z = scale * tiles[T_WJ]
                local = []
                for i in range(NODES):
                    weight = float(WEIGHTS[i])
                    from_y = y_product(planes[i], tiles, T_KY)
                    rest = scaled * from_y + scale_z * zed[step, j, i] + mass * planes[i]
                    local.append(scale_x * from_x[i] + rest * weight)
                outs.append(z_assembled(jnp.stack(local, 0), tiles))
            outs = y_assembled(outs, tiles)
            for j in range(cols):
                work[step, j] = outs[j]
            return carry

        lax.fori_loop(0, count, operator_body, 0)
        rho_next = 1.0 / (2.0 * ratio_bound - cheb_rho)

        def update_body(step, carry, first=first, rho_next=rho_next, cheb_rho=cheb_rho):
            at = first + 1 + step
            for j in range(cols):
                for i in range(NODES):
                    total = work[step + 1, j, i]
                    if i == 0:
                        total = total + work[step, j, NODES - 1]
                    if i == NODES - 1:
                        total = total + work[step + 2, j, 0]
                    left = resid[at, j, i] - total
                    resid[at, j, i] = left
                    update[at, j, i] = (rho_next * cheb_rho) * update[at, j, i] + (
                        2.0 * rho_next / half_width
                    ) * (inv[at, j, i] * left)
            return carry

        lax.fori_loop(0, count - 2, update_body, 0)
        cheb_rho = rho_next
        iterate = iterate + update[middle, column]
    pressure[...] = iterate

    scale = scales[wide_mid, column]
    planes = [iterate[i] for i in range(NODES)]
    grad_x = x_product(planes, DERIV)
    grad_z = z_product(iterate.reshape(NODES * NODES, lanes), deriv_w[...]).reshape(NODES, NODES, lanes)
    velocity = []
    for i in range(NODES):
        velocity.append(base_velocity[0, i] - scale * grad_x[i])
    for i in range(NODES):
        velocity.append(base_velocity[1, i] - scale * y_product(planes[i], tiles, T_DY))
    for i in range(NODES):
        velocity.append(base_velocity[2, i] - scale * grad_z[i])
    velocity = jnp.concatenate(velocity, 0)

    groups = (own,) + tuple(routed)
    pick, bases = [], []
    for group in groups:
        basis = [lagrange(group[axis : axis + 1, :], tiles) for axis in range(3)]
        ids = group[8:16, :]
        pick.append(jnp.concatenate(
            [jnp.where(ids == float(e + 1), basis[2], 0.0) for e in range(lanes // NODES)], 0))
        bases.append(basis)
    pick = jnp.concatenate(pick, 1)
    pick_high, pick_low = split_value(pick)
    vel_high, vel_low = split_value(velocity)
    partial = jnp.dot(
        jnp.concatenate([vel_high, vel_low, vel_high], 1),
        jnp.concatenate([pick_high, pick_high, pick_low], 0),
        preferred_element_type=F32,
    )
    capacity = own.shape[-1]
    spread = []
    for g, (group, basis) in enumerate(zip(groups, bases)):
        ids = group[8:9, :]
        cells = [basis[1] * basis[0][i : i + 1, :] for i in range(NODES)]
        accel_rows, parts = [], []
        for comp in range(3):
            total = None
            for i in range(NODES):
                row = (comp * NODES + i) * NODES
                term = partial[row : row + NODES, g * capacity : (g + 1) * capacity] * cells[i]
                total = term if total is None else total + term
            fluid = jnp.sum(total, axis=0, keepdims=True)
            accel = jnp.where(ids > 0.5, group[6:7, :] * (fluid - group[3 + comp : 4 + comp, :]), 0.0)
            accel_rows.append(accel)
            force = -group[7:8, :] * accel
            parts += [cells[i] * force for i in range(NODES)]
        accel_rows.append(jnp.zeros((NODES - 3, capacity), F32))
        (acc_own, acc_e1, acc_o1, acc_e2, acc_o2)[g][...] = jnp.concatenate(accel_rows, 0)
        spread.append(jnp.concatenate(parts, 0))
    spread = jnp.concatenate(spread, 1)
    spread_high, spread_low = split_value(spread)
    added = lax.dot_general(
        jnp.concatenate([spread_high, spread_low, spread_high], 1),
        jnp.concatenate([pick_high, pick_high, pick_low], 1),
        (((1,), (1,)), ((), ())),
        preferred_element_type=F32,
    )
    added = z_assembled(added.reshape(3, NODES, NODES, lanes), tiles)
    momentum[...] = added
    low_row = added[:, :, 0, :]
    high_row = added[:, :, NODES - 1, :]
    even = column % 2 == 0
    face_even[...] = jnp.where(even, high_row, low_row)
    face_odd[...] = jnp.where(even, low_row, high_row)


def middle_kernel(cols, momentum, face_even, face_odd, acc_e1, acc_o1, out, send_e1, send_o1):
    position = lax.axis_index("stream")
    column = lax.axis_index("cross")
    even = column % 2 == 0
    high = jnp.where(even, face_even[...], face_odd[...]) if cols > 2 else jnp.where(even, face_even[...], 0.0)
    low = jnp.where(even, face_odd[...], face_even[...]) if cols > 2 else jnp.where(even, 0.0, face_even[...])
    out[...] = momentum[...]
    out[:, :, 0, :] = momentum[:, :, 0, :] + low
    out[:, :, NODES - 1, :] = momentum[:, :, NODES - 1, :] + high
    lower = position % 2 == 0
    top = jnp.where(lower, NODES - 1, 0)
    bottom = NODES - 1 - top
    for comp in range(3):
        send_e1[comp] = out[comp, top]
        send_o1[comp] = out[comp, bottom]
    send_e1[3] = acc_e1[...]
    send_o1[3] = acc_o1[...]


def last_kernel(reach, momentum, got_e1, got_o1, acc_own, got_e2, got_o2, out, accel):
    position = lax.axis_index("stream")
    lower = position % 2 == 0
    top = jnp.where(lower, NODES - 1, 0)
    bottom = NODES - 1 - top
    out[...] = momentum[...]
    for comp in range(3):
        out[comp, top] = momentum[comp, top] + got_e1[comp]
        out[comp, bottom] = momentum[comp, bottom] + got_o1[comp]
    for axis in range(3):
        accel[3 * ((reach - 1) // 2) + axis] = acc_own[axis : axis + 1]
    arrived = (got_e1[3], got_o1[3], got_e2[...], got_o2[...])
    for route, value in zip(ROUTES, arrived):
        block = route_block(position, route, reach)
        for axis in range(3):
            accel[3 * block + axis] = value[axis : axis + 1]


def f32(*shape):
    return jax.ShapeDtypeStruct(shape, F32)


def near(*shape):
    return pltpu.VMEM(shape, F32)


def held(value):
    return pltpu.with_memory_space_constraint(value, pltpu.VMEM)


def step(
    source, metric, base_velocity, drop_elem, drop_coord, drop_vel, drop_prop, drop_counts
):
    slabs = lax.axis_size("stream")
    cols = lax.axis_size("cross")
    lanes = source.shape[-1]
    reach, capacity = drop_elem.shape[2:]
    elem_z = metric.shape[-1]
    vmem = pl.BlockSpec(memory_space=pltpu.VMEM)
    smem = pl.BlockSpec(memory_space=pltpu.SMEM)
    tiles = jnp.asarray(table_tiles(lanes))
    stiff_w = jnp.asarray(lane_weights(STIFF, lanes))
    deriv_w = jnp.asarray(lane_weights(DERIV, lanes))
    to_lanes = jnp.asarray(np.kron(np.eye(elem_z), np.ones((1, NODES))), F32)

    packed, own, *routed = pl.pallas_call(
        lambda *refs: pack_kernel(cols, reach, *refs),
        out_shape=[near(NODES + 1, NODES, lanes)] + [near(16, capacity)] * 5,
        in_specs=[vmem] * 7 + [smem],
        out_specs=[vmem] * 6,
        scratch_shapes=[pltpu.VMEM((reach, 16, capacity), F32)],
        name="pack",
    )(
        to_lanes,
        source,
        metric,
        drop_elem.reshape(reach, 1, capacity),
        drop_coord.reshape(3 * reach, 1, capacity),
        drop_vel.reshape(3 * reach, 1, capacity),
        drop_prop,
        drop_counts,
    )

    got = [
        lax.ppermute(value, "stream", neighbour_pairs(slabs, *route))
        for value, route in zip(routed, ROUTES)
    ]
    gathered = packed[None]
    bit = 1
    while bit < DEPTH:
        gathered = jnp.concatenate(
            [gathered, lax.ppermute(gathered, "stream", bit_pairs(slabs, bit))], 0
        )
        bit *= 2
    pieces = [gathered] + [
        lax.ppermute(gathered, "stream", neighbour_pairs(slabs, DEPTH, odd))
        for odd in (0, 1)
    ]
    columns = [pieces]
    bit = 1
    while bit < cols:
        columns = columns + [
            [lax.ppermute(piece, "cross", bit_pairs(cols, bit)) for piece in group]
            for group in columns
        ]
        bit *= 2
    flat = [piece for group in columns for piece in group]

    span = 2 * DEPTH - 1
    field = (cols, NODES, NODES, lanes)
    scratch_bytes = 4 * (9 * DEPTH + 1 + 5 * span) * int(np.prod(field))
    pressure, momentum, face_even, face_odd, *accels = pl.pallas_call(
        lambda *refs: main_kernel(slabs, cols, *refs),
        out_shape=[f32(NODES, NODES, lanes), near(3, NODES, NODES, lanes)]
        + [near(3, NODES, lanes)] * 2
        + [near(NODES, capacity)] * 5,
        in_specs=[vmem] * (9 + 3 * cols),
        out_specs=[vmem] * 9,
        scratch_shapes=[
            pltpu.VMEM((4 * DEPTH - 1,) + field, F32),
            pltpu.VMEM((4 * DEPTH - 1, cols, NODES, lanes), F32),
            pltpu.VMEM((span,) + field, F32),
            pltpu.VMEM((span,) + field, F32),
            pltpu.VMEM((span,) + field, F32),
            pltpu.VMEM((span + 2,) + field, F32),
            pltpu.VMEM((span + 2,) + field, F32),
        ],
        compiler_params=pltpu.CompilerParams(vmem_limit_bytes=2 * scratch_bytes + 2**23),
        name="sweeps_and_droplets",
    )(
        tiles,
        stiff_w,
        deriv_w,
        *[held(piece) for piece in flat],
        base_velocity,
        held(own),
        *[held(value) for value in got],
    )
    acc_own, acc_e1, acc_o1, acc_e2, acc_o2 = accels

    got_e2, got_o2 = [
        lax.ppermute(value, "stream", neighbour_pairs(slabs, *route))
        for value, route in zip((acc_e2, acc_o2), ROUTES[2:])
    ]
    face_even = lax.ppermute(face_even, "cross", neighbour_pairs(cols, 1, 0))
    if cols > 2:
        face_odd = lax.ppermute(face_odd, "cross", neighbour_pairs(cols, 1, 1))
    momentum, send_e1, send_o1 = pl.pallas_call(
        lambda *refs: middle_kernel(cols, *refs),
        out_shape=[near(3, NODES, NODES, lanes)] + [near(4, NODES, lanes)] * 2,
        in_specs=[vmem] * 5,
        out_specs=[vmem] * 3,
        name="cross_faces",
    )(*[held(value) for value in (momentum, face_even, face_odd, acc_e1, acc_o1)])
    got_e1, got_o1 = [
        lax.ppermute(value, "stream", neighbour_pairs(slabs, *route))
        for value, route in zip((send_e1, send_o1), ROUTES[:2])
    ]
    momentum, accel = pl.pallas_call(
        lambda *refs: last_kernel(reach, *refs),
        out_shape=[f32(3, NODES, NODES, lanes), f32(3 * reach, 1, capacity)],
        in_specs=[vmem] * 6,
        out_specs=[vmem] * 2,
        name="stream_faces",
    )(*[held(value) for value in (momentum, got_e1, got_o1, acc_own, got_e2, got_o2)])
    return (pressure, momentum, accel.reshape(1, 1, reach, 3, capacity))


def solution(mesh):
    in_specs = (
        P("stream", "cross", None),
        P("stream", "cross", None),
        P(None, "stream", "cross", None),
        P("stream", "cross", None, None),
        P("stream", "cross", None, None, None),
        P("stream", "cross", None, None, None),
        P("stream", "cross", None, None, None),
        P("stream", "cross", None),
    )
    out_specs = (
        P("stream", "cross", None),
        P(None, "stream", "cross", None),
        P("stream", "cross", None, None, None),
    )
    return jax.shard_map(step, mesh=mesh, in_specs=in_specs, out_specs=out_specs, check_vma=False)
```

```python
import jax
import jax.numpy as jnp
import numpy as np
from jax import lax
from jax.experimental import pallas as pl
from jax.experimental.pallas import tpu as pltpu
from jax.sharding import PartitionSpec as P


SWEEPS = 3
DEPTH = SWEEPS + 1
NODES = 8
MASS_SHIFT = 1.0
UPPER_BOUND = 2.5
LOWER_BOUND = UPPER_BOUND / 30.0
GLL_POINTS = [
    -1.0,
    -0.8717401485096066,
    -0.5917001814331423,
    -0.2092992179024789,
    0.2092992179024789,
    0.5917001814331423,
    0.8717401485096066,
    1.0,
]
F32 = jnp.float32
BF16 = jnp.bfloat16


def legendre_seven(points):
    before = points * 0.0 + 1.0
    current = points
    for order in range(1, 7):
        following = ((2.0 * order + 1.0) * points * current - order * before) / (order + 1.0)
        before = current
        current = following
    return current


def gll_tables():
    gll_nodes = np.array(GLL_POINTS)
    values = legendre_seven(gll_nodes)
    weights = 2.0 / (56.0 * values * values)
    deriv_mat = np.zeros((8, 8))
    for row_idx in range(8):
        for col_idx in range(8):
            if row_idx != col_idx:
                deriv_mat[row_idx, col_idx] = values[row_idx] / (
                    values[col_idx] * (gll_nodes[row_idx] - gll_nodes[col_idx])
                )
    deriv_mat[0, 0] = -14.0
    deriv_mat[7, 7] = 14.0
    return (gll_nodes, weights, deriv_mat)


NODE_POS, WEIGHTS, DERIV = gll_tables()
STIFF = DERIV.T @ (WEIGHTS[:, None] * DERIV)
STIFF_DIAG = np.diag(STIFF)


def split_pair(table):
    high = table.astype(np.float32).astype(jnp.bfloat16)
    low = (table - high.astype(np.float64)).astype(np.float32).astype(jnp.bfloat16)
    return high, low


def lane_weights(matrix, lanes):
    full = np.kron(np.eye(lanes // NODES), matrix.T)
    high, low = split_pair(full)
    zero = np.zeros_like(np.asarray(low))
    return np.concatenate(
        [np.concatenate([high, low], 1), np.concatenate([high, zero], 1)], 0
    ).astype(jnp.bfloat16)


F_FACE = (DEPTH - 1) * NODES
F_META = F_FACE + 1
F_COUNT = F_FACE + 2
ROUTES = ((1, 0), (1, 1), (2, 0), (2, 1))
T_KY, T_DY = 0, 8
T_WJ, T_QJ, T_WK, T_QK, T_Z7, T_Z0, T_Y7, T_Y0 = range(16, 24)
T_NODE = 24
T_INV = 31
T_COUNT = 32


def table_tiles(lanes):
    tiles = np.zeros((T_COUNT, NODES, lanes))
    for turn in range(NODES):
        for row in range(NODES):
            tiles[T_KY + turn, row, :] = STIFF[row, (row - turn) % NODES]
            tiles[T_DY + turn, row, :] = DERIV[row, (row - turn) % NODES]
    reps = lanes // NODES
    tiles[T_WJ] = WEIGHTS[:, None]
    tiles[T_QJ] = STIFF_DIAG[:, None]
    tiles[T_WK] = np.tile(WEIGHTS, reps)[None, :]
    tiles[T_QK] = np.tile(STIFF_DIAG, reps)[None, :]
    place = np.arange(lanes)
    tiles[T_Z7] = ((place % NODES == NODES - 1) & (place < lanes - 1))[None, :]
    tiles[T_Z0] = ((place % NODES == 0) & (place > 0))[None, :]
    tiles[T_Y7, NODES - 1] = 1.0
    tiles[T_Y0, 0] = 1.0
    for row in range(NODES):
        others = [m for m in range(NODES) if m != row]
        scale = 1.0
        for slot, other in enumerate(others):
            tiles[T_NODE + slot, row, :] = NODE_POS[other]
            scale *= NODE_POS[row] - NODE_POS[other]
        tiles[T_INV, row, :] = 1.0 / scale
    return tiles.astype(np.float32)


def swapped_bit(slabs, cols, bit):
    return [
        (i * cols + j, (i ^ bit) * cols + (j ^ 1)) for i in range(slabs) for j in range(cols)
    ]


def neighbours(slabs, cols, distance, odd, swap=0):
    partner = {}
    for low in range(slabs - distance):
        if (low // distance) % 2 == odd:
            partner[low] = low + distance
            partner[low + distance] = low
    pairs = []
    for i in range(slabs):
        for j in range(cols):
            if i in partner:
                pairs.append((i * cols + j, partner[i] * cols + (j ^ swap)))
            else:
                pairs.append((i * cols + j, i * cols + (j ^ 1)))
    return pairs


def column_pairs(cols, bit):
    return [(j, j ^ bit) for j in range(cols)]


def side_pairs(cols, odd):
    pairs = []
    for low in range(cols - 1):
        if low % 2 == odd:
            pairs += [(low, low + 1), (low + 1, low)]
    return pairs


def parity(slot):
    return bin(slot).count("1") % 2


def route_partner(position, route):
    distance, odd = route
    upward = (position // distance) % 2 == odd
    return jnp.where(upward, position + distance, position - distance), upward


def route_block(position, route, reach):
    middle = (reach - 1) // 2
    upward = route_partner(position, route)[1]
    return jnp.where(upward, middle + route[0], middle - route[0])


def route_open(position, route, slabs):
    partner = route_partner(position, route)[0]
    return jnp.logical_and(partner >= 0, partner < slabs)


def split_value(value):
    high = value.astype(BF16)
    low = (value - high.astype(F32)).astype(BF16)
    return high, low


def pack_kernel(cols, elem_z, source, metric, elem, coord, vel, prop, counts, first, own, *rest):
    first[0:NODES] = source[...]
    first[NODES] = jnp.zeros(first.shape[1:], F32)
    first[NODES, 0:1, 0 : metric.shape[-1]] = metric[0]
    routed, state = rest[:-1], rest[-1]
    position = lax.axis_index("stream")
    column = lax.axis_index("cross")
    reach, _, capacity = elem.shape
    middle = (reach - 1) // 2
    slot = lax.broadcasted_iota(jnp.int32, (1, capacity), 1)
    for block in range(reach):
        base = ((position + (block - middle)) * cols + column) * elem_z
        live = slot < counts[0, 0, block]
        ids = jnp.where(live, elem[block] - base + 1, 0).astype(F32)
        for axis in range(3):
            state[block, 0, axis : axis + 1, :] = coord[3 * block + axis]
            state[block, 0, 3 + axis : 4 + axis, :] = vel[3 * block + axis]
        state[block, 0, 6:8, :] = prop[0, 0, block]
        state[block, 1] = jnp.broadcast_to(ids, (NODES, capacity))
    own[...] = state[middle]
    for route, out in zip(ROUTES, routed):
        out[...] = state[route_block(position, route, reach)]


def near_kernel(first, from_source, from_metric, out):
    out[0] = first[...]
    out[1, 0:NODES] = from_source[...]
    out[1, NODES] = jnp.zeros(out.shape[2:], F32)
    out[1, NODES, 0:1, 0 : from_metric.shape[-1]] = from_metric[0]


def far_kernel(gathered, *outs):
    position = lax.axis_index("stream")
    group_even = (position // DEPTH) % 2 == 0
    for odd, out in enumerate(outs):
        upward = group_even if odd == 0 else jnp.logical_not(group_even)
        for slot in range(1, DEPTH):
            for i in range(NODES):
                out[(slot - 1) * NODES + i] = gathered[slot, i]
        out[F_FACE] = gathered[0, jnp.where(upward, NODES - 1, 0)]
        out[F_META] = jnp.zeros(out.shape[1:], F32)
        for slot in range(DEPTH):
            out[F_META, slot : slot + 1, :] = gathered[slot, NODES, 0:1, :]


def z_assembled(block, tiles):
    lanes = block.shape[-1]
    axis = block.ndim - 1
    after = pltpu.roll(block, lanes - 1, axis)
    before = pltpu.roll(block, 1, axis)
    return block + tiles[T_Z7] * after + tiles[T_Z0] * before


def y_assembled(blocks, tiles):
    axis = blocks[0].ndim - 2
    out = []
    for j, block in enumerate(blocks):
        total = block
        if j + 1 < len(blocks):
            total = total + tiles[T_Y7] * pltpu.roll(blocks[j + 1], NODES - 1, axis)
        if j > 0:
            total = total + tiles[T_Y0] * pltpu.roll(blocks[j - 1], 1, axis)
        out.append(total)
    return out


def x_product(planes, matrix):
    out = []
    for row in range(NODES):
        total = None
        for col in range(NODES):
            term = planes[col] * float(matrix[row, col])
            total = term if total is None else total + term
        out.append(total)
    return out


def y_product(block, tiles, start):
    total = block * tiles[start]
    for turn in range(1, NODES):
        total = total + pltpu.roll(block, turn, block.ndim - 2) * tiles[start + turn]
    return total


def z_product(rows, weights):
    lanes = rows.shape[-1]
    high, low = split_value(rows)
    both = jnp.concatenate([high, low], axis=1)
    wide = jnp.dot(both, weights, preferred_element_type=F32)
    return wide[:, :lanes] + wide[:, lanes:]


def lagrange(row, tiles):
    capacity = row.shape[-1]
    coords = jnp.broadcast_to(row, (NODES, capacity))
    factor = tiles[T_INV]
    for slot in range(NODES - 1):
        factor = factor * (coords - tiles[T_NODE + slot])
    return factor


def main_kernel(slabs, cols, *refs):
    tiles, stiff_w, deriv_w, spread_w = refs[0:4]
    pieces = refs[4 : 4 + 3 * cols]
    base_velocity, own = refs[4 + 3 * cols : 6 + 3 * cols]
    routed = refs[6 + 3 * cols : 10 + 3 * cols]
    (pressure, momentum, face_even, face_odd, acc_own, acc_e1, acc_o1, acc_e2, acc_o2,
     loads, scales, resid, update, inv, work, zed) = refs[10 + 3 * cols :]
    lanes = tiles.shape[-1]
    position = lax.axis_index("stream")
    column = lax.axis_index("cross")
    span = 2 * DEPTH - 1
    middle = DEPTH - 1

    group_even = (position // DEPTH) % 2 == 0
    rank = position % DEPTH
    wjk = tiles[T_WJ] * tiles[T_WK]
    flat = (NODES, lanes)

    def present(offset):
        where = position + offset
        return jnp.where((where >= 0) & (where < slabs), 1.0, 0.0).astype(F32)

    factors = []
    for slot_c in range(cols):
        near, *fars = pieces[3 * slot_c : 3 * slot_c + 3]
        factors += [near[slot, NODES, 0:1, :] for slot in range(DEPTH)]
        factors += [jnp.zeros((NODES - DEPTH, lanes), F32)] + [far[F_META] for far in fars]
    high, low = split_value(jnp.concatenate(factors, 0))
    factors = jnp.dot(
        jnp.concatenate([high, low], 1), spread_w[...], preferred_element_type=F32
    )
    for slot_c in range(cols):
        near, *fars = pieces[3 * slot_c : 3 * slot_c + 3]
        for slot in range(DEPTH):
            col = column ^ (slot_c ^ parity(slot))
            at = (rank ^ slot) - rank + (2 * DEPTH - 1)
            for i in range(NODES):
                loads[at, col, i] = near[slot, i] * (wjk * float(WEIGHTS[i]))
            row = 3 * NODES * slot_c + slot
            scales[at, col] = jnp.broadcast_to(factors[row : row + 1], flat)
        for odd, far in enumerate(fars):
            upper = group_even if odd == 0 else jnp.logical_not(group_even)
            shift = jnp.where(upper, DEPTH, -DEPTH)
            inside = present(shift)
            for slot in range(DEPTH):
                col = column ^ (slot_c ^ parity(slot) ^ 1)
                at = (rank ^ slot) - rank + shift + (2 * DEPTH - 1)
                if slot > 0:
                    for i in range(NODES):
                        loads[at, col, i] = far[(slot - 1) * NODES + i] * (
                            wjk * (inside * float(WEIGHTS[i]))
                        )
                else:
                    layer = jnp.where(upper, 0, NODES - 1)
                    loads[at, col, layer] = far[F_FACE] * (wjk * (inside * float(WEIGHTS[0])))
                row = 3 * NODES * slot_c + NODES * (1 + odd) + slot
                scales[at, col] = jnp.broadcast_to(factors[row : row + 1] * inside, flat)
    wide_mid = 2 * DEPTH - 1

    def sides(offset):
        at = wide_mid + offset
        stacks, diags = [], []
        for j in range(cols):
            stacks.append(z_assembled(loads[at, j], tiles))
        stacks = y_assembled(stacks, tiles)
        pres = present(offset)
        for j in range(cols):
            scale = scales[at, j]
            alpha = z_assembled(scale * tiles[T_WK], tiles)
            beta = z_assembled(scale * tiles[T_QK] + (MASS_SHIFT * pres) * tiles[T_WK], tiles)
            rows = []
            for i in range(NODES):
                first = tiles[T_WJ] * float(STIFF_DIAG[i]) + tiles[T_QJ] * float(WEIGHTS[i])
                rows.append(alpha * first + beta * (tiles[T_WJ] * float(WEIGHTS[i])))
            diags.append(jnp.stack(rows, 0))
        diags = y_assembled(diags, tiles)
        return stacks, diags

    def sides_body(step, carry):
        offset = step - DEPTH
        stacks, diags = sides(offset)
        for j in range(cols):
            work[step, j] = stacks[j]
            zed[step, j] = diags[j]
        return carry

    lax.fori_loop(0, 2 * DEPTH + 1, sides_body, 0)

    center = (UPPER_BOUND + LOWER_BOUND) / 2.0
    half_width = (UPPER_BOUND - LOWER_BOUND) / 2.0
    ratio_bound = center / half_width
    cheb_rho = 1.0 / ratio_bound

    def start_body(step, carry):
        gap = 1.0 - present(step - middle)
        for j in range(cols):
            for i in range(NODES):
                side = work[step + 1, j, i]
                diag = zed[step + 1, j, i]
                if i == 0:
                    side = side + work[step, j, NODES - 1]
                    diag = diag + zed[step, j, NODES - 1]
                if i == NODES - 1:
                    side = side + work[step + 2, j, 0]
                    diag = diag + zed[step + 2, j, 0]
                inverse = 1.0 / (diag + gap)
                inv[step, j, i] = inverse
                resid[step, j, i] = side
                update[step, j, i] = side * inverse * (1.0 / center)
        return carry

    lax.fori_loop(0, span, start_body, 0)

    iterate = update[middle, column]
    for sweep in range(SWEEPS):
        radius = SWEEPS - sweep
        first = middle - radius
        count = 2 * radius + 1
        rows = update[first : first + count].reshape(count * cols * NODES * NODES, lanes)
        zed[0:count] = z_product(rows, stiff_w[...]).reshape(count, cols, NODES, NODES, lanes)

        def operator_body(step, carry, first=first):
            offset = step + first - middle
            pres = present(offset)
            outs = []
            for j in range(cols):
                scale = scales[wide_mid + offset, j]
                scaled = scale * tiles[T_WK]
                value = update[first + step, j]
                planes = [value[i] for i in range(NODES)]
                from_x = x_product(planes, STIFF)
                mass = (MASS_SHIFT * pres) * wjk
                scale_x = scaled * tiles[T_WJ]
                scale_z = scale * tiles[T_WJ]
                local = []
                for i in range(NODES):
                    weight = float(WEIGHTS[i])
                    from_y = y_product(planes[i], tiles, T_KY)
                    rest = scaled * from_y + scale_z * zed[step, j, i] + mass * planes[i]
                    local.append(scale_x * from_x[i] + rest * weight)
                outs.append(z_assembled(jnp.stack(local, 0), tiles))
            outs = y_assembled(outs, tiles)
            for j in range(cols):
                work[step, j] = outs[j]
            return carry

        lax.fori_loop(0, count, operator_body, 0)
        rho_next = 1.0 / (2.0 * ratio_bound - cheb_rho)

        def update_body(step, carry, first=first, rho_next=rho_next, cheb_rho=cheb_rho):
            at = first + 1 + step
            for j in range(cols):
                for i in range(NODES):
                    total = work[step + 1, j, i]
                    if i == 0:
                        total = total + work[step, j, NODES - 1]
                    if i == NODES - 1:
                        total = total + work[step + 2, j, 0]
                    left = resid[at, j, i] - total
                    resid[at, j, i] = left
                    update[at, j, i] = (rho_next * cheb_rho) * update[at, j, i] + (
                        2.0 * rho_next / half_width
                    ) * (inv[at, j, i] * left)
            return carry

        lax.fori_loop(0, count - 2, update_body, 0)
        cheb_rho = rho_next
        iterate = iterate + update[middle, column]
    pressure[...] = iterate

    scale = scales[wide_mid, column]
    planes = [iterate[i] for i in range(NODES)]
    grad_x = x_product(planes, DERIV)
    grad_z = z_product(iterate.reshape(NODES * NODES, lanes), deriv_w[...]).reshape(NODES, NODES, lanes)
    velocity = []
    for i in range(NODES):
        velocity.append(base_velocity[0, i] - scale * grad_x[i])
    for i in range(NODES):
        velocity.append(base_velocity[1, i] - scale * y_product(planes[i], tiles, T_DY))
    for i in range(NODES):
        velocity.append(base_velocity[2, i] - scale * grad_z[i])
    velocity = jnp.concatenate(velocity, 0)

    groups = [(own[0], own[1])]
    for route, group in zip(ROUTES, routed):
        groups.append((group[0], jnp.where(route_open(position, route, slabs), group[1], 0.0)))
    pick, bases = [], []
    for group, ids in groups:
        basis = [lagrange(group[axis : axis + 1, :], tiles) for axis in range(3)]
        pick.append(jnp.concatenate(
            [jnp.where(ids == float(e + 1), basis[2], 0.0) for e in range(lanes // NODES)], 0))
        bases.append(basis)
    pick = jnp.concatenate(pick, 1)
    pick_high, pick_low = split_value(pick)
    vel_high, vel_low = split_value(velocity)
    partial = jnp.dot(
        jnp.concatenate([vel_high, vel_low, vel_high], 1),
        jnp.concatenate([pick_high, pick_high, pick_low], 0),
        preferred_element_type=F32,
    )
    capacity = own.shape[-1]
    spread = []
    for g, ((group, ids), basis) in enumerate(zip(groups, bases)):
        cells = [basis[1] * basis[0][i : i + 1, :] for i in range(NODES)]
        accel_rows, parts = [], []
        for comp in range(3):
            total = None
            for i in range(NODES):
                row = (comp * NODES + i) * NODES
                term = partial[row : row + NODES, g * capacity : (g + 1) * capacity] * cells[i]
                total = term if total is None else total + term
            fluid = jnp.sum(total, axis=0, keepdims=True)
            accel = jnp.where(ids[0:1, :] > 0.5, group[6:7, :] * (fluid - group[3 + comp : 4 + comp, :]), 0.0)
            accel_rows.append(accel)
            force = -group[7:8, :] * accel
            parts += [cells[i] * force for i in range(NODES)]
        accel_rows.append(jnp.zeros((NODES - 3, capacity), F32))
        (acc_own, acc_e1, acc_o1, acc_e2, acc_o2)[g][...] = jnp.concatenate(accel_rows, 0)
        spread.append(jnp.concatenate(parts, 0))
    spread = jnp.concatenate(spread, 1)
    spread_high, spread_low = split_value(spread)
    added = lax.dot_general(
        jnp.concatenate([spread_high, spread_low, spread_high], 1),
        jnp.concatenate([pick_high, pick_high, pick_low], 1),
        (((1,), (1,)), ((), ())),
        preferred_element_type=F32,
    )
    added = z_assembled(added.reshape(3, NODES, NODES, lanes), tiles)
    momentum[...] = added
    low_row = added[:, :, 0, :]
    high_row = added[:, :, NODES - 1, :]
    even = column % 2 == 0
    face_even[...] = jnp.where(even, high_row, low_row)
    face_odd[...] = jnp.where(even, low_row, high_row)


def middle_kernel(cols, momentum, face_even, face_odd, acc_e1, acc_o1, out, send_e1, send_o1):
    position = lax.axis_index("stream")
    column = lax.axis_index("cross")
    even = column % 2 == 0
    high = jnp.where(even, face_even[...], face_odd[...]) if cols > 2 else jnp.where(even, face_even[...], 0.0)
    low = jnp.where(even, face_odd[...], face_even[...]) if cols > 2 else jnp.where(even, 0.0, face_even[...])
    out[...] = momentum[...]
    out[:, :, 0, :] = momentum[:, :, 0, :] + low
    out[:, :, NODES - 1, :] = momentum[:, :, NODES - 1, :] + high
    lower = position % 2 == 0
    top = jnp.where(lower, NODES - 1, 0)
    bottom = NODES - 1 - top
    for comp in range(3):
        send_e1[comp] = out[comp, top]
        send_o1[comp] = out[comp, bottom]
    send_e1[3] = acc_e1[...]
    send_o1[3] = acc_o1[...]


def last_kernel(slabs, reach, momentum, got_e1, got_o1, acc_own, got_e2, got_o2, out, accel):
    position = lax.axis_index("stream")
    lower = position % 2 == 0
    top = jnp.where(lower, NODES - 1, 0)
    bottom = NODES - 1 - top
    out[...] = momentum[...]
    opened = [route_open(position, route, slabs) for route in ROUTES]
    for comp in range(3):
        out[comp, top] = momentum[comp, top] + jnp.where(opened[0], got_e1[comp], 0.0)
        out[comp, bottom] = momentum[comp, bottom] + jnp.where(opened[1], got_o1[comp], 0.0)
    for axis in range(3):
        accel[3 * ((reach - 1) // 2) + axis] = acc_own[axis : axis + 1]
    arrived = (got_e1[3], got_o1[3], got_e2[...], got_o2[...])
    for route, value, there in zip(ROUTES, arrived, opened):
        block = route_block(position, route, reach)
        for axis in range(3):
            accel[3 * block + axis] = jnp.where(there, value[axis : axis + 1], 0.0)


def f32(*shape):
    return jax.ShapeDtypeStruct(shape, F32)


def near(*shape):
    return pltpu.VMEM(shape, F32)


def held(value):
    return pltpu.with_memory_space_constraint(value, pltpu.VMEM)


def step(
    source, metric, base_velocity, drop_elem, drop_coord, drop_vel, drop_prop, drop_counts
):
    slabs = lax.axis_size("stream")
    cols = lax.axis_size("cross")
    lanes = source.shape[-1]
    reach, capacity = drop_elem.shape[2:]
    elem_z = metric.shape[-1]
    vmem = pl.BlockSpec(memory_space=pltpu.VMEM)
    smem = pl.BlockSpec(memory_space=pltpu.SMEM)
    tiles = jnp.asarray(table_tiles(lanes))
    stiff_w = jnp.asarray(lane_weights(STIFF, lanes))
    deriv_w = jnp.asarray(lane_weights(DERIV, lanes))
    to_lanes = np.zeros((lanes, lanes))
    to_lanes[:elem_z] = np.kron(np.eye(elem_z), np.ones((1, NODES)))
    spread_w = jnp.asarray(np.concatenate([to_lanes, to_lanes], 0), BF16)

    first, own, *routed = pl.pallas_call(
        lambda *refs: pack_kernel(cols, elem_z, *refs),
        out_shape=[near(NODES + 1, NODES, lanes)] + [near(2, NODES, capacity)] * 5,
        in_specs=[vmem] * 6 + [smem],
        out_specs=[vmem] * 6,
        scratch_shapes=[pltpu.VMEM((reach, 2, NODES, capacity), F32)],
        name="pack",
    )(
        source,
        metric,
        drop_elem.reshape(reach, 1, capacity),
        drop_coord.reshape(3 * reach, 1, capacity),
        drop_vel.reshape(3 * reach, 1, capacity),
        drop_prop,
        drop_counts,
    )
    whole = ("stream", "cross")

    routed = [
        lax.ppermute(value, whole, neighbours(slabs, cols, *route))
        for value, route in zip(routed, ROUTES)
    ]
    from_source = lax.ppermute(source, whole, swapped_bit(slabs, cols, 1))
    from_metric = lax.ppermute(metric, whole, swapped_bit(slabs, cols, 1))
    gathered = pl.pallas_call(
        near_kernel,
        out_shape=near(2, NODES + 1, NODES, lanes),
        in_specs=[vmem] * 3,
        out_specs=vmem,
        name="near_pair",
    )(held(first), held(from_source), held(from_metric))
    gathered = jnp.concatenate(
        [gathered, lax.ppermute(gathered, whole, swapped_bit(slabs, cols, 2))], 0
    )
    to_far = pl.pallas_call(
        far_kernel,
        out_shape=[near(F_COUNT, NODES, lanes)] * 2,
        in_specs=[vmem],
        out_specs=[vmem] * 2,
        name="far_records",
    )(held(gathered))
    pieces = [gathered] + [
        lax.ppermute(value, whole, neighbours(slabs, cols, DEPTH, odd, 1))
        for odd, value in enumerate(to_far)
    ]
    columns = [pieces]
    bit = 1
    while bit < cols:
        columns = columns + [
            [lax.ppermute(piece, "cross", column_pairs(cols, bit)) for piece in group]
            for group in columns
        ]
        bit *= 2
    flat = [piece for group in columns for piece in group]

    span = 2 * DEPTH - 1
    field = (cols, NODES, NODES, lanes)
    scratch_bytes = 4 * (9 * DEPTH + 1 + 5 * span) * int(np.prod(field))
    pressure, momentum, face_even, face_odd, *accels = pl.pallas_call(
        lambda *refs: main_kernel(slabs, cols, *refs),
        out_shape=[f32(NODES, NODES, lanes), near(3, NODES, NODES, lanes)]
        + [near(3, NODES, lanes)] * 2
        + [near(NODES, capacity)] * 5,
        in_specs=[vmem] * (10 + 3 * cols),
        out_specs=[vmem] * 9,
        scratch_shapes=[
            pltpu.VMEM((4 * DEPTH - 1,) + field, F32),
            pltpu.VMEM((4 * DEPTH - 1, cols, NODES, lanes), F32),
            pltpu.VMEM((span,) + field, F32),
            pltpu.VMEM((span,) + field, F32),
            pltpu.VMEM((span,) + field, F32),
            pltpu.VMEM((span + 2,) + field, F32),
            pltpu.VMEM((span + 2,) + field, F32),
        ],
        compiler_params=pltpu.CompilerParams(vmem_limit_bytes=2 * scratch_bytes + 2**23),
        name="sweeps_and_droplets",
    )(
        tiles,
        stiff_w,
        deriv_w,
        spread_w,
        *[held(piece) for piece in flat],
        base_velocity,
        held(own),
        *[held(value) for value in routed],
    )
    acc_own, acc_e1, acc_o1, acc_e2, acc_o2 = accels

    got_e2, got_o2 = [
        lax.ppermute(value, whole, neighbours(slabs, cols, *route))
        for value, route in zip((acc_e2, acc_o2), ROUTES[2:])
    ]
    face_even = lax.ppermute(face_even, "cross", side_pairs(cols, 0))
    if cols > 2:
        face_odd = lax.ppermute(face_odd, "cross", side_pairs(cols, 1))
    momentum, send_e1, send_o1 = pl.pallas_call(
        lambda *refs: middle_kernel(cols, *refs),
        out_shape=[near(3, NODES, NODES, lanes)] + [near(4, NODES, lanes)] * 2,
        in_specs=[vmem] * 5,
        out_specs=[vmem] * 3,
        name="cross_faces",
    )(*[held(value) for value in (momentum, face_even, face_odd, acc_e1, acc_o1)])
    got_e1, got_o1 = [
        lax.ppermute(value, whole, neighbours(slabs, cols, *route))
        for value, route in zip((send_e1, send_o1), ROUTES[:2])
    ]
    momentum, accel = pl.pallas_call(
        lambda *refs: last_kernel(slabs, reach, *refs),
        out_shape=[f32(3, NODES, NODES, lanes), f32(3 * reach, 1, capacity)],
        in_specs=[vmem] * 6,
        out_specs=[vmem] * 2,
        name="stream_faces",
    )(*[held(value) for value in (momentum, got_e1, got_o1, acc_own, got_e2, got_o2)])
    return (pressure, momentum, accel.reshape(1, 1, reach, 3, capacity))


def solution(mesh):
    in_specs = (
        P("stream", "cross", None),
        P("stream", "cross", None),
        P(None, "stream", "cross", None),
        P("stream", "cross", None, None),
        P("stream", "cross", None, None, None),
        P("stream", "cross", None, None, None),
        P("stream", "cross", None, None, None),
        P("stream", "cross", None),
    )
    out_specs = (
        P("stream", "cross", None),
        P(None, "stream", "cross", None),
        P("stream", "cross", None, None, None),
    )
    return jax.shard_map(step, mesh=mesh, in_specs=in_specs, out_specs=out_specs, check_vma=False)
```

```python
import jax
import jax.numpy as jnp
import numpy as np
from jax import lax
from jax.experimental import pallas as pl
from jax.experimental.pallas import tpu as pltpu
from jax.sharding import PartitionSpec as P


SWEEPS = 3
DEPTH = SWEEPS + 1
NODES = 8
MASS_SHIFT = 1.0
UPPER_BOUND = 2.5
LOWER_BOUND = UPPER_BOUND / 30.0
GLL_POINTS = [
    -1.0,
    -0.8717401485096066,
    -0.5917001814331423,
    -0.2092992179024789,
    0.2092992179024789,
    0.5917001814331423,
    0.8717401485096066,
    1.0,
]
F32 = jnp.float32
BF16 = jnp.bfloat16


def legendre_seven(points):
    before = points * 0.0 + 1.0
    current = points
    for order in range(1, 7):
        following = ((2.0 * order + 1.0) * points * current - order * before) / (order + 1.0)
        before = current
        current = following
    return current


def gll_tables():
    gll_nodes = np.array(GLL_POINTS)
    values = legendre_seven(gll_nodes)
    weights = 2.0 / (56.0 * values * values)
    deriv_mat = np.zeros((8, 8))
    for row_idx in range(8):
        for col_idx in range(8):
            if row_idx != col_idx:
                deriv_mat[row_idx, col_idx] = values[row_idx] / (
                    values[col_idx] * (gll_nodes[row_idx] - gll_nodes[col_idx])
                )
    deriv_mat[0, 0] = -14.0
    deriv_mat[7, 7] = 14.0
    return (gll_nodes, weights, deriv_mat)


NODE_POS, WEIGHTS, DERIV = gll_tables()
STIFF = DERIV.T @ (WEIGHTS[:, None] * DERIV)
STIFF_DIAG = np.diag(STIFF)


def split_pair(table):
    high = table.astype(np.float32).astype(jnp.bfloat16)
    low = (table - high.astype(np.float64)).astype(np.float32).astype(jnp.bfloat16)
    return high, low


def lane_weights(matrix, lanes, summed):
    full = np.kron(np.eye(lanes // NODES), matrix.T)
    if summed:
        shared = np.eye(lanes)
        for last in range(NODES - 1, lanes - 1, NODES):
            shared[last, last + 1] = shared[last + 1, last] = 1.0
        full = full @ shared
    high, low = split_pair(full)
    zero = np.zeros_like(np.asarray(low))
    return np.concatenate(
        [np.concatenate([high, low], 1), np.concatenate([high, zero], 1)], 0
    ).astype(jnp.bfloat16)


F_FACE = (DEPTH - 1) * NODES
F_META = F_FACE + 1
F_COUNT = F_FACE + 2
ROUTES = ((1, 0), (1, 1), (2, 0), (2, 1))
T_KY, T_DY = 0, 8
T_WJ, T_QJ, T_WK, T_QK, T_Z7, T_Z0, T_Y7, T_Y0 = range(16, 24)
T_NODE = 24
T_INV = 31
T_WKS = 32
T_COUNT = 33
HALF = NODES // 2


def table_tiles(lanes):
    tiles = np.zeros((T_COUNT, NODES, lanes))
    for turn in range(NODES):
        outer, inner = turn % HALF, turn - turn % HALF
        for row in range(NODES):
            to, of = (row + outer) % NODES, (row - inner) % NODES
            tiles[T_KY + turn, row, :] = STIFF[to, of]
            tiles[T_DY + turn, row, :] = DERIV[to, of]
    reps = lanes // NODES
    tiles[T_WJ] = WEIGHTS[:, None]
    tiles[T_QJ] = STIFF_DIAG[:, None]
    tiles[T_WK] = np.tile(WEIGHTS, reps)[None, :]
    tiles[T_QK] = np.tile(STIFF_DIAG, reps)[None, :]
    place = np.arange(lanes)
    tiles[T_Z7] = ((place % NODES == NODES - 1) & (place < lanes - 1))[None, :]
    tiles[T_Z0] = ((place % NODES == 0) & (place > 0))[None, :]
    assembled = np.tile(WEIGHTS, reps)
    assembled[NODES - 1 : -1 : NODES] += WEIGHTS[0]
    assembled[NODES::NODES] += WEIGHTS[-1]
    tiles[T_WKS] = assembled[None, :]
    tiles[T_Y7, NODES - 1] = 1.0
    tiles[T_Y0, 0] = 1.0
    for row in range(NODES):
        others = [m for m in range(NODES) if m != row]
        scale = 1.0
        for slot, other in enumerate(others):
            tiles[T_NODE + slot, row, :] = NODE_POS[other]
            scale *= NODE_POS[row] - NODE_POS[other]
        tiles[T_INV, row, :] = 1.0 / scale
    return tiles.astype(np.float32)


def swapped_bit(slabs, cols, bit):
    return [
        (i * cols + j, (i ^ bit) * cols + (j ^ 1)) for i in range(slabs) for j in range(cols)
    ]


def neighbours(slabs, cols, distance, odd, swap=0):
    partner = {}
    for low in range(slabs - distance):
        if (low // distance) % 2 == odd:
            partner[low] = low + distance
            partner[low + distance] = low
    pairs = []
    for i in range(slabs):
        for j in range(cols):
            if i in partner:
                pairs.append((i * cols + j, partner[i] * cols + (j ^ swap)))
            else:
                pairs.append((i * cols + j, i * cols + (j ^ 1)))
    return pairs


def column_pairs(cols, bit):
    return [(j, j ^ bit) for j in range(cols)]


def side_pairs(cols, odd):
    pairs = []
    for low in range(cols - 1):
        if low % 2 == odd:
            pairs += [(low, low + 1), (low + 1, low)]
    return pairs


def parity(slot):
    return bin(slot).count("1") % 2


def route_partner(position, route):
    distance, odd = route
    upward = (position // distance) % 2 == odd
    return jnp.where(upward, position + distance, position - distance), upward


def route_block(position, route, reach):
    middle = (reach - 1) // 2
    upward = route_partner(position, route)[1]
    return jnp.where(upward, middle + route[0], middle - route[0])


def route_open(position, route, slabs):
    partner = route_partner(position, route)[0]
    return jnp.logical_and(partner >= 0, partner < slabs)


def split_value(value):
    high = value.astype(BF16)
    low = (value - high.astype(F32)).astype(BF16)
    return high, low


def pack_kernel(cols, elem_z, source, metric, elem, coord, vel, prop, counts, first, own, *rest):
    first[0:NODES] = source[...]
    first[NODES] = jnp.zeros(first.shape[1:], F32)
    first[NODES, 0:1, 0 : metric.shape[-1]] = metric[0]
    routed, state = rest[:-1], rest[-1]
    position = lax.axis_index("stream")
    column = lax.axis_index("cross")
    reach, _, capacity = elem.shape
    middle = (reach - 1) // 2
    slot = lax.broadcasted_iota(jnp.int32, (1, capacity), 1)
    for block in range(reach):
        base = ((position + (block - middle)) * cols + column) * elem_z
        live = slot < counts[0, 0, block]
        ids = jnp.where(live, elem[block] - base + 1, 0).astype(F32)
        for axis in range(3):
            state[block, 0, axis : axis + 1, :] = coord[3 * block + axis]
            state[block, 0, 3 + axis : 4 + axis, :] = vel[3 * block + axis]
        state[block, 0, 6:8, :] = prop[0, 0, block]
        state[block, 1] = jnp.broadcast_to(ids, (NODES, capacity))
    own[...] = state[middle]
    for route, out in zip(ROUTES, routed):
        out[...] = state[route_block(position, route, reach)]


def near_kernel(first, from_source, from_metric, out):
    out[0] = first[...]
    out[1, 0:NODES] = from_source[...]
    out[1, NODES] = jnp.zeros(out.shape[2:], F32)
    out[1, NODES, 0:1, 0 : from_metric.shape[-1]] = from_metric[0]


def far_kernel(gathered, *outs):
    position = lax.axis_index("stream")
    group_even = (position // DEPTH) % 2 == 0
    for odd, out in enumerate(outs):
        upward = group_even if odd == 0 else jnp.logical_not(group_even)
        for slot in range(1, DEPTH):
            for i in range(NODES):
                out[(slot - 1) * NODES + i] = gathered[slot, i]
        out[F_FACE] = gathered[0, jnp.where(upward, NODES - 1, 0)]
        out[F_META] = jnp.zeros(out.shape[1:], F32)
        for slot in range(DEPTH):
            out[F_META, slot : slot + 1, :] = gathered[slot, NODES, 0:1, :]


def z_assembled(block, tiles):
    lanes = block.shape[-1]
    axis = block.ndim - 1
    after = pltpu.roll(block, lanes - 1, axis)
    before = pltpu.roll(block, 1, axis)
    return block + tiles[T_Z7] * after + tiles[T_Z0] * before


def y_assembled(blocks, tiles):
    axis = blocks[0].ndim - 2
    out = []
    for j, block in enumerate(blocks):
        total = block
        if j + 1 < len(blocks):
            total = total + tiles[T_Y7] * pltpu.roll(blocks[j + 1], NODES - 1, axis)
        if j > 0:
            total = total + tiles[T_Y0] * pltpu.roll(blocks[j - 1], 1, axis)
        out.append(total)
    return out


def halves(planes):
    even = [planes[m] + planes[NODES - 1 - m] for m in range(HALF)]
    odd = [planes[m] - planes[NODES - 1 - m] for m in range(HALF)]
    return even, odd


def row_pair(even, odd, matrix, row, mirrored):
    sums = []
    for values, sign in ((even, 0.5), (odd, -0.5)):
        total = None
        for m in range(HALF):
            factor = 0.5 * matrix[row, m] + sign * matrix[row, NODES - 1 - m]
            term = values[m] * float(factor)
            total = term if total is None else total + term
        sums.append(total)
    first = sums[0] + sums[1]
    second = sums[0] - sums[1] if mirrored > 0 else sums[1] - sums[0]
    return first, second


def x_product(planes, matrix, mirrored):
    even, odd = halves(planes)
    pairs = [row_pair(even, odd, matrix, row, mirrored) for row in range(HALF)]
    return [pair[0] for pair in pairs] + [pair[1] for pair in reversed(pairs)]


def y_product(block, tiles, start):
    axis = block.ndim - 2
    far = pltpu.roll(block, HALF, axis)
    total = None
    for outer in range(HALF):
        part = block * tiles[start + outer] + far * tiles[start + HALF + outer]
        if outer > 0:
            part = pltpu.roll(part, outer, axis)
        total = part if total is None else total + part
    return total


def z_product(rows, weights):
    lanes = rows.shape[-1]
    high, low = split_value(rows)
    both = jnp.concatenate([high, low], axis=1)
    wide = jnp.dot(both, weights, preferred_element_type=F32)
    return wide[:, :lanes] + wide[:, lanes:]


def lagrange(row, tiles):
    capacity = row.shape[-1]
    coords = jnp.broadcast_to(row, (NODES, capacity))
    factor = tiles[T_INV]
    for slot in range(NODES - 1):
        factor = factor * (coords - tiles[T_NODE + slot])
    return factor


def main_kernel(slabs, cols, *refs):
    tiles, stiff_w, deriv_w, spread_w = refs[0:4]
    pieces = refs[4 : 4 + 3 * cols]
    base_velocity, own = refs[4 + 3 * cols : 6 + 3 * cols]
    routed = refs[6 + 3 * cols : 10 + 3 * cols]
    (pressure, momentum, face_even, face_odd, acc_own, acc_e1, acc_o1, acc_e2, acc_o2,
     loads, scales, resid, update, inv, work, spans, layers) = refs[10 + 3 * cols :]
    lanes = tiles.shape[-1]
    position = lax.axis_index("stream")
    column = lax.axis_index("cross")
    middle = DEPTH - 1

    group_even = (position // DEPTH) % 2 == 0
    rank = position % DEPTH
    wjk = tiles[T_WJ] * tiles[T_WK]
    flat = (NODES, lanes)

    def present(offset):
        where = position + offset
        return jnp.where((where >= 0) & (where < slabs), 1.0, 0.0).astype(F32)

    factors = []
    for slot_c in range(cols):
        near, *fars = pieces[3 * slot_c : 3 * slot_c + 3]
        factors += [near[slot, NODES, 0:1, :] for slot in range(DEPTH)]
        factors += [jnp.zeros((NODES - DEPTH, lanes), F32)] + [far[F_META] for far in fars]
    high, low = split_value(jnp.concatenate(factors, 0))
    factors = jnp.dot(
        jnp.concatenate([high, low], 1), spread_w[...], preferred_element_type=F32
    )
    for slot_c in range(cols):
        near, *fars = pieces[3 * slot_c : 3 * slot_c + 3]
        for slot in range(DEPTH):
            col = column ^ (slot_c ^ parity(slot))
            at = (rank ^ slot) - rank + (2 * DEPTH - 1)
            for i in range(NODES):
                loads[at, col, i] = near[slot, i] * (wjk * float(WEIGHTS[i]))
            row = 3 * NODES * slot_c + slot
            scales[at, col] = jnp.broadcast_to(factors[row : row + 1], flat)
        for odd, far in enumerate(fars):
            upper = group_even if odd == 0 else jnp.logical_not(group_even)
            shift = jnp.where(upper, DEPTH, -DEPTH)
            inside = present(shift)
            for slot in range(DEPTH):
                col = column ^ (slot_c ^ parity(slot) ^ 1)
                at = (rank ^ slot) - rank + shift + (2 * DEPTH - 1)
                if slot > 0:
                    for i in range(NODES):
                        loads[at, col, i] = far[(slot - 1) * NODES + i] * (
                            wjk * (inside * float(WEIGHTS[i]))
                        )
                else:
                    layer = jnp.where(upper, 0, NODES - 1)
                    loads[at, col, layer] = far[F_FACE] * (wjk * (inside * float(WEIGHTS[0])))
                row = 3 * NODES * slot_c + NODES * (1 + odd) + slot
                scales[at, col] = jnp.broadcast_to(factors[row : row + 1] * inside, flat)
    wide_mid = 2 * DEPTH - 1

    columns = range(cols)
    for offset in range(-DEPTH, DEPTH + 1):
        at = wide_mid + offset
        mass = (MASS_SHIFT * present(offset)) * tiles[T_WKS]
        alphas = [z_assembled(scales[at, j] * tiles[T_WK], tiles) for j in columns]
        betas = [z_assembled(scales[at, j] * tiles[T_QK], tiles) + mass for j in columns]
        sigmas = y_assembled([tiles[T_WJ] * alphas[j] for j in columns], tiles)
        taus = y_assembled([tiles[T_WJ] * scales[at, j] for j in columns], tiles)
        rests = y_assembled(
            [tiles[T_QJ] * alphas[j] + tiles[T_WJ] * betas[j] for j in columns], tiles
        )
        masses = y_assembled([tiles[T_WJ] * mass] * cols, tiles)
        for j in columns:
            for index, value in enumerate((alphas[j], sigmas[j], taus[j], rests[j], masses[j])):
                spans[index, DEPTH + offset, j] = value
        if abs(offset) < DEPTH:
            sides = [loads[at, j] for j in columns]
            sides = y_assembled([z_assembled(side, tiles) for side in sides], tiles)
            for j in columns:
                work[DEPTH + offset, j] = sides[j]
        else:
            layer = NODES - 1 if offset < 0 else 0
            sides = [loads[at, j, layer] for j in columns]
            sides = y_assembled([z_assembled(side, tiles) for side in sides], tiles)
            for j in columns:
                work[DEPTH + offset, j, layer] = sides[j]

    center = (UPPER_BOUND + LOWER_BOUND) / 2.0
    half_width = (UPPER_BOUND - LOWER_BOUND) / 2.0
    ratio_bound = center / half_width
    cheb_rho = 1.0 / ratio_bound
    ends = {0: -1, NODES - 1: 1}

    def joined(index, offset, j, i):
        tile = spans[index, DEPTH + offset, j]
        if i in ends:
            tile = tile + spans[index, DEPTH + offset + ends[i], j]
        return tile

    for offset in range(-middle, middle + 1):
        at = middle + offset
        gap = 1.0 - present(offset)
        for j in columns:
            for i in range(NODES):
                side = work[DEPTH + offset, j, i]
                if i in ends:
                    side = side + work[DEPTH + offset + ends[i], j, NODES - 1 - i]
                diag = joined(1, offset, j, i) * float(STIFF_DIAG[i]) + (
                    joined(3, offset, j, i) * float(WEIGHTS[i]) + gap
                )
                inverse = 1.0 / diag
                inv[at, j, i] = inverse
                resid[at, j, i] = side
                update[at, j, i] = side * inverse * (1.0 / center)

    iterate = update[middle, column]
    for sweep in range(SWEEPS):
        reach = SWEEPS - 1 - sweep
        rho_next = 1.0 / (2.0 * ratio_bound - cheb_rho)
        for offset in range(-reach - 1, reach + 2):
            for j in columns:
                sigma = spans[1, DEPTH + offset, j]
                planes = [sigma * update[middle + offset, j, i] for i in range(NODES)]
                first, last = row_pair(*halves(planes), STIFF, 0, 1)
                layers[DEPTH + offset, j, 0] = first
                layers[DEPTH + offset, j, 1] = last
        for offset in range(-reach, reach + 1):
            at = middle + offset
            weighted = [[update[at, j, i] * float(WEIGHTS[i]) for i in range(NODES)] for j in columns]
            rows = [
                joined(2, offset, j, i) * weighted[j][i] for j in columns for i in range(NODES)
            ]
            from_z = z_product(jnp.concatenate(rows, 0), stiff_w[...])
            from_y = y_assembled(
                [
                    y_product(
                        jnp.stack([joined(0, offset, j, i) * weighted[j][i] for i in range(NODES)], 0),
                        tiles,
                        T_KY,
                    )
                    for j in columns
                ],
                tiles,
            )
            for j in columns:
                sigma = spans[1, DEPTH + offset, j]
                planes = [sigma * update[at, j, i] for i in range(NODES)]
                even, odd = halves(planes)
                from_x = [None] * NODES
                from_x[0] = layers[DEPTH + offset, j, 0] + layers[DEPTH + offset - 1, j, 1]
                from_x[-1] = layers[DEPTH + offset, j, 1] + layers[DEPTH + offset + 1, j, 0]
                for row in range(1, HALF):
                    from_x[row], from_x[NODES - 1 - row] = row_pair(even, odd, STIFF, row, 1)
                for i in range(NODES):
                    row = (j * NODES + i) * NODES
                    total = from_x[i] + from_y[j][i] + from_z[row : row + NODES]
                    total = total + joined(4, offset, j, i) * weighted[j][i]
                    left = resid[at, j, i] - total
                    resid[at, j, i] = left
                    update[at, j, i] = (rho_next * cheb_rho) * update[at, j, i] + (
                        2.0 * rho_next / half_width
                    ) * (inv[at, j, i] * left)
        cheb_rho = rho_next
        iterate = iterate + update[middle, column]
    pressure[...] = iterate

    scale = scales[wide_mid, column]
    planes = [iterate[i] for i in range(NODES)]
    grad_x = x_product(planes, DERIV, -1)
    grad_z = z_product(iterate.reshape(NODES * NODES, lanes), deriv_w[...]).reshape(NODES, NODES, lanes)
    velocity = []
    for i in range(NODES):
        velocity.append(base_velocity[0, i] - scale * grad_x[i])
    for i in range(NODES):
        velocity.append(base_velocity[1, i] - scale * y_product(planes[i], tiles, T_DY))
    for i in range(NODES):
        velocity.append(base_velocity[2, i] - scale * grad_z[i])
    velocity = jnp.concatenate(velocity, 0)

    groups = [(own[0], own[1])]
    for route, group in zip(ROUTES, routed):
        groups.append((group[0], jnp.where(route_open(position, route, slabs), group[1], 0.0)))
    pick, bases = [], []
    for group, ids in groups:
        basis = [lagrange(group[axis : axis + 1, :], tiles) for axis in range(3)]
        pick.append(jnp.concatenate(
            [jnp.where(ids == float(e + 1), basis[2], 0.0) for e in range(lanes // NODES)], 0))
        bases.append(basis)
    pick = jnp.concatenate(pick, 1)
    pick_high, pick_low = split_value(pick)
    vel_high, vel_low = split_value(velocity)
    partial = jnp.dot(
        jnp.concatenate([vel_high, vel_low, vel_high], 1),
        jnp.concatenate([pick_high, pick_high, pick_low], 0),
        preferred_element_type=F32,
    )
    capacity = own.shape[-1]
    spread = []
    for g, ((group, ids), basis) in enumerate(zip(groups, bases)):
        cells = [basis[1] * basis[0][i : i + 1, :] for i in range(NODES)]
        accel_rows, parts = [], []
        for comp in range(3):
            total = None
            for i in range(NODES):
                row = (comp * NODES + i) * NODES
                term = partial[row : row + NODES, g * capacity : (g + 1) * capacity] * cells[i]
                total = term if total is None else total + term
            fluid = jnp.sum(total, axis=0, keepdims=True)
            accel = jnp.where(ids[0:1, :] > 0.5, group[6:7, :] * (fluid - group[3 + comp : 4 + comp, :]), 0.0)
            accel_rows.append(accel)
            force = -group[7:8, :] * accel
            parts += [cells[i] * force for i in range(NODES)]
        accel_rows.append(jnp.zeros((NODES - 3, capacity), F32))
        (acc_own, acc_e1, acc_o1, acc_e2, acc_o2)[g][...] = jnp.concatenate(accel_rows, 0)
        spread.append(jnp.concatenate(parts, 0))
    spread = jnp.concatenate(spread, 1)
    spread_high, spread_low = split_value(spread)
    added = lax.dot_general(
        jnp.concatenate([spread_high, spread_low, spread_high], 1),
        jnp.concatenate([pick_high, pick_high, pick_low], 1),
        (((1,), (1,)), ((), ())),
        preferred_element_type=F32,
    )
    added = z_assembled(added.reshape(3, NODES, NODES, lanes), tiles)
    momentum[...] = added
    low_row = added[:, :, 0, :]
    high_row = added[:, :, NODES - 1, :]
    even = column % 2 == 0
    face_even[...] = jnp.where(even, high_row, low_row)
    face_odd[...] = jnp.where(even, low_row, high_row)


def middle_kernel(cols, momentum, face_even, face_odd, acc_e1, acc_o1, out, send_e1, send_o1):
    position = lax.axis_index("stream")
    column = lax.axis_index("cross")
    even = column % 2 == 0
    high = jnp.where(even, face_even[...], face_odd[...]) if cols > 2 else jnp.where(even, face_even[...], 0.0)
    low = jnp.where(even, face_odd[...], face_even[...]) if cols > 2 else jnp.where(even, 0.0, face_even[...])
    out[...] = momentum[...]
    out[:, :, 0, :] = momentum[:, :, 0, :] + low
    out[:, :, NODES - 1, :] = momentum[:, :, NODES - 1, :] + high
    lower = position % 2 == 0
    top = jnp.where(lower, NODES - 1, 0)
    bottom = NODES - 1 - top
    for comp in range(3):
        send_e1[comp] = out[comp, top]
        send_o1[comp] = out[comp, bottom]
    send_e1[3] = acc_e1[...]
    send_o1[3] = acc_o1[...]


def last_kernel(slabs, reach, momentum, got_e1, got_o1, acc_own, got_e2, got_o2, out, accel):
    position = lax.axis_index("stream")
    lower = position % 2 == 0
    top = jnp.where(lower, NODES - 1, 0)
    bottom = NODES - 1 - top
    out[...] = momentum[...]
    opened = [route_open(position, route, slabs) for route in ROUTES]
    for comp in range(3):
        out[comp, top] = momentum[comp, top] + jnp.where(opened[0], got_e1[comp], 0.0)
        out[comp, bottom] = momentum[comp, bottom] + jnp.where(opened[1], got_o1[comp], 0.0)
    for axis in range(3):
        accel[3 * ((reach - 1) // 2) + axis] = acc_own[axis : axis + 1]
    arrived = (got_e1[3], got_o1[3], got_e2[...], got_o2[...])
    for route, value, there in zip(ROUTES, arrived, opened):
        block = route_block(position, route, reach)
        for axis in range(3):
            accel[3 * block + axis] = jnp.where(there, value[axis : axis + 1], 0.0)


def f32(*shape):
    return jax.ShapeDtypeStruct(shape, F32)


def near(*shape):
    return pltpu.VMEM(shape, F32)


def held(value):
    return pltpu.with_memory_space_constraint(value, pltpu.VMEM)


def step(
    source, metric, base_velocity, drop_elem, drop_coord, drop_vel, drop_prop, drop_counts
):
    slabs = lax.axis_size("stream")
    cols = lax.axis_size("cross")
    lanes = source.shape[-1]
    reach, capacity = drop_elem.shape[2:]
    elem_z = metric.shape[-1]
    vmem = pl.BlockSpec(memory_space=pltpu.VMEM)
    smem = pl.BlockSpec(memory_space=pltpu.SMEM)
    tiles = jnp.asarray(table_tiles(lanes))
    stiff_w = jnp.asarray(lane_weights(STIFF, lanes, True))
    deriv_w = jnp.asarray(lane_weights(DERIV, lanes, False))
    to_lanes = np.zeros((lanes, lanes))
    to_lanes[:elem_z] = np.kron(np.eye(elem_z), np.ones((1, NODES)))
    spread_w = jnp.asarray(np.concatenate([to_lanes, to_lanes], 0), BF16)

    first, own, *routed = pl.pallas_call(
        lambda *refs: pack_kernel(cols, elem_z, *refs),
        out_shape=[near(NODES + 1, NODES, lanes)] + [near(2, NODES, capacity)] * 5,
        in_specs=[vmem] * 6 + [smem],
        out_specs=[vmem] * 6,
        scratch_shapes=[pltpu.VMEM((reach, 2, NODES, capacity), F32)],
        name="pack",
    )(
        source,
        metric,
        drop_elem.reshape(reach, 1, capacity),
        drop_coord.reshape(3 * reach, 1, capacity),
        drop_vel.reshape(3 * reach, 1, capacity),
        drop_prop,
        drop_counts,
    )
    whole = ("stream", "cross")

    routed = [
        lax.ppermute(value, whole, neighbours(slabs, cols, *route))
        for value, route in zip(routed, ROUTES)
    ]
    from_source = lax.ppermute(source, whole, swapped_bit(slabs, cols, 1))
    from_metric = lax.ppermute(metric, whole, swapped_bit(slabs, cols, 1))
    gathered = pl.pallas_call(
        near_kernel,
        out_shape=near(2, NODES + 1, NODES, lanes),
        in_specs=[vmem] * 3,
        out_specs=vmem,
        name="near_pair",
    )(held(first), held(from_source), held(from_metric))
    gathered = jnp.concatenate(
        [gathered, lax.ppermute(gathered, whole, swapped_bit(slabs, cols, 2))], 0
    )
    to_far = pl.pallas_call(
        far_kernel,
        out_shape=[near(F_COUNT, NODES, lanes)] * 2,
        in_specs=[vmem],
        out_specs=[vmem] * 2,
        name="far_records",
    )(held(gathered))
    pieces = [gathered] + [
        lax.ppermute(value, whole, neighbours(slabs, cols, DEPTH, odd, 1))
        for odd, value in enumerate(to_far)
    ]
    columns = [pieces]
    bit = 1
    while bit < cols:
        columns = columns + [
            [lax.ppermute(piece, "cross", column_pairs(cols, bit)) for piece in group]
            for group in columns
        ]
        bit *= 2
    flat = [piece for group in columns for piece in group]

    span = 2 * DEPTH - 1
    field = (cols, NODES, NODES, lanes)
    scratch_bytes = 4 * (9 * DEPTH + 1 + 5 * span) * int(np.prod(field))
    pressure, momentum, face_even, face_odd, *accels = pl.pallas_call(
        lambda *refs: main_kernel(slabs, cols, *refs),
        out_shape=[f32(NODES, NODES, lanes), near(3, NODES, NODES, lanes)]
        + [near(3, NODES, lanes)] * 2
        + [near(NODES, capacity)] * 5,
        in_specs=[vmem] * (10 + 3 * cols),
        out_specs=[vmem] * 9,
        scratch_shapes=[
            pltpu.VMEM((4 * DEPTH - 1,) + field, F32),
            pltpu.VMEM((4 * DEPTH - 1, cols, NODES, lanes), F32),
            pltpu.VMEM((span,) + field, F32),
            pltpu.VMEM((span,) + field, F32),
            pltpu.VMEM((span,) + field, F32),
            pltpu.VMEM((span + 2,) + field, F32),
            pltpu.VMEM((5, span + 2, cols, NODES, lanes), F32),
            pltpu.VMEM((span + 2, cols, 2, NODES, lanes), F32),
        ],
        compiler_params=pltpu.CompilerParams(vmem_limit_bytes=2 * scratch_bytes + 2**23),
        name="sweeps_and_droplets",
    )(
        tiles,
        stiff_w,
        deriv_w,
        spread_w,
        *[held(piece) for piece in flat],
        base_velocity,
        held(own),
        *[held(value) for value in routed],
    )
    acc_own, acc_e1, acc_o1, acc_e2, acc_o2 = accels

    got_e2, got_o2 = [
        lax.ppermute(value, whole, neighbours(slabs, cols, *route))
        for value, route in zip((acc_e2, acc_o2), ROUTES[2:])
    ]
    face_even = lax.ppermute(face_even, "cross", side_pairs(cols, 0))
    if cols > 2:
        face_odd = lax.ppermute(face_odd, "cross", side_pairs(cols, 1))
    momentum, send_e1, send_o1 = pl.pallas_call(
        lambda *refs: middle_kernel(cols, *refs),
        out_shape=[near(3, NODES, NODES, lanes)] + [near(4, NODES, lanes)] * 2,
        in_specs=[vmem] * 5,
        out_specs=[vmem] * 3,
        name="cross_faces",
    )(*[held(value) for value in (momentum, face_even, face_odd, acc_e1, acc_o1)])
    got_e1, got_o1 = [
        lax.ppermute(value, whole, neighbours(slabs, cols, *route))
        for value, route in zip((send_e1, send_o1), ROUTES[:2])
    ]
    momentum, accel = pl.pallas_call(
        lambda *refs: last_kernel(slabs, reach, *refs),
        out_shape=[f32(3, NODES, NODES, lanes), f32(3 * reach, 1, capacity)],
        in_specs=[vmem] * 6,
        out_specs=[vmem] * 2,
        name="stream_faces",
    )(*[held(value) for value in (momentum, got_e1, got_o1, acc_own, got_e2, got_o2)])
    return (pressure, momentum, accel.reshape(1, 1, reach, 3, capacity))


def solution(mesh):
    in_specs = (
        P("stream", "cross", None),
        P("stream", "cross", None),
        P(None, "stream", "cross", None),
        P("stream", "cross", None, None),
        P("stream", "cross", None, None, None),
        P("stream", "cross", None, None, None),
        P("stream", "cross", None, None, None),
        P("stream", "cross", None),
    )
    out_specs = (
        P("stream", "cross", None),
        P(None, "stream", "cross", None),
        P("stream", "cross", None, None, None),
    )
    return jax.shard_map(step, mesh=mesh, in_specs=in_specs, out_specs=out_specs, check_vma=False)
```

```python
import jax
import jax.numpy as jnp
import numpy as np
from jax import lax
from jax.experimental import pallas as pl
from jax.experimental.pallas import tpu as pltpu
from jax.sharding import PartitionSpec as P


SWEEPS = 3
DEPTH = SWEEPS + 1
NODES = 8
MASS_SHIFT = 1.0
UPPER_BOUND = 2.5
LOWER_BOUND = UPPER_BOUND / 30.0
GLL_POINTS = [
    -1.0,
    -0.8717401485096066,
    -0.5917001814331423,
    -0.2092992179024789,
    0.2092992179024789,
    0.5917001814331423,
    0.8717401485096066,
    1.0,
]
F32 = jnp.float32
BF16 = jnp.bfloat16


def legendre_seven(points):
    before = points * 0.0 + 1.0
    current = points
    for order in range(1, 7):
        following = ((2.0 * order + 1.0) * points * current - order * before) / (order + 1.0)
        before = current
        current = following
    return current


def gll_tables():
    gll_nodes = np.array(GLL_POINTS)
    values = legendre_seven(gll_nodes)
    weights = 2.0 / (56.0 * values * values)
    deriv_mat = np.zeros((8, 8))
    for row_idx in range(8):
        for col_idx in range(8):
            if row_idx != col_idx:
                deriv_mat[row_idx, col_idx] = values[row_idx] / (
                    values[col_idx] * (gll_nodes[row_idx] - gll_nodes[col_idx])
                )
    deriv_mat[0, 0] = -14.0
    deriv_mat[7, 7] = 14.0
    return (gll_nodes, weights, deriv_mat)


NODE_POS, WEIGHTS, DERIV = gll_tables()
STIFF = DERIV.T @ (WEIGHTS[:, None] * DERIV)
STIFF_DIAG = np.diag(STIFF)


def split_pair(table):
    high = table.astype(np.float32).astype(jnp.bfloat16)
    low = (table - high.astype(np.float64)).astype(np.float32).astype(jnp.bfloat16)
    return high, low


def lane_weights(matrix, lanes, summed):
    full = np.kron(np.eye(lanes // NODES), matrix.T)
    if summed:
        shared = np.eye(lanes)
        for last in range(NODES - 1, lanes - 1, NODES):
            shared[last, last + 1] = shared[last + 1, last] = 1.0
        full = full @ shared
    high, low = split_pair(full)
    zero = np.zeros_like(np.asarray(low))
    return np.concatenate(
        [np.concatenate([high, low], 1), np.concatenate([high, zero], 1)], 0
    ).astype(jnp.bfloat16)


F_FACE = (DEPTH - 1) * NODES
F_META = F_FACE + 1
F_COUNT = F_FACE + 2
ROUTES = ((1, 0), (1, 1), (2, 0), (2, 1))
T_KY, T_DY = 0, 8
T_WJ, T_QJ, T_WK, T_QK, T_Z7, T_Z0, T_Y7, T_Y0 = range(16, 24)
T_NODE = 24
T_INV = 31
T_WKS = 32
T_COUNT = 33
HALF = NODES // 2


def table_tiles(lanes):
    tiles = np.zeros((T_COUNT, NODES, lanes))
    for turn in range(NODES):
        outer, inner = turn % HALF, turn - turn % HALF
        for row in range(NODES):
            to, of = (row + outer) % NODES, (row - inner) % NODES
            tiles[T_KY + turn, row, :] = STIFF[to, of]
            tiles[T_DY + turn, row, :] = DERIV[to, of]
    reps = lanes // NODES
    tiles[T_WJ] = WEIGHTS[:, None]
    tiles[T_QJ] = STIFF_DIAG[:, None]
    tiles[T_WK] = np.tile(WEIGHTS, reps)[None, :]
    tiles[T_QK] = np.tile(STIFF_DIAG, reps)[None, :]
    place = np.arange(lanes)
    tiles[T_Z7] = ((place % NODES == NODES - 1) & (place < lanes - 1))[None, :]
    tiles[T_Z0] = ((place % NODES == 0) & (place > 0))[None, :]
    assembled = np.tile(WEIGHTS, reps)
    assembled[NODES - 1 : -1 : NODES] += WEIGHTS[0]
    assembled[NODES::NODES] += WEIGHTS[-1]
    tiles[T_WKS] = assembled[None, :]
    tiles[T_Y7, NODES - 1] = 1.0
    tiles[T_Y0, 0] = 1.0
    for row in range(NODES):
        others = [m for m in range(NODES) if m != row]
        scale = 1.0
        for slot, other in enumerate(others):
            tiles[T_NODE + slot, row, :] = NODE_POS[other]
            scale *= NODE_POS[row] - NODE_POS[other]
        tiles[T_INV, row, :] = 1.0 / scale
    return tiles.astype(np.float32)


def swapped_bit(slabs, cols, bit):
    return [
        (i * cols + j, (i ^ bit) * cols + (j ^ 1)) for i in range(slabs) for j in range(cols)
    ]


def neighbours(slabs, cols, distance, odd, swap=0):
    partner = {}
    for low in range(slabs - distance):
        if (low // distance) % 2 == odd:
            partner[low] = low + distance
            partner[low + distance] = low
    pairs = []
    for i in range(slabs):
        for j in range(cols):
            if i in partner:
                pairs.append((i * cols + j, partner[i] * cols + (j ^ swap)))
            else:
                pairs.append((i * cols + j, i * cols + (j ^ 1)))
    return pairs


def column_pairs(cols, bit):
    return [(j, j ^ bit) for j in range(cols)]


def side_pairs(cols, odd):
    pairs = []
    for low in range(cols - 1):
        if low % 2 == odd:
            pairs += [(low, low + 1), (low + 1, low)]
    return pairs


def parity(slot):
    return bin(slot).count("1") % 2


def route_partner(position, route):
    distance, odd = route
    upward = (position // distance) % 2 == odd
    return jnp.where(upward, position + distance, position - distance), upward


def route_block(position, route, reach):
    middle = (reach - 1) // 2
    upward = route_partner(position, route)[1]
    return jnp.where(upward, middle + route[0], middle - route[0])


def route_open(position, route, slabs):
    partner = route_partner(position, route)[0]
    return jnp.logical_and(partner >= 0, partner < slabs)


def split_value(value):
    high = value.astype(BF16)
    low = (value - high.astype(F32)).astype(BF16)
    return high, low


def pack_kernel(cols, elem_z, source, metric, elem, coord, vel, prop, counts, first, own, *rest):
    first[0:NODES] = source[...]
    first[NODES] = jnp.zeros(first.shape[1:], F32)
    first[NODES, 0:1, 0 : metric.shape[-1]] = metric[0]
    routed, state = rest[:-1], rest[-1]
    position = lax.axis_index("stream")
    column = lax.axis_index("cross")
    reach, _, capacity = elem.shape
    middle = (reach - 1) // 2
    slot = lax.broadcasted_iota(jnp.int32, (1, capacity), 1)
    for block in range(reach):
        base = ((position + (block - middle)) * cols + column) * elem_z
        live = slot < counts[0, 0, block]
        ids = jnp.where(live, elem[block] - base + 1, 0).astype(F32)
        for axis in range(3):
            state[block, 0, axis : axis + 1, :] = coord[3 * block + axis]
            state[block, 0, 3 + axis : 4 + axis, :] = vel[3 * block + axis]
        state[block, 0, 6:8, :] = prop[0, 0, block]
        state[block, 1] = jnp.broadcast_to(ids, (NODES, capacity))
    own[...] = state[middle]
    for route, out in zip(ROUTES, routed):
        out[...] = state[route_block(position, route, reach)]


def near_kernel(first, from_source, from_metric, out):
    out[0] = first[...]
    out[1, 0:NODES] = from_source[...]
    out[1, NODES] = jnp.zeros(out.shape[2:], F32)
    out[1, NODES, 0:1, 0 : from_metric.shape[-1]] = from_metric[0]


def far_kernel(gathered, *outs):
    position = lax.axis_index("stream")
    group_even = (position // DEPTH) % 2 == 0
    for odd, out in enumerate(outs):
        upward = group_even if odd == 0 else jnp.logical_not(group_even)
        for slot in range(1, DEPTH):
            for i in range(NODES):
                out[(slot - 1) * NODES + i] = gathered[slot, i]
        out[F_FACE] = gathered[0, jnp.where(upward, NODES - 1, 0)]
        out[F_META] = jnp.zeros(out.shape[1:], F32)
        for slot in range(DEPTH):
            out[F_META, slot : slot + 1, :] = gathered[slot, NODES, 0:1, :]


def z_assembled(block, tiles):
    lanes = block.shape[-1]
    axis = block.ndim - 1
    after = pltpu.roll(block, lanes - 1, axis)
    before = pltpu.roll(block, 1, axis)
    return block + tiles[T_Z7] * after + tiles[T_Z0] * before


def y_assembled(blocks, tiles):
    axis = blocks[0].ndim - 2
    out = []
    for j, block in enumerate(blocks):
        total = block
        if j + 1 < len(blocks):
            total = total + tiles[T_Y7] * pltpu.roll(blocks[j + 1], NODES - 1, axis)
        if j > 0:
            total = total + tiles[T_Y0] * pltpu.roll(blocks[j - 1], 1, axis)
        out.append(total)
    return out


def halves(planes):
    even = [planes[m] + planes[NODES - 1 - m] for m in range(HALF)]
    odd = [planes[m] - planes[NODES - 1 - m] for m in range(HALF)]
    return even, odd


def row_pair(even, odd, matrix, row, mirrored):
    sums = []
    for values, sign in ((even, 0.5), (odd, -0.5)):
        total = None
        for m in range(HALF):
            factor = 0.5 * matrix[row, m] + sign * matrix[row, NODES - 1 - m]
            term = values[m] * float(factor)
            total = term if total is None else total + term
        sums.append(total)
    first = sums[0] + sums[1]
    second = sums[0] - sums[1] if mirrored > 0 else sums[1] - sums[0]
    return first, second


def x_product(planes, matrix, mirrored):
    even, odd = halves(planes)
    pairs = [row_pair(even, odd, matrix, row, mirrored) for row in range(HALF)]
    return [pair[0] for pair in pairs] + [pair[1] for pair in reversed(pairs)]


def y_product(block, tiles, start):
    axis = block.ndim - 2
    far = pltpu.roll(block, HALF, axis)
    total = None
    for outer in range(HALF):
        part = block * tiles[start + outer] + far * tiles[start + HALF + outer]
        if outer > 0:
            part = pltpu.roll(part, outer, axis)
        total = part if total is None else total + part
    return total


def z_product(rows, weights):
    lanes = rows.shape[-1]
    high, low = split_value(rows)
    both = jnp.concatenate([high, low], axis=1)
    wide = jnp.dot(both, weights, preferred_element_type=F32)
    return wide[:, :lanes] + wide[:, lanes:]


def lagrange(row, tiles):
    capacity = row.shape[-1]
    coords = jnp.broadcast_to(row, (NODES, capacity))
    factor = tiles[T_INV]
    for slot in range(NODES - 1):
        factor = factor * (coords - tiles[T_NODE + slot])
    return factor


def basis_kernel(slabs, tiles, own, *rest):
    routed, (high, low, cells, live) = rest[:4], rest[4:]
    position = lax.axis_index("stream")
    lanes, capacity = tiles.shape[-1], own.shape[-1]
    opened = [None] + [route_open(position, route, slabs) for route in ROUTES]
    for g, (group, there) in enumerate(zip((own,) + tuple(routed), opened)):
        ids = group[1]
        if there is not None:
            ids = jnp.where(there, ids, 0.0)
        live[g] = ids
        basis = [lagrange(group[0, axis : axis + 1, :], tiles) for axis in range(3)]
        pick = jnp.concatenate(
            [jnp.where(ids == float(e + 1), basis[2], 0.0) for e in range(lanes // NODES)], 0
        )
        place = slice(g * capacity, (g + 1) * capacity)
        high[:, place], low[:, place] = split_value(pick)
        for i in range(NODES):
            cells[g, i] = basis[1] * basis[0][i : i + 1, :]


def main_kernel(slabs, cols, *refs):
    tiles, stiff_w, deriv_w, spread_w = refs[0:4]
    pieces = refs[4 : 4 + 3 * cols]
    base_velocity, own = refs[4 + 3 * cols : 6 + 3 * cols]
    routed = refs[6 + 3 * cols : 10 + 3 * cols]
    picks_high, picks_low, cells_ref, live = refs[10 + 3 * cols : 14 + 3 * cols]
    (pressure, momentum, face_even, acc_own, acc_e1, acc_o1, acc_e2, acc_o2,
     *face_odd, loads, scales, resid, update, inv, work, spans, layers) = refs[14 + 3 * cols :]
    lanes = tiles.shape[-1]
    position = lax.axis_index("stream")
    column = lax.axis_index("cross")
    middle = DEPTH - 1

    group_even = (position // DEPTH) % 2 == 0
    rank = position % DEPTH
    wjk = tiles[T_WJ] * tiles[T_WK]
    flat = (NODES, lanes)

    def present(offset):
        where = position + offset
        return jnp.where((where >= 0) & (where < slabs), 1.0, 0.0).astype(F32)

    factors = []
    for slot_c in range(cols):
        near, *fars = pieces[3 * slot_c : 3 * slot_c + 3]
        factors += [near[slot, NODES, 0:1, :] for slot in range(DEPTH)]
        factors += [jnp.zeros((NODES - DEPTH, lanes), F32)] + [far[F_META] for far in fars]
    high, low = split_value(jnp.concatenate(factors, 0))
    factors = jnp.dot(
        jnp.concatenate([high, low], 1), spread_w[...], preferred_element_type=F32
    )
    for slot_c in range(cols):
        near, *fars = pieces[3 * slot_c : 3 * slot_c + 3]
        for slot in range(DEPTH):
            col = column ^ (slot_c ^ parity(slot))
            at = (rank ^ slot) - rank + (2 * DEPTH - 1)
            for i in range(NODES):
                loads[at, col, i] = near[slot, i] * (wjk * float(WEIGHTS[i]))
            row = 3 * NODES * slot_c + slot
            scales[at, col] = jnp.broadcast_to(factors[row : row + 1], flat)
        for odd, far in enumerate(fars):
            upper = group_even if odd == 0 else jnp.logical_not(group_even)
            shift = jnp.where(upper, DEPTH, -DEPTH)
            inside = present(shift)
            for slot in range(DEPTH):
                col = column ^ (slot_c ^ parity(slot) ^ 1)
                at = (rank ^ slot) - rank + shift + (2 * DEPTH - 1)
                if slot > 0:
                    for i in range(NODES):
                        loads[at, col, i] = far[(slot - 1) * NODES + i] * (
                            wjk * (inside * float(WEIGHTS[i]))
                        )
                else:
                    layer = jnp.where(upper, 0, NODES - 1)
                    loads[at, col, layer] = far[F_FACE] * (wjk * (inside * float(WEIGHTS[0])))
                row = 3 * NODES * slot_c + NODES * (1 + odd) + slot
                scales[at, col] = jnp.broadcast_to(factors[row : row + 1] * inside, flat)
    wide_mid = 2 * DEPTH - 1

    columns = range(cols)
    for offset in range(-DEPTH, DEPTH + 1):
        at = wide_mid + offset
        mass = (MASS_SHIFT * present(offset)) * tiles[T_WKS]
        alphas = [z_assembled(scales[at, j] * tiles[T_WK], tiles) for j in columns]
        betas = [z_assembled(scales[at, j] * tiles[T_QK], tiles) + mass for j in columns]
        sigmas = y_assembled([tiles[T_WJ] * alphas[j] for j in columns], tiles)
        taus = y_assembled([tiles[T_WJ] * scales[at, j] for j in columns], tiles)
        rests = y_assembled(
            [tiles[T_QJ] * alphas[j] + tiles[T_WJ] * betas[j] for j in columns], tiles
        )
        masses = y_assembled([tiles[T_WJ] * mass] * cols, tiles)
        for j in columns:
            for index, value in enumerate((alphas[j], sigmas[j], taus[j], rests[j], masses[j])):
                spans[index, DEPTH + offset, j] = value
        if abs(offset) < DEPTH:
            sides = [loads[at, j] for j in columns]
            sides = y_assembled([z_assembled(side, tiles) for side in sides], tiles)
            for j in columns:
                work[DEPTH + offset, j] = sides[j]
        else:
            layer = NODES - 1 if offset < 0 else 0
            sides = [loads[at, j, layer] for j in columns]
            sides = y_assembled([z_assembled(side, tiles) for side in sides], tiles)
            for j in columns:
                work[DEPTH + offset, j, layer] = sides[j]

    center = (UPPER_BOUND + LOWER_BOUND) / 2.0
    half_width = (UPPER_BOUND - LOWER_BOUND) / 2.0
    ratio_bound = center / half_width
    cheb_rho = 1.0 / ratio_bound
    ends = {0: -1, NODES - 1: 1}

    def joined(index, offset, j, i):
        tile = spans[index, DEPTH + offset, j]
        if i in ends:
            tile = tile + spans[index, DEPTH + offset + ends[i], j]
        return tile

    for offset in range(-middle, middle + 1):
        at = middle + offset
        gap = 1.0 - present(offset)
        for j in columns:
            for i in range(NODES):
                side = work[DEPTH + offset, j, i]
                if i in ends:
                    side = side + work[DEPTH + offset + ends[i], j, NODES - 1 - i]
                diag = joined(1, offset, j, i) * float(STIFF_DIAG[i]) + (
                    joined(3, offset, j, i) * float(WEIGHTS[i]) + gap
                )
                inverse = 1.0 / diag
                inv[at, j, i] = inverse
                resid[at, j, i] = side
                update[at, j, i] = side * inverse * (1.0 / center)

    iterate = update[middle, column]
    for sweep in range(SWEEPS):
        reach = SWEEPS - 1 - sweep
        rho_next = 1.0 / (2.0 * ratio_bound - cheb_rho)
        for offset in range(-reach - 1, reach + 2):
            for j in columns:
                sigma = spans[1, DEPTH + offset, j]
                planes = [sigma * update[middle + offset, j, i] for i in range(NODES)]
                first, last = row_pair(*halves(planes), STIFF, 0, 1)
                layers[DEPTH + offset, j, 0] = first
                layers[DEPTH + offset, j, 1] = last
        for offset in range(-reach, reach + 1):
            at = middle + offset
            weighted = [[update[at, j, i] * float(WEIGHTS[i]) for i in range(NODES)] for j in columns]
            rows = [
                joined(2, offset, j, i) * weighted[j][i] for j in columns for i in range(NODES)
            ]
            from_z = z_product(jnp.concatenate(rows, 0), stiff_w[...])
            from_y = y_assembled(
                [
                    y_product(
                        jnp.stack([joined(0, offset, j, i) * weighted[j][i] for i in range(NODES)], 0),
                        tiles,
                        T_KY,
                    )
                    for j in columns
                ],
                tiles,
            )
            for j in columns:
                sigma = spans[1, DEPTH + offset, j]
                planes = [sigma * update[at, j, i] for i in range(NODES)]
                even, odd = halves(planes)
                from_x = [None] * NODES
                from_x[0] = layers[DEPTH + offset, j, 0] + layers[DEPTH + offset - 1, j, 1]
                from_x[-1] = layers[DEPTH + offset, j, 1] + layers[DEPTH + offset + 1, j, 0]
                for row in range(1, HALF):
                    from_x[row], from_x[NODES - 1 - row] = row_pair(even, odd, STIFF, row, 1)
                for i in range(NODES):
                    row = (j * NODES + i) * NODES
                    total = from_x[i] + from_y[j][i] + from_z[row : row + NODES]
                    total = total + joined(4, offset, j, i) * weighted[j][i]
                    left = resid[at, j, i] - total
                    resid[at, j, i] = left
                    update[at, j, i] = (rho_next * cheb_rho) * update[at, j, i] + (
                        2.0 * rho_next / half_width
                    ) * (inv[at, j, i] * left)
        cheb_rho = rho_next
        iterate = iterate + update[middle, column]
    pressure[...] = iterate

    scale = scales[wide_mid, column]
    planes = [iterate[i] for i in range(NODES)]
    grad_x = x_product(planes, DERIV, -1)
    grad_z = z_product(iterate.reshape(NODES * NODES, lanes), deriv_w[...]).reshape(NODES, NODES, lanes)
    velocity = []
    for i in range(NODES):
        velocity.append(base_velocity[0, i] - scale * grad_x[i])
    for i in range(NODES):
        velocity.append(base_velocity[1, i] - scale * y_product(planes[i], tiles, T_DY))
    for i in range(NODES):
        velocity.append(base_velocity[2, i] - scale * grad_z[i])
    velocity = jnp.concatenate(velocity, 0)

    pick_high, pick_low = picks_high[...], picks_low[...]
    vel_high, vel_low = split_value(velocity)
    partial = jnp.dot(
        jnp.concatenate([vel_high, vel_low, vel_high], 1),
        jnp.concatenate([pick_high, pick_high, pick_low], 0),
        preferred_element_type=F32,
    )
    capacity = own.shape[-1]
    spread = []
    for g, group in enumerate((own,) + tuple(routed)):
        group, ids = group.at[0], live.at[g]
        cells = [cells_ref[g, i] for i in range(NODES)]
        accel_rows, parts = [], []
        for comp in range(3):
            total = None
            for i in range(NODES):
                row = (comp * NODES + i) * NODES
                term = partial[row : row + NODES, g * capacity : (g + 1) * capacity] * cells[i]
                total = term if total is None else total + term
            fluid = jnp.sum(total, axis=0, keepdims=True)
            accel = jnp.where(ids[0:1, :] > 0.5, group[6:7, :] * (fluid - group[3 + comp : 4 + comp, :]), 0.0)
            accel_rows.append(accel)
            force = -group[7:8, :] * accel
            parts += [cells[i] * force for i in range(NODES)]
        accel_rows.append(jnp.zeros((NODES - 3, capacity), F32))
        (acc_own, acc_e1, acc_o1, acc_e2, acc_o2)[g][...] = jnp.concatenate(accel_rows, 0)
        spread.append(jnp.concatenate(parts, 0))
    spread = jnp.concatenate(spread, 1)
    spread_high, spread_low = split_value(spread)
    added = lax.dot_general(
        jnp.concatenate([spread_high, spread_low, spread_high], 1),
        jnp.concatenate([pick_high, pick_high, pick_low], 1),
        (((1,), (1,)), ((), ())),
        preferred_element_type=F32,
    )
    added = z_assembled(added.reshape(3, NODES, NODES, lanes), tiles)
    momentum[...] = added
    low_row = added[:, :, 0, :]
    high_row = added[:, :, NODES - 1, :]
    even = column % 2 == 0
    face_even[...] = jnp.where(even, high_row, low_row)
    if face_odd:
        face_odd[0][...] = jnp.where(even, low_row, high_row)


def middle_kernel(momentum, face_even, face_odd, acc_e1, acc_o1, out, send_e1, send_o1):
    position = lax.axis_index("stream")
    column = lax.axis_index("cross")
    even = column % 2 == 0
    high = jnp.where(even, face_even[...], face_odd[...])
    low = jnp.where(even, face_odd[...], face_even[...])
    out[...] = momentum[...]
    out[:, :, 0, :] = momentum[:, :, 0, :] + low
    out[:, :, NODES - 1, :] = momentum[:, :, NODES - 1, :] + high
    lower = position % 2 == 0
    top = jnp.where(lower, NODES - 1, 0)
    bottom = NODES - 1 - top
    for comp in range(3):
        send_e1[comp] = out[comp, top]
        send_o1[comp] = out[comp, bottom]
    send_e1[3] = acc_e1[...]
    send_o1[3] = acc_o1[...]


def bundle_kernel(momentum, face_even, acc_e1, acc_o1, acc_o2, out):
    side = jnp.where(lax.axis_index("stream") % 2 == 0, NODES - 1, 0)
    for comp in range(3):
        out[comp] = face_even[comp]
        out[3 + comp] = momentum[comp, side]
        out[6 + comp] = momentum[comp, NODES - 1 - side]
    out[9] = acc_e1[...]
    out[10] = acc_o1[...]
    out[11] = acc_o2[...]


def exchange_kernel(momentum, got, out, send_e1, send_o1, send_o2):
    even = lax.axis_index("cross") % 2 == 0
    side = jnp.where(lax.axis_index("stream") % 2 == 0, NODES - 1, 0)
    layer = got[0:3]
    out[...] = momentum[...]
    out[:, :, 0, :] = momentum[:, :, 0, :] + jnp.where(even, 0.0, layer)
    out[:, :, NODES - 1, :] = momentum[:, :, NODES - 1, :] + jnp.where(even, layer, 0.0)
    here = jnp.where(even, NODES - 1, 0)
    there = pl.ds(NODES - 1 - here, 1)
    for comp in range(3):
        for send, start, at in ((send_e1, 3, side), (send_o1, 6, NODES - 1 - side)):
            send[comp] = got[start + comp]
            edge = momentum[comp, at, pl.ds(here, 1), :]
            send[comp, there, :] = got[start + comp, there, :] + edge
    send_e1[3] = got[9]
    send_o1[3] = got[10]
    send_o2[...] = got[11]


def last_kernel(
    slabs, reach, iterate, momentum, got_e1, got_o1, acc_own, got_e2, got_o2, pressure, out, accel
):
    pressure[...] = iterate[...]
    position = lax.axis_index("stream")
    lower = position % 2 == 0
    top = jnp.where(lower, NODES - 1, 0)
    bottom = NODES - 1 - top
    out[...] = momentum[...]
    opened = [route_open(position, route, slabs) for route in ROUTES]
    for comp in range(3):
        out[comp, top] = momentum[comp, top] + jnp.where(opened[0], got_e1[comp], 0.0)
        out[comp, bottom] = momentum[comp, bottom] + jnp.where(opened[1], got_o1[comp], 0.0)
    for axis in range(3):
        accel[3 * ((reach - 1) // 2) + axis] = acc_own[axis : axis + 1]
    arrived = (got_e1[3], got_o1[3], got_e2[...], got_o2[...])
    for route, value, there in zip(ROUTES, arrived, opened):
        block = route_block(position, route, reach)
        for axis in range(3):
            accel[3 * block + axis] = jnp.where(there, value[axis : axis + 1], 0.0)


def f32(*shape):
    return jax.ShapeDtypeStruct(shape, F32)


def near(*shape):
    return pltpu.VMEM(shape, F32)


def held(value):
    return pltpu.with_memory_space_constraint(value, pltpu.VMEM)


def step(
    source, metric, base_velocity, drop_elem, drop_coord, drop_vel, drop_prop, drop_counts
):
    slabs = lax.axis_size("stream")
    cols = lax.axis_size("cross")
    lanes = source.shape[-1]
    reach, capacity = drop_elem.shape[2:]
    elem_z = metric.shape[-1]
    vmem = pl.BlockSpec(memory_space=pltpu.VMEM)
    smem = pl.BlockSpec(memory_space=pltpu.SMEM)
    tiles = jnp.asarray(table_tiles(lanes))
    stiff_w = jnp.asarray(lane_weights(STIFF, lanes, True))
    deriv_w = jnp.asarray(lane_weights(DERIV, lanes, False))
    to_lanes = np.zeros((lanes, lanes))
    to_lanes[:elem_z] = np.kron(np.eye(elem_z), np.ones((1, NODES)))
    spread_w = jnp.asarray(np.concatenate([to_lanes, to_lanes], 0), BF16)

    first, own, *routed = pl.pallas_call(
        lambda *refs: pack_kernel(cols, elem_z, *refs),
        out_shape=[near(NODES + 1, NODES, lanes)] + [near(2, NODES, capacity)] * 5,
        in_specs=[vmem] * 6 + [smem],
        out_specs=[vmem] * 6,
        scratch_shapes=[pltpu.VMEM((reach, 2, NODES, capacity), F32)],
        name="pack",
    )(
        source,
        metric,
        drop_elem.reshape(reach, 1, capacity),
        drop_coord.reshape(3 * reach, 1, capacity),
        drop_vel.reshape(3 * reach, 1, capacity),
        drop_prop,
        drop_counts,
    )
    whole = ("stream", "cross")

    routed = [
        lax.ppermute(value, whole, neighbours(slabs, cols, *route))
        for value, route in zip(routed, ROUTES)
    ]
    from_source = lax.ppermute(source, whole, swapped_bit(slabs, cols, 1))
    from_metric = lax.ppermute(metric, whole, swapped_bit(slabs, cols, 1))
    gathered = pl.pallas_call(
        near_kernel,
        out_shape=near(2, NODES + 1, NODES, lanes),
        in_specs=[vmem] * 3,
        out_specs=vmem,
        name="near_pair",
    )(held(first), held(from_source), held(from_metric))
    gathered = jnp.concatenate(
        [gathered, lax.ppermute(gathered, whole, swapped_bit(slabs, cols, 2))], 0
    )
    to_far = pl.pallas_call(
        far_kernel,
        out_shape=[near(F_COUNT, NODES, lanes)] * 2,
        in_specs=[vmem],
        out_specs=[vmem] * 2,
        name="far_records",
    )(held(gathered))
    pieces = [gathered] + [
        lax.ppermute(value, whole, neighbours(slabs, cols, DEPTH, odd, 1))
        for odd, value in enumerate(to_far)
    ]
    columns = [pieces]
    bit = 1
    while bit < cols:
        columns = columns + [
            [lax.ppermute(piece, "cross", column_pairs(cols, bit)) for piece in group]
            for group in columns
        ]
        bit *= 2
    flat = [piece for group in columns for piece in group]

    span = 2 * DEPTH - 1
    field = (cols, NODES, NODES, lanes)
    scratch_bytes = 4 * (9 * DEPTH + 1 + 5 * span) * int(np.prod(field))
    slots = 5 * capacity
    bases = pl.pallas_call(
        lambda *refs: basis_kernel(slabs, *refs),
        out_shape=[pltpu.VMEM((lanes, slots), BF16)] * 2
        + [near(5, NODES, NODES, capacity), near(5, NODES, capacity)],
        in_specs=[vmem] * 6,
        out_specs=[vmem] * 4,
        name="bases",
    )(held(tiles), held(own), *[held(value) for value in routed])
    pressure, momentum, face_even, *accels = pl.pallas_call(
        lambda *refs: main_kernel(slabs, cols, *refs),
        out_shape=[near(NODES, NODES, lanes), near(3, NODES, NODES, lanes)]
        + [near(3, NODES, lanes)]
        + [near(NODES, capacity)] * 5
        + [near(3, NODES, lanes)] * (cols > 2),
        in_specs=[vmem] * (14 + 3 * cols),
        out_specs=[vmem] * (8 + (cols > 2)),
        scratch_shapes=[
            pltpu.VMEM((4 * DEPTH - 1,) + field, F32),
            pltpu.VMEM((4 * DEPTH - 1, cols, NODES, lanes), F32),
            pltpu.VMEM((span,) + field, F32),
            pltpu.VMEM((span,) + field, F32),
            pltpu.VMEM((span,) + field, F32),
            pltpu.VMEM((span + 2,) + field, F32),
            pltpu.VMEM((5, span + 2, cols, NODES, lanes), F32),
            pltpu.VMEM((span + 2, cols, 2, NODES, lanes), F32),
        ],
        compiler_params=pltpu.CompilerParams(vmem_limit_bytes=2 * scratch_bytes + 2**23),
        name="sweeps_and_droplets",
    )(
        tiles,
        stiff_w,
        deriv_w,
        spread_w,
        *[held(piece) for piece in flat],
        base_velocity,
        held(own),
        *[held(value) for value in (*routed, *bases)],
    )
    acc_own, acc_e1, acc_o1, acc_e2, acc_o2, *face_odd = accels

    def returned(value, index, swap):
        pairs = neighbours(slabs, cols, *ROUTES[index], swap)
        return lax.ppermute(value, whole, pairs)

    got_e2 = returned(acc_e2, 2, 0)
    if cols == 2:
        swap = 1
        bundle = pl.pallas_call(
            bundle_kernel,
            out_shape=near(12, NODES, lanes),
            in_specs=[vmem] * 5,
            out_specs=vmem,
            name="bundle",
        )(*[held(value) for value in (momentum, face_even, acc_e1, acc_o1, acc_o2)])
        bundle = lax.ppermute(bundle, "cross", side_pairs(cols, 0))
        momentum, send_e1, send_o1, send_o2 = pl.pallas_call(
            exchange_kernel,
            out_shape=[near(3, NODES, NODES, lanes)]
            + [near(4, NODES, lanes)] * 2
            + [near(NODES, capacity)],
            in_specs=[vmem] * 2,
            out_specs=[vmem] * 4,
            name="cross_faces",
        )(held(momentum), held(bundle))
    else:
        swap = 0
        face_even = lax.ppermute(face_even, "cross", side_pairs(cols, 0))
        face_odd = lax.ppermute(face_odd[0], "cross", side_pairs(cols, 1))
        momentum, send_e1, send_o1 = pl.pallas_call(
            middle_kernel,
            out_shape=[near(3, NODES, NODES, lanes)] + [near(4, NODES, lanes)] * 2,
            in_specs=[vmem] * 5,
            out_specs=[vmem] * 3,
            name="cross_faces",
        )(*[held(value) for value in (momentum, face_even, face_odd, acc_e1, acc_o1)])
        send_o2 = acc_o2
    got_o2 = returned(send_o2, 3, swap)
    got_e1 = returned(send_e1, 0, swap)
    got_o1 = returned(send_o1, 1, swap)
    pressure, momentum, accel = pl.pallas_call(
        lambda *refs: last_kernel(slabs, reach, *refs),
        out_shape=[f32(NODES, NODES, lanes), f32(3, NODES, NODES, lanes), f32(3 * reach, 1, capacity)],
        in_specs=[vmem] * 7,
        out_specs=[vmem] * 3,
        name="stream_faces",
    )(*[held(value) for value in (pressure, momentum, got_e1, got_o1, acc_own, got_e2, got_o2)])
    return (pressure, momentum, accel.reshape(1, 1, reach, 3, capacity))


def solution(mesh):
    in_specs = (
        P("stream", "cross", None),
        P("stream", "cross", None),
        P(None, "stream", "cross", None),
        P("stream", "cross", None, None),
        P("stream", "cross", None, None, None),
        P("stream", "cross", None, None, None),
        P("stream", "cross", None, None, None),
        P("stream", "cross", None),
    )
    out_specs = (
        P("stream", "cross", None),
        P(None, "stream", "cross", None),
        P("stream", "cross", None, None, None),
    )
    return jax.shard_map(step, mesh=mesh, in_specs=in_specs, out_specs=out_specs, check_vma=False)
```

```python
import jax
import jax.numpy as jnp
import numpy as np
from jax import lax
from jax.experimental import pallas as pl
from jax.experimental.pallas import tpu as pltpu
from jax.sharding import PartitionSpec as P


SWEEPS = 3
DEPTH = SWEEPS + 1
NODES = 8
MASS_SHIFT = 1.0
UPPER_BOUND = 2.5
LOWER_BOUND = UPPER_BOUND / 30.0
GLL_POINTS = [
    -1.0,
    -0.8717401485096066,
    -0.5917001814331423,
    -0.2092992179024789,
    0.2092992179024789,
    0.5917001814331423,
    0.8717401485096066,
    1.0,
]
F32 = jnp.float32
BF16 = jnp.bfloat16


def legendre_seven(points):
    before = points * 0.0 + 1.0
    current = points
    for order in range(1, 7):
        following = ((2.0 * order + 1.0) * points * current - order * before) / (order + 1.0)
        before = current
        current = following
    return current


def gll_tables():
    gll_nodes = np.array(GLL_POINTS)
    values = legendre_seven(gll_nodes)
    weights = 2.0 / (56.0 * values * values)
    deriv_mat = np.zeros((8, 8))
    for row_idx in range(8):
        for col_idx in range(8):
            if row_idx != col_idx:
                deriv_mat[row_idx, col_idx] = values[row_idx] / (
                    values[col_idx] * (gll_nodes[row_idx] - gll_nodes[col_idx])
                )
    deriv_mat[0, 0] = -14.0
    deriv_mat[7, 7] = 14.0
    return (gll_nodes, weights, deriv_mat)


NODE_POS, WEIGHTS, DERIV = gll_tables()
STIFF = DERIV.T @ (WEIGHTS[:, None] * DERIV)
STIFF_DIAG = np.diag(STIFF)


def split_pair(table):
    high = table.astype(np.float32).astype(jnp.bfloat16)
    low = (table - high.astype(np.float64)).astype(np.float32).astype(jnp.bfloat16)
    return high, low


def lane_weights(matrix, lanes, summed):
    full = np.kron(np.eye(lanes // NODES), matrix.T)
    if summed:
        shared = np.eye(lanes)
        for last in range(NODES - 1, lanes - 1, NODES):
            shared[last, last + 1] = shared[last + 1, last] = 1.0
        full = full @ shared
    high, low = split_pair(full)
    zero = np.zeros_like(np.asarray(low))
    return np.concatenate(
        [np.concatenate([high, low], 1), np.concatenate([high, zero], 1)], 0
    ).astype(jnp.bfloat16)


F_FACE = (DEPTH - 1) * NODES
F_META = F_FACE + 1
F_COUNT = F_FACE + 2
ROUTES = ((1, 0), (1, 1), (2, 0), (2, 1))
T_KY, T_DY = 0, 8
T_WJ, T_QJ, T_WK, T_QK, T_Z7, T_Z0, T_Y7, T_Y0 = range(16, 24)
T_NODE = 24
T_INV = 31
T_WKS = 32
T_COUNT = 33
HALF = NODES // 2


def table_tiles(lanes):
    tiles = np.zeros((T_COUNT, NODES, lanes))
    for turn in range(NODES):
        outer, inner = turn % HALF, turn - turn % HALF
        for row in range(NODES):
            to, of = (row + outer) % NODES, (row - inner) % NODES
            tiles[T_KY + turn, row, :] = STIFF[to, of]
            tiles[T_DY + turn, row, :] = DERIV[to, of]
    reps = lanes // NODES
    tiles[T_WJ] = WEIGHTS[:, None]
    tiles[T_QJ] = STIFF_DIAG[:, None]
    tiles[T_WK] = np.tile(WEIGHTS, reps)[None, :]
    tiles[T_QK] = np.tile(STIFF_DIAG, reps)[None, :]
    place = np.arange(lanes)
    tiles[T_Z7] = ((place % NODES == NODES - 1) & (place < lanes - 1))[None, :]
    tiles[T_Z0] = ((place % NODES == 0) & (place > 0))[None, :]
    assembled = np.tile(WEIGHTS, reps)
    assembled[NODES - 1 : -1 : NODES] += WEIGHTS[0]
    assembled[NODES::NODES] += WEIGHTS[-1]
    tiles[T_WKS] = assembled[None, :]
    tiles[T_Y7, NODES - 1] = 1.0
    tiles[T_Y0, 0] = 1.0
    for row in range(NODES):
        others = [m for m in range(NODES) if m != row]
        scale = 1.0
        for slot, other in enumerate(others):
            tiles[T_NODE + slot, row, :] = NODE_POS[other]
            scale *= NODE_POS[row] - NODE_POS[other]
        tiles[T_INV, row, :] = 1.0 / scale
    return tiles.astype(np.float32)


def swapped_bit(slabs, cols, bit):
    return [
        (i * cols + j, (i ^ bit) * cols + (j ^ 1)) for i in range(slabs) for j in range(cols)
    ]


def neighbours(slabs, cols, distance, odd, swap=0):
    partner = {}
    for low in range(slabs - distance):
        if (low // distance) % 2 == odd:
            partner[low] = low + distance
            partner[low + distance] = low
    pairs = []
    for i in range(slabs):
        for j in range(cols):
            if i in partner:
                pairs.append((i * cols + j, partner[i] * cols + (j ^ swap)))
            else:
                pairs.append((i * cols + j, i * cols + (j ^ 1)))
    return pairs


def column_pairs(cols, bit):
    return [(j, j ^ bit) for j in range(cols)]


def side_pairs(cols, odd):
    pairs = []
    for low in range(cols - 1):
        if low % 2 == odd:
            pairs += [(low, low + 1), (low + 1, low)]
    return pairs


def parity(slot):
    return bin(slot).count("1") % 2


def route_partner(position, route):
    distance, odd = route
    upward = (position // distance) % 2 == odd
    return jnp.where(upward, position + distance, position - distance), upward


def route_block(position, route, reach):
    middle = (reach - 1) // 2
    upward = route_partner(position, route)[1]
    return jnp.where(upward, middle + route[0], middle - route[0])


def route_open(position, route, slabs):
    partner = route_partner(position, route)[0]
    return jnp.logical_and(partner >= 0, partner < slabs)


def split_value(value):
    high = value.astype(BF16)
    low = (value - high.astype(F32)).astype(BF16)
    return high, low


def pack_kernel(cols, elem_z, source, metric, elem, coord, vel, prop, counts, first, own, *rest):
    first[0:NODES] = source[...]
    first[NODES] = jnp.zeros(first.shape[1:], F32)
    first[NODES, 0:1, 0 : metric.shape[-1]] = metric[0]
    routed, state = rest[:-1], rest[-1]
    position = lax.axis_index("stream")
    column = lax.axis_index("cross")
    reach, _, capacity = elem.shape
    middle = (reach - 1) // 2
    slot = lax.broadcasted_iota(jnp.int32, (1, capacity), 1)
    for block in range(reach):
        base = ((position + (block - middle)) * cols + column) * elem_z
        live = slot < counts[0, 0, block]
        ids = jnp.where(live, elem[block] - base + 1, 0).astype(F32)
        for axis in range(3):
            state[block, 0, axis : axis + 1, :] = coord[3 * block + axis]
            state[block, 0, 3 + axis : 4 + axis, :] = vel[3 * block + axis]
        state[block, 0, 6:8, :] = prop[0, 0, block]
        state[block, 1] = jnp.broadcast_to(ids, (NODES, capacity))
    own[...] = state[middle]
    for route, out in zip(ROUTES, routed):
        out[...] = state[route_block(position, route, reach)]


def near_kernel(first, from_source, from_metric, out):
    out[0] = first[...]
    out[1, 0:NODES] = from_source[...]
    out[1, NODES] = jnp.zeros(out.shape[2:], F32)
    out[1, NODES, 0:1, 0 : from_metric.shape[-1]] = from_metric[0]


def far_kernel(gathered, *outs):
    position = lax.axis_index("stream")
    group_even = (position // DEPTH) % 2 == 0
    for odd, out in enumerate(outs):
        upward = group_even if odd == 0 else jnp.logical_not(group_even)
        for slot in range(1, DEPTH):
            for i in range(NODES):
                out[(slot - 1) * NODES + i] = gathered[slot, i]
        out[F_FACE] = gathered[0, jnp.where(upward, NODES - 1, 0)]
        out[F_META] = jnp.zeros(out.shape[1:], F32)
        for slot in range(DEPTH):
            out[F_META, slot : slot + 1, :] = gathered[slot, NODES, 0:1, :]


def z_assembled(block, tiles):
    lanes = block.shape[-1]
    axis = block.ndim - 1
    after = pltpu.roll(block, lanes - 1, axis)
    before = pltpu.roll(block, 1, axis)
    return block + tiles[T_Z7] * after + tiles[T_Z0] * before


def y_assembled(blocks, tiles):
    axis = blocks[0].ndim - 2
    out = []
    for j, block in enumerate(blocks):
        total = block
        if j + 1 < len(blocks):
            total = total + tiles[T_Y7] * pltpu.roll(blocks[j + 1], NODES - 1, axis)
        if j > 0:
            total = total + tiles[T_Y0] * pltpu.roll(blocks[j - 1], 1, axis)
        out.append(total)
    return out


def halves(planes):
    even = [planes[m] + planes[NODES - 1 - m] for m in range(HALF)]
    odd = [planes[m] - planes[NODES - 1 - m] for m in range(HALF)]
    return even, odd


def row_pair(even, odd, matrix, row, mirrored):
    sums = []
    for values, sign in ((even, 0.5), (odd, -0.5)):
        total = None
        for m in range(HALF):
            factor = 0.5 * matrix[row, m] + sign * matrix[row, NODES - 1 - m]
            term = values[m] * float(factor)
            total = term if total is None else total + term
        sums.append(total)
    first = sums[0] + sums[1]
    second = sums[0] - sums[1] if mirrored > 0 else sums[1] - sums[0]
    return first, second


def x_product(planes, matrix, mirrored):
    even, odd = halves(planes)
    pairs = [row_pair(even, odd, matrix, row, mirrored) for row in range(HALF)]
    return [pair[0] for pair in pairs] + [pair[1] for pair in reversed(pairs)]


def y_product(block, tiles, start):
    axis = block.ndim - 2
    far = pltpu.roll(block, HALF, axis)
    total = None
    for outer in range(HALF):
        part = block * tiles[start + outer] + far * tiles[start + HALF + outer]
        if outer > 0:
            part = pltpu.roll(part, outer, axis)
        total = part if total is None else total + part
    return total


def z_product(rows, weights):
    lanes = rows.shape[-1]
    high, low = split_value(rows)
    both = jnp.concatenate([high, low], axis=1)
    wide = jnp.dot(both, weights, preferred_element_type=F32)
    return wide[:, :lanes] + wide[:, lanes:]


def lagrange(row, tiles):
    capacity = row.shape[-1]
    coords = jnp.broadcast_to(row, (NODES, capacity))
    factor = tiles[T_INV]
    for slot in range(NODES - 1):
        factor = factor * (coords - tiles[T_NODE + slot])
    return factor


def basis_kernel(slabs, tiles, own, *rest):
    routed, (picks, cells, live) = rest[:4], rest[4:]
    position = lax.axis_index("stream")
    lanes, capacity = tiles.shape[-1], own.shape[-1]
    opened = [None] + [route_open(position, route, slabs) for route in ROUTES]
    for g, (group, there) in enumerate(zip((own,) + tuple(routed), opened)):
        ids = group[1]
        if there is not None:
            ids = jnp.where(there, ids, 0.0)
        live[g] = ids
        basis = [lagrange(group[0, axis : axis + 1, :], tiles) for axis in range(3)]
        pick = jnp.concatenate(
            [jnp.where(ids == float(e + 1), basis[2], 0.0) for e in range(lanes // NODES)], 0
        )
        place = slice(g * capacity, (g + 1) * capacity)
        picks[0:lanes, place], picks[lanes : 2 * lanes, place] = split_value(pick)
        for i in range(NODES):
            cells[g, i] = basis[1] * basis[0][i : i + 1, :]


def main_kernel(slabs, cols, *refs):
    tiles, stiff_w, deriv_w, spread_w = refs[0:4]
    pieces = refs[4 : 4 + 3 * cols]
    base_velocity, own = refs[4 + 3 * cols : 6 + 3 * cols]
    routed = refs[6 + 3 * cols : 10 + 3 * cols]
    picks, cells_ref, live = refs[10 + 3 * cols : 13 + 3 * cols]
    (pressure, momentum, face_even, acc_own, acc_e1, acc_o1, acc_e2, acc_o2,
     *face_odd, loads, scales, resid, update, inv, work, spans, layers) = refs[13 + 3 * cols :]
    lanes = tiles.shape[-1]
    position = lax.axis_index("stream")
    column = lax.axis_index("cross")
    middle = DEPTH - 1

    group_even = (position // DEPTH) % 2 == 0
    rank = position % DEPTH
    wjk = tiles[T_WJ] * tiles[T_WK]
    flat = (NODES, lanes)

    def present(offset):
        where = position + offset
        return jnp.where((where >= 0) & (where < slabs), 1.0, 0.0).astype(F32)

    factors = []
    for slot_c in range(cols):
        near, *fars = pieces[3 * slot_c : 3 * slot_c + 3]
        factors += [near[slot, NODES, 0:1, :] for slot in range(DEPTH)]
        factors += [jnp.zeros((NODES - DEPTH, lanes), F32)] + [far[F_META] for far in fars]
    high, low = split_value(jnp.concatenate(factors, 0))
    factors = jnp.dot(
        jnp.concatenate([high, low], 1), spread_w[...], preferred_element_type=F32
    )
    for slot_c in range(cols):
        near, *fars = pieces[3 * slot_c : 3 * slot_c + 3]
        for slot in range(DEPTH):
            col = column ^ (slot_c ^ parity(slot))
            at = (rank ^ slot) - rank + (2 * DEPTH - 1)
            for i in range(NODES):
                loads[at, col, i] = near[slot, i] * (wjk * float(WEIGHTS[i]))
            row = 3 * NODES * slot_c + slot
            scales[at, col] = jnp.broadcast_to(factors[row : row + 1], flat)
        for odd, far in enumerate(fars):
            upper = group_even if odd == 0 else jnp.logical_not(group_even)
            shift = jnp.where(upper, DEPTH, -DEPTH)
            inside = present(shift)
            for slot in range(DEPTH):
                col = column ^ (slot_c ^ parity(slot) ^ 1)
                at = (rank ^ slot) - rank + shift + (2 * DEPTH - 1)
                if slot > 0:
                    for i in range(NODES):
                        loads[at, col, i] = far[(slot - 1) * NODES + i] * (
                            wjk * (inside * float(WEIGHTS[i]))
                        )
                else:
                    layer = jnp.where(upper, 0, NODES - 1)
                    loads[at, col, layer] = far[F_FACE] * (wjk * (inside * float(WEIGHTS[0])))
                row = 3 * NODES * slot_c + NODES * (1 + odd) + slot
                scales[at, col] = jnp.broadcast_to(factors[row : row + 1] * inside, flat)
    wide_mid = 2 * DEPTH - 1

    columns = range(cols)
    for offset in range(-DEPTH, DEPTH + 1):
        at = wide_mid + offset
        mass = (MASS_SHIFT * present(offset)) * tiles[T_WKS]
        alphas = [z_assembled(scales[at, j] * tiles[T_WK], tiles) for j in columns]
        betas = [z_assembled(scales[at, j] * tiles[T_QK], tiles) + mass for j in columns]
        sigmas = y_assembled([tiles[T_WJ] * alphas[j] for j in columns], tiles)
        taus = y_assembled([tiles[T_WJ] * scales[at, j] for j in columns], tiles)
        rests = y_assembled(
            [tiles[T_QJ] * alphas[j] + tiles[T_WJ] * betas[j] for j in columns], tiles
        )
        masses = y_assembled([tiles[T_WJ] * mass] * cols, tiles)
        for j in columns:
            for index, value in enumerate((alphas[j], sigmas[j], taus[j], rests[j], masses[j])):
                spans[index, DEPTH + offset, j] = value
        if abs(offset) < DEPTH:
            sides = [loads[at, j] for j in columns]
            sides = y_assembled([z_assembled(side, tiles) for side in sides], tiles)
            for j in columns:
                work[DEPTH + offset, j] = sides[j]
        else:
            layer = NODES - 1 if offset < 0 else 0
            sides = [loads[at, j, layer] for j in columns]
            sides = y_assembled([z_assembled(side, tiles) for side in sides], tiles)
            for j in columns:
                work[DEPTH + offset, j, layer] = sides[j]

    center = (UPPER_BOUND + LOWER_BOUND) / 2.0
    half_width = (UPPER_BOUND - LOWER_BOUND) / 2.0
    ratio_bound = center / half_width
    cheb_rho = 1.0 / ratio_bound
    ends = {0: -1, NODES - 1: 1}

    def joined(index, offset, j, i):
        tile = spans[index, DEPTH + offset, j]
        if i in ends:
            tile = tile + spans[index, DEPTH + offset + ends[i], j]
        return tile

    for offset in range(-middle, middle + 1):
        at = middle + offset
        gap = 1.0 - present(offset)
        for j in columns:
            for i in range(NODES):
                side = work[DEPTH + offset, j, i]
                if i in ends:
                    side = side + work[DEPTH + offset + ends[i], j, NODES - 1 - i]
                diag = joined(1, offset, j, i) * float(STIFF_DIAG[i]) + (
                    joined(3, offset, j, i) * float(WEIGHTS[i]) + gap
                )
                inverse = 1.0 / diag
                inv[at, j, i] = inverse
                resid[at, j, i] = side
                update[at, j, i] = side * inverse * (1.0 / center)

    iterate = update[middle, column]
    for sweep in range(SWEEPS):
        reach = SWEEPS - 1 - sweep
        rho_next = 1.0 / (2.0 * ratio_bound - cheb_rho)
        for offset in range(-reach - 1, reach + 2):
            for j in columns:
                sigma = spans[1, DEPTH + offset, j]
                planes = [sigma * update[middle + offset, j, i] for i in range(NODES)]
                first, last = row_pair(*halves(planes), STIFF, 0, 1)
                layers[DEPTH + offset, j, 0] = first
                layers[DEPTH + offset, j, 1] = last
        for offset in range(-reach, reach + 1):
            at = middle + offset
            weighted = [[update[at, j, i] * float(WEIGHTS[i]) for i in range(NODES)] for j in columns]
            rows = [
                joined(2, offset, j, i) * weighted[j][i] for j in columns for i in range(NODES)
            ]
            from_z = z_product(jnp.concatenate(rows, 0), stiff_w[...])
            from_y = y_assembled(
                [
                    y_product(
                        jnp.stack([joined(0, offset, j, i) * weighted[j][i] for i in range(NODES)], 0),
                        tiles,
                        T_KY,
                    )
                    for j in columns
                ],
                tiles,
            )
            for j in columns:
                sigma = spans[1, DEPTH + offset, j]
                planes = [sigma * update[at, j, i] for i in range(NODES)]
                even, odd = halves(planes)
                from_x = [None] * NODES
                from_x[0] = layers[DEPTH + offset, j, 0] + layers[DEPTH + offset - 1, j, 1]
                from_x[-1] = layers[DEPTH + offset, j, 1] + layers[DEPTH + offset + 1, j, 0]
                for row in range(1, HALF):
                    from_x[row], from_x[NODES - 1 - row] = row_pair(even, odd, STIFF, row, 1)
                for i in range(NODES):
                    row = (j * NODES + i) * NODES
                    total = from_x[i] + from_y[j][i] + from_z[row : row + NODES]
                    total = total + joined(4, offset, j, i) * weighted[j][i]
                    left = resid[at, j, i] - total
                    resid[at, j, i] = left
                    update[at, j, i] = (rho_next * cheb_rho) * update[at, j, i] + (
                        2.0 * rho_next / half_width
                    ) * (inv[at, j, i] * left)
        cheb_rho = rho_next
        iterate = iterate + update[middle, column]
    pressure[...] = iterate

    scale = scales[wide_mid, column]
    planes = [iterate[i] for i in range(NODES)]
    grad_x = x_product(planes, DERIV, -1)
    grad_z = z_product(iterate.reshape(NODES * NODES, lanes), deriv_w[...]).reshape(NODES, NODES, lanes)
    velocity = []
    for i in range(NODES):
        velocity.append(base_velocity[0, i] - scale * grad_x[i])
    for i in range(NODES):
        velocity.append(base_velocity[1, i] - scale * y_product(planes[i], tiles, T_DY))
    for i in range(NODES):
        velocity.append(base_velocity[2, i] - scale * grad_z[i])
    velocity = jnp.concatenate(velocity, 0)

    count = 3 * NODES * NODES
    high, low = split_value(velocity)
    partial = jnp.dot(
        jnp.concatenate(
            [jnp.concatenate([high, high], 1), jnp.concatenate([low, low], 1)], 0
        ),
        picks[...],
        preferred_element_type=F32,
    )
    partial = partial[:count] + partial[count:]
    capacity = own.shape[-1]
    spread = []
    for g, group in enumerate((own,) + tuple(routed)):
        group, ids = group.at[0], live.at[g]
        cells = [cells_ref[g, i] for i in range(NODES)]
        accel_rows, parts = [], []
        for comp in range(3):
            total = None
            for i in range(NODES):
                row = (comp * NODES + i) * NODES
                term = partial[row : row + NODES, g * capacity : (g + 1) * capacity] * cells[i]
                total = term if total is None else total + term
            fluid = jnp.sum(total, axis=0, keepdims=True)
            accel = jnp.where(ids[0:1, :] > 0.5, group[6:7, :] * (fluid - group[3 + comp : 4 + comp, :]), 0.0)
            accel_rows.append(accel)
            force = -group[7:8, :] * accel
            parts += [cells[i] * force for i in range(NODES)]
        accel_rows.append(jnp.zeros((NODES - 3, capacity), F32))
        (acc_own, acc_e1, acc_o1, acc_e2, acc_o2)[g][...] = jnp.concatenate(accel_rows, 0)
        spread.append(jnp.concatenate(parts, 0))
    spread = jnp.concatenate(spread, 1)
    added = lax.dot_general(
        jnp.concatenate(split_value(spread), 0),
        picks[...],
        (((1,), (1,)), ((), ())),
        preferred_element_type=F32,
    )
    added = added[:count] + added[count:]
    added = added[:, :lanes] + added[:, lanes:]
    added = z_assembled(added.reshape(3, NODES, NODES, lanes), tiles)
    momentum[...] = added
    low_row = added[:, :, 0, :]
    high_row = added[:, :, NODES - 1, :]
    even = column % 2 == 0
    face_even[...] = jnp.where(even, high_row, low_row)
    if face_odd:
        face_odd[0][...] = jnp.where(even, low_row, high_row)


def middle_kernel(momentum, face_even, face_odd, acc_e1, acc_o1, out, send_e1, send_o1):
    position = lax.axis_index("stream")
    column = lax.axis_index("cross")
    even = column % 2 == 0
    high = jnp.where(even, face_even[...], face_odd[...])
    low = jnp.where(even, face_odd[...], face_even[...])
    out[...] = momentum[...]
    out[:, :, 0, :] = momentum[:, :, 0, :] + low
    out[:, :, NODES - 1, :] = momentum[:, :, NODES - 1, :] + high
    lower = position % 2 == 0
    top = jnp.where(lower, NODES - 1, 0)
    bottom = NODES - 1 - top
    for comp in range(3):
        send_e1[comp] = out[comp, top]
        send_o1[comp] = out[comp, bottom]
    send_e1[3] = acc_e1[...]
    send_o1[3] = acc_o1[...]


def bundle_kernel(momentum, face_even, acc_e1, acc_o1, acc_o2, out):
    side = jnp.where(lax.axis_index("stream") % 2 == 0, NODES - 1, 0)
    for comp in range(3):
        out[comp] = face_even[comp]
        out[3 + comp] = momentum[comp, side]
        out[6 + comp] = momentum[comp, NODES - 1 - side]
    out[9] = acc_e1[...]
    out[10] = acc_o1[...]
    out[11] = acc_o2[...]


def exchange_kernel(momentum, got, out, send_e1, send_o1, send_o2):
    even = lax.axis_index("cross") % 2 == 0
    side = jnp.where(lax.axis_index("stream") % 2 == 0, NODES - 1, 0)
    layer = got[0:3]
    out[...] = momentum[...]
    out[:, :, 0, :] = momentum[:, :, 0, :] + jnp.where(even, 0.0, layer)
    out[:, :, NODES - 1, :] = momentum[:, :, NODES - 1, :] + jnp.where(even, layer, 0.0)
    here = jnp.where(even, NODES - 1, 0)
    there = pl.ds(NODES - 1 - here, 1)
    for comp in range(3):
        for send, start, at in ((send_e1, 3, side), (send_o1, 6, NODES - 1 - side)):
            send[comp] = got[start + comp]
            edge = momentum[comp, at, pl.ds(here, 1), :]
            send[comp, there, :] = got[start + comp, there, :] + edge
    send_e1[3] = got[9]
    send_o1[3] = got[10]
    send_o2[...] = got[11]


def last_kernel(
    slabs, reach, iterate, momentum, got_e1, got_o1, acc_own, got_e2, got_o2, pressure, out, accel
):
    pressure[...] = iterate[...]
    position = lax.axis_index("stream")
    lower = position % 2 == 0
    top = jnp.where(lower, NODES - 1, 0)
    bottom = NODES - 1 - top
    out[...] = momentum[...]
    opened = [route_open(position, route, slabs) for route in ROUTES]
    for comp in range(3):
        out[comp, top] = momentum[comp, top] + jnp.where(opened[0], got_e1[comp], 0.0)
        out[comp, bottom] = momentum[comp, bottom] + jnp.where(opened[1], got_o1[comp], 0.0)
    for axis in range(3):
        accel[3 * ((reach - 1) // 2) + axis] = acc_own[axis : axis + 1]
    arrived = (got_e1[3], got_o1[3], got_e2[...], got_o2[...])
    for route, value, there in zip(ROUTES, arrived, opened):
        block = route_block(position, route, reach)
        for axis in range(3):
            accel[3 * block + axis] = jnp.where(there, value[axis : axis + 1], 0.0)


def f32(*shape):
    return jax.ShapeDtypeStruct(shape, F32)


def near(*shape):
    return pltpu.VMEM(shape, F32)


def held(value):
    return pltpu.with_memory_space_constraint(value, pltpu.VMEM)


def step(
    source, metric, base_velocity, drop_elem, drop_coord, drop_vel, drop_prop, drop_counts
):
    slabs = lax.axis_size("stream")
    cols = lax.axis_size("cross")
    lanes = source.shape[-1]
    reach, capacity = drop_elem.shape[2:]
    elem_z = metric.shape[-1]
    vmem = pl.BlockSpec(memory_space=pltpu.VMEM)
    smem = pl.BlockSpec(memory_space=pltpu.SMEM)
    tiles = jnp.asarray(table_tiles(lanes))
    stiff_w = jnp.asarray(lane_weights(STIFF, lanes, True))
    deriv_w = jnp.asarray(lane_weights(DERIV, lanes, False))
    to_lanes = np.zeros((lanes, lanes))
    to_lanes[:elem_z] = np.kron(np.eye(elem_z), np.ones((1, NODES)))
    spread_w = jnp.asarray(np.concatenate([to_lanes, to_lanes], 0), BF16)

    first, own, *routed = pl.pallas_call(
        lambda *refs: pack_kernel(cols, elem_z, *refs),
        out_shape=[near(NODES + 1, NODES, lanes)] + [near(2, NODES, capacity)] * 5,
        in_specs=[vmem] * 6 + [smem],
        out_specs=[vmem] * 6,
        scratch_shapes=[pltpu.VMEM((reach, 2, NODES, capacity), F32)],
        name="pack",
    )(
        source,
        metric,
        drop_elem.reshape(reach, 1, capacity),
        drop_coord.reshape(3 * reach, 1, capacity),
        drop_vel.reshape(3 * reach, 1, capacity),
        drop_prop,
        drop_counts,
    )
    whole = ("stream", "cross")

    routed = [
        lax.ppermute(value, whole, neighbours(slabs, cols, *route))
        for value, route in zip(routed, ROUTES)
    ]
    from_source = lax.ppermute(source, whole, swapped_bit(slabs, cols, 1))
    from_metric = lax.ppermute(metric, whole, swapped_bit(slabs, cols, 1))
    gathered = pl.pallas_call(
        near_kernel,
        out_shape=near(2, NODES + 1, NODES, lanes),
        in_specs=[vmem] * 3,
        out_specs=vmem,
        name="near_pair",
    )(held(first), held(from_source), held(from_metric))
    gathered = jnp.concatenate(
        [gathered, lax.ppermute(gathered, whole, swapped_bit(slabs, cols, 2))], 0
    )
    to_far = pl.pallas_call(
        far_kernel,
        out_shape=[near(F_COUNT, NODES, lanes)] * 2,
        in_specs=[vmem],
        out_specs=[vmem] * 2,
        name="far_records",
    )(held(gathered))
    pieces = [gathered] + [
        lax.ppermute(value, whole, neighbours(slabs, cols, DEPTH, odd, 1))
        for odd, value in enumerate(to_far)
    ]
    columns = [pieces]
    bit = 1
    while bit < cols:
        columns = columns + [
            [lax.ppermute(piece, "cross", column_pairs(cols, bit)) for piece in group]
            for group in columns
        ]
        bit *= 2
    flat = [piece for group in columns for piece in group]

    span = 2 * DEPTH - 1
    field = (cols, NODES, NODES, lanes)
    scratch_bytes = 4 * (9 * DEPTH + 1 + 5 * span) * int(np.prod(field))
    slots = 5 * capacity
    bases = pl.pallas_call(
        lambda *refs: basis_kernel(slabs, *refs),
        out_shape=[pltpu.VMEM((2 * lanes, slots), BF16)]
        + [near(5, NODES, NODES, capacity), near(5, NODES, capacity)],
        in_specs=[vmem] * 6,
        out_specs=[vmem] * 3,
        name="bases",
    )(held(tiles), held(own), *[held(value) for value in routed])
    pressure, momentum, face_even, *accels = pl.pallas_call(
        lambda *refs: main_kernel(slabs, cols, *refs),
        out_shape=[near(NODES, NODES, lanes), near(3, NODES, NODES, lanes)]
        + [near(3, NODES, lanes)]
        + [near(NODES, capacity)] * 5
        + [near(3, NODES, lanes)] * (cols > 2),
        in_specs=[vmem] * (13 + 3 * cols),
        out_specs=[vmem] * (8 + (cols > 2)),
        scratch_shapes=[
            pltpu.VMEM((4 * DEPTH - 1,) + field, F32),
            pltpu.VMEM((4 * DEPTH - 1, cols, NODES, lanes), F32),
            pltpu.VMEM((span,) + field, F32),
            pltpu.VMEM((span,) + field, F32),
            pltpu.VMEM((span,) + field, F32),
            pltpu.VMEM((span + 2,) + field, F32),
            pltpu.VMEM((5, span + 2, cols, NODES, lanes), F32),
            pltpu.VMEM((span + 2, cols, 2, NODES, lanes), F32),
        ],
        compiler_params=pltpu.CompilerParams(vmem_limit_bytes=2 * scratch_bytes + 2**23),
        name="sweeps_and_droplets",
    )(
        tiles,
        stiff_w,
        deriv_w,
        spread_w,
        *[held(piece) for piece in flat],
        base_velocity,
        held(own),
        *[held(value) for value in (*routed, *bases)],
    )
    acc_own, acc_e1, acc_o1, acc_e2, acc_o2, *face_odd = accels

    def returned(value, index, swap):
        pairs = neighbours(slabs, cols, *ROUTES[index], swap)
        return lax.ppermute(value, whole, pairs)

    got_e2 = returned(acc_e2, 2, 0)
    if cols == 2:
        swap = 1
        bundle = pl.pallas_call(
            bundle_kernel,
            out_shape=near(12, NODES, lanes),
            in_specs=[vmem] * 5,
            out_specs=vmem,
            name="bundle",
        )(*[held(value) for value in (momentum, face_even, acc_e1, acc_o1, acc_o2)])
        bundle = lax.ppermute(bundle, "cross", side_pairs(cols, 0))
        momentum, send_e1, send_o1, send_o2 = pl.pallas_call(
            exchange_kernel,
            out_shape=[near(3, NODES, NODES, lanes)]
            + [near(4, NODES, lanes)] * 2
            + [near(NODES, capacity)],
            in_specs=[vmem] * 2,
            out_specs=[vmem] * 4,
            name="cross_faces",
        )(held(momentum), held(bundle))
    else:
        swap = 0
        face_even = lax.ppermute(face_even, "cross", side_pairs(cols, 0))
        face_odd = lax.ppermute(face_odd[0], "cross", side_pairs(cols, 1))
        momentum, send_e1, send_o1 = pl.pallas_call(
            middle_kernel,
            out_shape=[near(3, NODES, NODES, lanes)] + [near(4, NODES, lanes)] * 2,
            in_specs=[vmem] * 5,
            out_specs=[vmem] * 3,
            name="cross_faces",
        )(*[held(value) for value in (momentum, face_even, face_odd, acc_e1, acc_o1)])
        send_o2 = acc_o2
    got_o2 = returned(send_o2, 3, swap)
    got_e1 = returned(send_e1, 0, swap)
    got_o1 = returned(send_o1, 1, swap)
    pressure, momentum, accel = pl.pallas_call(
        lambda *refs: last_kernel(slabs, reach, *refs),
        out_shape=[f32(NODES, NODES, lanes), f32(3, NODES, NODES, lanes), f32(3 * reach, 1, capacity)],
        in_specs=[vmem] * 7,
        out_specs=[vmem] * 3,
        name="stream_faces",
    )(*[held(value) for value in (pressure, momentum, got_e1, got_o1, acc_own, got_e2, got_o2)])
    return (pressure, momentum, accel.reshape(1, 1, reach, 3, capacity))


def solution(mesh):
    in_specs = (
        P("stream", "cross", None),
        P("stream", "cross", None),
        P(None, "stream", "cross", None),
        P("stream", "cross", None, None),
        P("stream", "cross", None, None, None),
        P("stream", "cross", None, None, None),
        P("stream", "cross", None, None, None),
        P("stream", "cross", None),
    )
    out_specs = (
        P("stream", "cross", None),
        P(None, "stream", "cross", None),
        P("stream", "cross", None, None, None),
    )
    return jax.shard_map(step, mesh=mesh, in_specs=in_specs, out_specs=out_specs, check_vma=False)
```

```python
import jax
import jax.numpy as jnp
import numpy as np
from jax import lax
from jax.experimental import pallas as pl
from jax.experimental.pallas import tpu as pltpu
from jax.sharding import PartitionSpec as P


SWEEPS = 3
DEPTH = SWEEPS + 1
NODES = 8
MASS_SHIFT = 1.0
UPPER_BOUND = 2.5
LOWER_BOUND = UPPER_BOUND / 30.0
GLL_POINTS = [
    -1.0,
    -0.8717401485096066,
    -0.5917001814331423,
    -0.2092992179024789,
    0.2092992179024789,
    0.5917001814331423,
    0.8717401485096066,
    1.0,
]
F32 = jnp.float32
BF16 = jnp.bfloat16


def legendre_seven(points):
    before = points * 0.0 + 1.0
    current = points
    for order in range(1, 7):
        following = ((2.0 * order + 1.0) * points * current - order * before) / (order + 1.0)
        before = current
        current = following
    return current


def gll_tables():
    gll_nodes = np.array(GLL_POINTS)
    values = legendre_seven(gll_nodes)
    weights = 2.0 / (56.0 * values * values)
    deriv_mat = np.zeros((8, 8))
    for row_idx in range(8):
        for col_idx in range(8):
            if row_idx != col_idx:
                deriv_mat[row_idx, col_idx] = values[row_idx] / (
                    values[col_idx] * (gll_nodes[row_idx] - gll_nodes[col_idx])
                )
    deriv_mat[0, 0] = -14.0
    deriv_mat[7, 7] = 14.0
    return (gll_nodes, weights, deriv_mat)


NODE_POS, WEIGHTS, DERIV = gll_tables()
STIFF = DERIV.T @ (WEIGHTS[:, None] * DERIV)
STIFF_DIAG = np.diag(STIFF)


def split_pair(table):
    high = table.astype(np.float32).astype(jnp.bfloat16)
    low = (table - high.astype(np.float64)).astype(np.float32).astype(jnp.bfloat16)
    return high, low


def lane_weights(matrix, lanes, summed):
    full = np.kron(np.eye(lanes // NODES), matrix.T)
    if summed:
        shared = np.eye(lanes)
        for last in range(NODES - 1, lanes - 1, NODES):
            shared[last, last + 1] = shared[last + 1, last] = 1.0
        full = full @ shared
    high, low = split_pair(full)
    zero = np.zeros_like(np.asarray(low))
    return np.concatenate(
        [np.concatenate([high, low], 1), np.concatenate([high, zero], 1)], 0
    ).astype(jnp.bfloat16)


F_FACE = (DEPTH - 1) * NODES
F_META = F_FACE + 1
F_COUNT = F_FACE + 2
ROUTES = ((1, 0), (1, 1), (2, 0), (2, 1))
T_KY, T_DY = 0, 8
T_WJ, T_QJ, T_WK, T_QK, T_Z7, T_Z0, T_Y7, T_Y0 = range(16, 24)
T_NODE = 24
T_INV = 31
T_WKS = 32
T_COUNT = 33
HALF = NODES // 2


def table_tiles(lanes):
    tiles = np.zeros((T_COUNT, NODES, lanes))
    for turn in range(NODES):
        outer, inner = turn % HALF, turn - turn % HALF
        for row in range(NODES):
            to, of = (row + outer) % NODES, (row - inner) % NODES
            tiles[T_KY + turn, row, :] = STIFF[to, of]
            tiles[T_DY + turn, row, :] = DERIV[to, of]
    reps = lanes // NODES
    tiles[T_WJ] = WEIGHTS[:, None]
    tiles[T_QJ] = STIFF_DIAG[:, None]
    tiles[T_WK] = np.tile(WEIGHTS, reps)[None, :]
    tiles[T_QK] = np.tile(STIFF_DIAG, reps)[None, :]
    place = np.arange(lanes)
    tiles[T_Z7] = ((place % NODES == NODES - 1) & (place < lanes - 1))[None, :]
    tiles[T_Z0] = ((place % NODES == 0) & (place > 0))[None, :]
    assembled = np.tile(WEIGHTS, reps)
    assembled[NODES - 1 : -1 : NODES] += WEIGHTS[0]
    assembled[NODES::NODES] += WEIGHTS[-1]
    tiles[T_WKS] = assembled[None, :]
    tiles[T_Y7, NODES - 1] = 1.0
    tiles[T_Y0, 0] = 1.0
    for row in range(NODES):
        others = [m for m in range(NODES) if m != row]
        scale = 1.0
        for slot, other in enumerate(others):
            tiles[T_NODE + slot, row, :] = NODE_POS[other]
            scale *= NODE_POS[row] - NODE_POS[other]
        tiles[T_INV, row, :] = 1.0 / scale
    return tiles.astype(np.float32)


def swapped_bit(slabs, cols, bit):
    return [
        (i * cols + j, (i ^ bit) * cols + (j ^ 1)) for i in range(slabs) for j in range(cols)
    ]


def neighbours(slabs, cols, distance, odd, swap=0):
    partner = {}
    for low in range(slabs - distance):
        if (low // distance) % 2 == odd:
            partner[low] = low + distance
            partner[low + distance] = low
    pairs = []
    for i in range(slabs):
        for j in range(cols):
            if i in partner:
                pairs.append((i * cols + j, partner[i] * cols + (j ^ swap)))
            else:
                pairs.append((i * cols + j, i * cols + (j ^ 1)))
    return pairs


def column_pairs(cols, bit):
    return [(j, j ^ bit) for j in range(cols)]


def side_pairs(cols, odd):
    pairs = []
    for low in range(cols - 1):
        if low % 2 == odd:
            pairs += [(low, low + 1), (low + 1, low)]
    return pairs


def parity(slot):
    return bin(slot).count("1") % 2


def route_partner(position, route):
    distance, odd = route
    upward = (position // distance) % 2 == odd
    return jnp.where(upward, position + distance, position - distance), upward


def route_block(position, route, reach):
    middle = (reach - 1) // 2
    upward = route_partner(position, route)[1]
    return jnp.where(upward, middle + route[0], middle - route[0])


def route_open(position, route, slabs):
    partner = route_partner(position, route)[0]
    return jnp.logical_and(partner >= 0, partner < slabs)


def split_value(value):
    high = value.astype(BF16)
    low = (value - high.astype(F32)).astype(BF16)
    return high, low


def pack_kernel(cols, elem_z, source, metric, elem, coord, vel, prop, counts, first, own, *rest):
    first[0:NODES] = source[...]
    first[NODES] = jnp.zeros(first.shape[1:], F32)
    first[NODES, 0:1, 0 : metric.shape[-1]] = metric[0]
    routed, state = rest[:-1], rest[-1]
    position = lax.axis_index("stream")
    column = lax.axis_index("cross")
    reach, _, capacity = elem.shape
    middle = (reach - 1) // 2
    slot = lax.broadcasted_iota(jnp.int32, (1, capacity), 1)
    for block in range(reach):
        base = ((position + (block - middle)) * cols + column) * elem_z
        live = slot < counts[0, 0, block]
        ids = jnp.where(live, elem[block] - base + 1, 0).astype(F32)
        for axis in range(3):
            state[block, 0, axis : axis + 1, :] = coord[3 * block + axis]
            state[block, 0, 3 + axis : 4 + axis, :] = vel[3 * block + axis]
        state[block, 0, 6:8, :] = prop[0, 0, block]
        state[block, 1] = jnp.broadcast_to(ids, (NODES, capacity))
    own[...] = state[middle]
    for route, out in zip(ROUTES, routed):
        out[...] = state[route_block(position, route, reach)]


def near_kernel(first, from_source, from_metric, out):
    out[0] = first[...]
    out[1, 0:NODES] = from_source[...]
    out[1, NODES] = jnp.zeros(out.shape[2:], F32)
    out[1, NODES, 0:1, 0 : from_metric.shape[-1]] = from_metric[0]


def far_kernel(gathered, *outs):
    position = lax.axis_index("stream")
    group_even = (position // DEPTH) % 2 == 0
    for odd, out in enumerate(outs):
        upward = group_even if odd == 0 else jnp.logical_not(group_even)
        for slot in range(1, DEPTH):
            for i in range(NODES):
                out[(slot - 1) * NODES + i] = gathered[slot, i]
        out[F_FACE] = gathered[0, jnp.where(upward, NODES - 1, 0)]
        out[F_META] = jnp.zeros(out.shape[1:], F32)
        for slot in range(DEPTH):
            out[F_META, slot : slot + 1, :] = gathered[slot, NODES, 0:1, :]


def z_assembled(block, tiles):
    lanes = block.shape[-1]
    axis = block.ndim - 1
    after = pltpu.roll(block, lanes - 1, axis)
    before = pltpu.roll(block, 1, axis)
    return block + tiles[T_Z7] * after + tiles[T_Z0] * before


def y_assembled(blocks, tiles):
    axis = blocks[0].ndim - 2
    out = []
    for j, block in enumerate(blocks):
        total = block
        if j + 1 < len(blocks):
            total = total + tiles[T_Y7] * pltpu.roll(blocks[j + 1], NODES - 1, axis)
        if j > 0:
            total = total + tiles[T_Y0] * pltpu.roll(blocks[j - 1], 1, axis)
        out.append(total)
    return out


def halves(planes):
    even = [planes[m] + planes[NODES - 1 - m] for m in range(HALF)]
    odd = [planes[m] - planes[NODES - 1 - m] for m in range(HALF)]
    return even, odd


def row_pair(even, odd, matrix, row, mirrored):
    sums = []
    for values, sign in ((even, 0.5), (odd, -0.5)):
        total = None
        for m in range(HALF):
            factor = 0.5 * matrix[row, m] + sign * matrix[row, NODES - 1 - m]
            term = values[m] * float(factor)
            total = term if total is None else total + term
        sums.append(total)
    first = sums[0] + sums[1]
    second = sums[0] - sums[1] if mirrored > 0 else sums[1] - sums[0]
    return first, second


def x_product(planes, matrix, mirrored):
    even, odd = halves(planes)
    pairs = [row_pair(even, odd, matrix, row, mirrored) for row in range(HALF)]
    return [pair[0] for pair in pairs] + [pair[1] for pair in reversed(pairs)]


def y_product(block, tiles, start):
    axis = block.ndim - 2
    far = pltpu.roll(block, HALF, axis)
    total = None
    for outer in range(HALF):
        part = block * tiles[start + outer] + far * tiles[start + HALF + outer]
        if outer > 0:
            part = pltpu.roll(part, outer, axis)
        total = part if total is None else total + part
    return total


def z_product(rows, weights):
    lanes = rows.shape[-1]
    high, low = split_value(rows)
    both = jnp.concatenate([high, low], axis=1)
    wide = jnp.dot(both, weights, preferred_element_type=F32)
    return wide[:, :lanes] + wide[:, lanes:]


def lagrange(row, tiles):
    capacity = row.shape[-1]
    coords = jnp.broadcast_to(row, (NODES, capacity))
    factor = tiles[T_INV]
    for slot in range(NODES - 1):
        factor = factor * (coords - tiles[T_NODE + slot])
    return factor


def basis_kernel(slabs, tiles, own, *rest):
    routed, (picks, cells, live) = rest[:4], rest[4:]
    position = lax.axis_index("stream")
    lanes, capacity = tiles.shape[-1], own.shape[-1]
    opened = [None] + [route_open(position, route, slabs) for route in ROUTES]
    for g, (group, there) in enumerate(zip((own,) + tuple(routed), opened)):
        ids = group[1]
        if there is not None:
            ids = jnp.where(there, ids, 0.0)
        live[g] = ids
        basis = [lagrange(group[0, axis : axis + 1, :], tiles) for axis in range(3)]
        pick = jnp.concatenate(
            [jnp.where(ids == float(e + 1), basis[2], 0.0) for e in range(lanes // NODES)], 0
        )
        place = slice(g * capacity, (g + 1) * capacity)
        picks[0:lanes, place], picks[lanes : 2 * lanes, place] = split_value(pick)
        for i in range(NODES):
            cells[g, i] = basis[1] * basis[0][i : i + 1, :]


def main_kernel(slabs, cols, *refs):
    tiles, stiff_w, deriv_w, spread_w = refs[0:4]
    pieces = refs[4 : 4 + 3 * cols]
    base_velocity, own = refs[4 + 3 * cols : 6 + 3 * cols]
    routed = refs[6 + 3 * cols : 10 + 3 * cols]
    picks, cells_ref, live = refs[10 + 3 * cols : 13 + 3 * cols]
    (pressure, momentum, face_even, acc_own, acc_e1, acc_o1, acc_e2, acc_o2,
     *face_odd, loads, scales, resid, update, inv, work, spans, layers) = refs[13 + 3 * cols :]
    lanes = tiles.shape[-1]
    position = lax.axis_index("stream")
    column = lax.axis_index("cross")
    middle = DEPTH - 1

    group_even = (position // DEPTH) % 2 == 0
    rank = position % DEPTH
    wjk = tiles[T_WJ] * tiles[T_WK]
    flat = (NODES, lanes)

    def present(offset):
        where = position + offset
        return jnp.where((where >= 0) & (where < slabs), 1.0, 0.0).astype(F32)

    factors = []
    for slot_c in range(cols):
        near, *fars = pieces[3 * slot_c : 3 * slot_c + 3]
        factors += [near[slot, NODES, 0:1, :] for slot in range(DEPTH)]
        factors += [jnp.zeros((NODES - DEPTH, lanes), F32)] + [far[F_META] for far in fars]
    high, low = split_value(jnp.concatenate(factors, 0))
    factors = jnp.dot(
        jnp.concatenate([high, low], 1), spread_w[...], preferred_element_type=F32
    )
    for slot_c in range(cols):
        near, *fars = pieces[3 * slot_c : 3 * slot_c + 3]
        for slot in range(DEPTH):
            col = column ^ (slot_c ^ parity(slot))
            at = (rank ^ slot) - rank + (2 * DEPTH - 1)
            for i in range(NODES):
                loads[at, col, i] = near[slot, i] * (wjk * float(WEIGHTS[i]))
            row = 3 * NODES * slot_c + slot
            scales[at, col] = jnp.broadcast_to(factors[row : row + 1], flat)
        for odd, far in enumerate(fars):
            upper = group_even if odd == 0 else jnp.logical_not(group_even)
            shift = jnp.where(upper, DEPTH, -DEPTH)
            inside = present(shift)
            for slot in range(DEPTH):
                col = column ^ (slot_c ^ parity(slot) ^ 1)
                at = (rank ^ slot) - rank + shift + (2 * DEPTH - 1)
                if slot > 0:
                    for i in range(NODES):
                        loads[at, col, i] = far[(slot - 1) * NODES + i] * (
                            wjk * (inside * float(WEIGHTS[i]))
                        )
                else:
                    layer = jnp.where(upper, 0, NODES - 1)
                    loads[at, col, layer] = far[F_FACE] * (wjk * (inside * float(WEIGHTS[0])))
                row = 3 * NODES * slot_c + NODES * (1 + odd) + slot
                scales[at, col] = jnp.broadcast_to(factors[row : row + 1] * inside, flat)
    wide_mid = 2 * DEPTH - 1

    columns = range(cols)
    for offset in range(-DEPTH, DEPTH + 1):
        at = wide_mid + offset
        mass = (MASS_SHIFT * present(offset)) * tiles[T_WKS]
        alphas = [z_assembled(scales[at, j] * tiles[T_WK], tiles) for j in columns]
        betas = [z_assembled(scales[at, j] * tiles[T_QK], tiles) + mass for j in columns]
        sigmas = y_assembled([tiles[T_WJ] * alphas[j] for j in columns], tiles)
        taus = y_assembled([tiles[T_WJ] * scales[at, j] for j in columns], tiles)
        rests = y_assembled(
            [tiles[T_QJ] * alphas[j] + tiles[T_WJ] * betas[j] for j in columns], tiles
        )
        masses = y_assembled([tiles[T_WJ] * mass] * cols, tiles)
        for j in columns:
            for index, value in enumerate((alphas[j], sigmas[j], taus[j], rests[j], masses[j])):
                spans[index, DEPTH + offset, j] = value
        if abs(offset) < DEPTH:
            sides = [loads[at, j] for j in columns]
            sides = y_assembled([z_assembled(side, tiles) for side in sides], tiles)
            for j in columns:
                work[DEPTH + offset, j] = sides[j]
        else:
            layer = NODES - 1 if offset < 0 else 0
            sides = [loads[at, j, layer] for j in columns]
            sides = y_assembled([z_assembled(side, tiles) for side in sides], tiles)
            for j in columns:
                work[DEPTH + offset, j, layer] = sides[j]

    center = (UPPER_BOUND + LOWER_BOUND) / 2.0
    half_width = (UPPER_BOUND - LOWER_BOUND) / 2.0
    ratio_bound = center / half_width
    cheb_rho = 1.0 / ratio_bound
    ends = {0: -1, NODES - 1: 1}

    def joined(index, offset, j, i):
        tile = spans[index, DEPTH + offset, j]
        if i in ends:
            tile = tile + spans[index, DEPTH + offset + ends[i], j]
        return tile

    for offset in range(-middle, middle + 1):
        at = middle + offset
        gap = 1.0 - present(offset)
        for j in columns:
            for i in range(NODES):
                side = work[DEPTH + offset, j, i]
                if i in ends:
                    side = side + work[DEPTH + offset + ends[i], j, NODES - 1 - i]
                diag = joined(1, offset, j, i) * float(STIFF_DIAG[i]) + (
                    joined(3, offset, j, i) * float(WEIGHTS[i]) + gap
                )
                inverse = 1.0 / diag
                inv[at, j, i] = inverse
                resid[at, j, i] = side
                update[at, j, i] = side * inverse * (1.0 / center)

    iterate = update[middle, column]
    for sweep in range(SWEEPS):
        reach = SWEEPS - 1 - sweep
        alone = reach == 0 and cols == 2
        active = [column] if alone else list(columns)
        rho_next = 1.0 / (2.0 * ratio_bound - cheb_rho)
        for offset in range(-reach - 1, reach + 2):
            for j in active:
                sigma = spans[1, DEPTH + offset, j]
                planes = [sigma * update[middle + offset, j, i] for i in range(NODES)]
                first, last = row_pair(*halves(planes), STIFF, 0, 1)
                layers[DEPTH + offset, j, 0] = first
                layers[DEPTH + offset, j, 1] = last
        for offset in range(-reach, reach + 1):
            at = middle + offset
            seen = [column, column ^ 1] if alone else active
            weighted = [[update[at, j, i] * float(WEIGHTS[i]) for i in range(NODES)] for j in seen]
            rows = [
                joined(2, offset, j, i) * weighted[place][i]
                for place, j in enumerate(active)
                for i in range(NODES)
            ]
            from_z = z_product(jnp.concatenate(rows, 0), stiff_w[...])
            along_y = [
                y_product(
                    jnp.stack(
                        [joined(0, offset, j, i) * weighted[place][i] for i in range(NODES)], 0
                    ),
                    tiles,
                    T_KY,
                )
                for place, j in enumerate(seen)
            ]
            if alone:
                mine, other = along_y
                first = column == 0
                shared = jnp.where(
                    first, pltpu.roll(other, NODES - 1, 1), pltpu.roll(other, 1, 1)
                )
                from_y = [mine + jnp.where(first, tiles[T_Y7], tiles[T_Y0]) * shared]
            else:
                from_y = y_assembled(along_y, tiles)
            for place, j in enumerate(active):
                sigma = spans[1, DEPTH + offset, j]
                planes = [sigma * update[at, j, i] for i in range(NODES)]
                even, odd = halves(planes)
                from_x = [None] * NODES
                from_x[0] = layers[DEPTH + offset, j, 0] + layers[DEPTH + offset - 1, j, 1]
                from_x[-1] = layers[DEPTH + offset, j, 1] + layers[DEPTH + offset + 1, j, 0]
                for row in range(1, HALF):
                    from_x[row], from_x[NODES - 1 - row] = row_pair(even, odd, STIFF, row, 1)
                for i in range(NODES):
                    row = (place * NODES + i) * NODES
                    total = from_x[i] + from_y[place][i] + from_z[row : row + NODES]
                    total = total + joined(4, offset, j, i) * weighted[place][i]
                    left = resid[at, j, i] - total
                    resid[at, j, i] = left
                    update[at, j, i] = (rho_next * cheb_rho) * update[at, j, i] + (
                        2.0 * rho_next / half_width
                    ) * (inv[at, j, i] * left)
        cheb_rho = rho_next
        iterate = iterate + update[middle, column]
    pressure[...] = iterate

    scale = scales[wide_mid, column]
    planes = [iterate[i] for i in range(NODES)]
    grad_x = x_product(planes, DERIV, -1)
    grad_z = z_product(iterate.reshape(NODES * NODES, lanes), deriv_w[...]).reshape(NODES, NODES, lanes)
    velocity = []
    for i in range(NODES):
        velocity.append(base_velocity[0, i] - scale * grad_x[i])
    for i in range(NODES):
        velocity.append(base_velocity[1, i] - scale * y_product(planes[i], tiles, T_DY))
    for i in range(NODES):
        velocity.append(base_velocity[2, i] - scale * grad_z[i])
    velocity = jnp.concatenate(velocity, 0)

    count = 3 * NODES * NODES
    high, low = split_value(velocity)
    partial = jnp.dot(
        jnp.concatenate(
            [jnp.concatenate([high, high], 1), jnp.concatenate([low, low], 1)], 0
        ),
        picks[...],
        preferred_element_type=F32,
    )
    partial = partial[:count] + partial[count:]
    capacity = own.shape[-1]
    spread = []
    for g, group in enumerate((own,) + tuple(routed)):
        group, ids = group.at[0], live.at[g]
        cells = [cells_ref[g, i] for i in range(NODES)]
        accel_rows, parts = [], []
        for comp in range(3):
            total = None
            for i in range(NODES):
                row = (comp * NODES + i) * NODES
                term = partial[row : row + NODES, g * capacity : (g + 1) * capacity] * cells[i]
                total = term if total is None else total + term
            fluid = jnp.sum(total, axis=0, keepdims=True)
            accel = jnp.where(ids[0:1, :] > 0.5, group[6:7, :] * (fluid - group[3 + comp : 4 + comp, :]), 0.0)
            accel_rows.append(accel)
            force = -group[7:8, :] * accel
            parts += [cells[i] * force for i in range(NODES)]
        accel_rows.append(jnp.zeros((NODES - 3, capacity), F32))
        (acc_own, acc_e1, acc_o1, acc_e2, acc_o2)[g][...] = jnp.concatenate(accel_rows, 0)
        spread.append(jnp.concatenate(parts, 0))
    spread = jnp.concatenate(spread, 1)
    added = lax.dot_general(
        jnp.concatenate(split_value(spread), 0),
        picks[...],
        (((1,), (1,)), ((), ())),
        preferred_element_type=F32,
    )
    added = added[:count] + added[count:]
    added = added[:, :lanes] + added[:, lanes:]
    added = z_assembled(added.reshape(3, NODES, NODES, lanes), tiles)
    momentum[...] = added
    low_row = added[:, :, 0, :]
    high_row = added[:, :, NODES - 1, :]
    even = column % 2 == 0
    face_even[...] = jnp.where(even, high_row, low_row)
    if face_odd:
        face_odd[0][...] = jnp.where(even, low_row, high_row)


def middle_kernel(momentum, face_even, face_odd, acc_e1, acc_o1, out, send_e1, send_o1):
    position = lax.axis_index("stream")
    column = lax.axis_index("cross")
    even = column % 2 == 0
    high = jnp.where(even, face_even[...], face_odd[...])
    low = jnp.where(even, face_odd[...], face_even[...])
    out[...] = momentum[...]
    out[:, :, 0, :] = momentum[:, :, 0, :] + low
    out[:, :, NODES - 1, :] = momentum[:, :, NODES - 1, :] + high
    lower = position % 2 == 0
    top = jnp.where(lower, NODES - 1, 0)
    bottom = NODES - 1 - top
    for comp in range(3):
        send_e1[comp] = out[comp, top]
        send_o1[comp] = out[comp, bottom]
    send_e1[3] = acc_e1[...]
    send_o1[3] = acc_o1[...]


def bundle_kernel(momentum, face_even, acc_e1, acc_o1, acc_o2, out):
    side = jnp.where(lax.axis_index("stream") % 2 == 0, NODES - 1, 0)
    for comp in range(3):
        out[comp] = face_even[comp]
        out[3 + comp] = momentum[comp, side]
        out[6 + comp] = momentum[comp, NODES - 1 - side]
    out[9] = acc_e1[...]
    out[10] = acc_o1[...]
    out[11] = acc_o2[...]


def exchange_kernel(momentum, got, out, send_e1, send_o1, send_o2):
    even = lax.axis_index("cross") % 2 == 0
    side = jnp.where(lax.axis_index("stream") % 2 == 0, NODES - 1, 0)
    layer = got[0:3]
    out[...] = momentum[...]
    out[:, :, 0, :] = momentum[:, :, 0, :] + jnp.where(even, 0.0, layer)
    out[:, :, NODES - 1, :] = momentum[:, :, NODES - 1, :] + jnp.where(even, layer, 0.0)
    here = jnp.where(even, NODES - 1, 0)
    there = pl.ds(NODES - 1 - here, 1)
    for comp in range(3):
        for send, start, at in ((send_e1, 3, side), (send_o1, 6, NODES - 1 - side)):
            send[comp] = got[start + comp]
            edge = momentum[comp, at, pl.ds(here, 1), :]
            send[comp, there, :] = got[start + comp, there, :] + edge
    send_e1[3] = got[9]
    send_o1[3] = got[10]
    send_o2[...] = got[11]


def last_kernel(
    slabs, reach, iterate, momentum, got_e1, got_o1, acc_own, got_e2, got_o2, pressure, out, accel
):
    pressure[...] = iterate[...]
    position = lax.axis_index("stream")
    lower = position % 2 == 0
    top = jnp.where(lower, NODES - 1, 0)
    bottom = NODES - 1 - top
    out[...] = momentum[...]
    opened = [route_open(position, route, slabs) for route in ROUTES]
    for comp in range(3):
        out[comp, top] = momentum[comp, top] + jnp.where(opened[0], got_e1[comp], 0.0)
        out[comp, bottom] = momentum[comp, bottom] + jnp.where(opened[1], got_o1[comp], 0.0)
    for axis in range(3):
        accel[3 * ((reach - 1) // 2) + axis] = acc_own[axis : axis + 1]
    arrived = (got_e1[3], got_o1[3], got_e2[...], got_o2[...])
    for route, value, there in zip(ROUTES, arrived, opened):
        block = route_block(position, route, reach)
        for axis in range(3):
            accel[3 * block + axis] = jnp.where(there, value[axis : axis + 1], 0.0)


def f32(*shape):
    return jax.ShapeDtypeStruct(shape, F32)


def near(*shape):
    return pltpu.VMEM(shape, F32)


def held(value):
    return pltpu.with_memory_space_constraint(value, pltpu.VMEM)


def step(
    source, metric, base_velocity, drop_elem, drop_coord, drop_vel, drop_prop, drop_counts
):
    slabs = lax.axis_size("stream")
    cols = lax.axis_size("cross")
    lanes = source.shape[-1]
    reach, capacity = drop_elem.shape[2:]
    elem_z = metric.shape[-1]
    vmem = pl.BlockSpec(memory_space=pltpu.VMEM)
    smem = pl.BlockSpec(memory_space=pltpu.SMEM)
    tiles = jnp.asarray(table_tiles(lanes))
    stiff_w = jnp.asarray(lane_weights(STIFF, lanes, True))
    deriv_w = jnp.asarray(lane_weights(DERIV, lanes, False))
    to_lanes = np.zeros((lanes, lanes))
    to_lanes[:elem_z] = np.kron(np.eye(elem_z), np.ones((1, NODES)))
    spread_w = jnp.asarray(np.concatenate([to_lanes, to_lanes], 0), BF16)

    first, own, *routed = pl.pallas_call(
        lambda *refs: pack_kernel(cols, elem_z, *refs),
        out_shape=[near(NODES + 1, NODES, lanes)] + [near(2, NODES, capacity)] * 5,
        in_specs=[vmem] * 6 + [smem],
        out_specs=[vmem] * 6,
        scratch_shapes=[pltpu.VMEM((reach, 2, NODES, capacity), F32)],
        name="pack",
    )(
        source,
        metric,
        drop_elem.reshape(reach, 1, capacity),
        drop_coord.reshape(3 * reach, 1, capacity),
        drop_vel.reshape(3 * reach, 1, capacity),
        drop_prop,
        drop_counts,
    )
    whole = ("stream", "cross")

    routed = [
        lax.ppermute(value, whole, neighbours(slabs, cols, *route))
        for value, route in zip(routed, ROUTES)
    ]
    from_source = lax.ppermute(source, whole, swapped_bit(slabs, cols, 1))
    from_metric = lax.ppermute(metric, whole, swapped_bit(slabs, cols, 1))
    gathered = pl.pallas_call(
        near_kernel,
        out_shape=near(2, NODES + 1, NODES, lanes),
        in_specs=[vmem] * 3,
        out_specs=vmem,
        name="near_pair",
    )(held(first), held(from_source), held(from_metric))
    gathered = jnp.concatenate(
        [gathered, lax.ppermute(gathered, whole, swapped_bit(slabs, cols, 2))], 0
    )
    to_far = pl.pallas_call(
        far_kernel,
        out_shape=[near(F_COUNT, NODES, lanes)] * 2,
        in_specs=[vmem],
        out_specs=[vmem] * 2,
        name="far_records",
    )(held(gathered))
    pieces = [gathered] + [
        lax.ppermute(value, whole, neighbours(slabs, cols, DEPTH, odd, 1))
        for odd, value in enumerate(to_far)
    ]
    columns = [pieces]
    bit = 1
    while bit < cols:
        columns = columns + [
            [lax.ppermute(piece, "cross", column_pairs(cols, bit)) for piece in group]
            for group in columns
        ]
        bit *= 2
    flat = [piece for group in columns for piece in group]

    span = 2 * DEPTH - 1
    field = (cols, NODES, NODES, lanes)
    scratch_bytes = 4 * (9 * DEPTH + 1 + 5 * span) * int(np.prod(field))
    slots = 5 * capacity
    bases = pl.pallas_call(
        lambda *refs: basis_kernel(slabs, *refs),
        out_shape=[pltpu.VMEM((2 * lanes, slots), BF16)]
        + [near(5, NODES, NODES, capacity), near(5, NODES, capacity)],
        in_specs=[vmem] * 6,
        out_specs=[vmem] * 3,
        name="bases",
    )(held(tiles), held(own), *[held(value) for value in routed])
    pressure, momentum, face_even, *accels = pl.pallas_call(
        lambda *refs: main_kernel(slabs, cols, *refs),
        out_shape=[near(NODES, NODES, lanes), near(3, NODES, NODES, lanes)]
        + [near(3, NODES, lanes)]
        + [near(NODES, capacity)] * 5
        + [near(3, NODES, lanes)] * (cols > 2),
        in_specs=[vmem] * (13 + 3 * cols),
        out_specs=[vmem] * (8 + (cols > 2)),
        scratch_shapes=[
            pltpu.VMEM((4 * DEPTH - 1,) + field, F32),
            pltpu.VMEM((4 * DEPTH - 1, cols, NODES, lanes), F32),
            pltpu.VMEM((span,) + field, F32),
            pltpu.VMEM((span,) + field, F32),
            pltpu.VMEM((span,) + field, F32),
            pltpu.VMEM((span + 2,) + field, F32),
            pltpu.VMEM((5, span + 2, cols, NODES, lanes), F32),
            pltpu.VMEM((span + 2, cols, 2, NODES, lanes), F32),
        ],
        compiler_params=pltpu.CompilerParams(vmem_limit_bytes=2 * scratch_bytes + 2**23),
        name="sweeps_and_droplets",
    )(
        tiles,
        stiff_w,
        deriv_w,
        spread_w,
        *[held(piece) for piece in flat],
        base_velocity,
        held(own),
        *[held(value) for value in (*routed, *bases)],
    )
    acc_own, acc_e1, acc_o1, acc_e2, acc_o2, *face_odd = accels

    def returned(value, index, swap):
        pairs = neighbours(slabs, cols, *ROUTES[index], swap)
        return lax.ppermute(value, whole, pairs)

    got_e2 = returned(acc_e2, 2, 0)
    if cols == 2:
        swap = 1
        bundle = pl.pallas_call(
            bundle_kernel,
            out_shape=near(12, NODES, lanes),
            in_specs=[vmem] * 5,
            out_specs=vmem,
            name="bundle",
        )(*[held(value) for value in (momentum, face_even, acc_e1, acc_o1, acc_o2)])
        bundle = lax.ppermute(bundle, "cross", side_pairs(cols, 0))
        momentum, send_e1, send_o1, send_o2 = pl.pallas_call(
            exchange_kernel,
            out_shape=[near(3, NODES, NODES, lanes)]
            + [near(4, NODES, lanes)] * 2
            + [near(NODES, capacity)],
            in_specs=[vmem] * 2,
            out_specs=[vmem] * 4,
            name="cross_faces",
        )(held(momentum), held(bundle))
    else:
        swap = 0
        face_even = lax.ppermute(face_even, "cross", side_pairs(cols, 0))
        face_odd = lax.ppermute(face_odd[0], "cross", side_pairs(cols, 1))
        momentum, send_e1, send_o1 = pl.pallas_call(
            middle_kernel,
            out_shape=[near(3, NODES, NODES, lanes)] + [near(4, NODES, lanes)] * 2,
            in_specs=[vmem] * 5,
            out_specs=[vmem] * 3,
            name="cross_faces",
        )(*[held(value) for value in (momentum, face_even, face_odd, acc_e1, acc_o1)])
        send_o2 = acc_o2
    got_o2 = returned(send_o2, 3, swap)
    got_e1 = returned(send_e1, 0, swap)
    got_o1 = returned(send_o1, 1, swap)
    pressure, momentum, accel = pl.pallas_call(
        lambda *refs: last_kernel(slabs, reach, *refs),
        out_shape=[f32(NODES, NODES, lanes), f32(3, NODES, NODES, lanes), f32(3 * reach, 1, capacity)],
        in_specs=[vmem] * 7,
        out_specs=[vmem] * 3,
        name="stream_faces",
    )(*[held(value) for value in (pressure, momentum, got_e1, got_o1, acc_own, got_e2, got_o2)])
    return (pressure, momentum, accel.reshape(1, 1, reach, 3, capacity))


def solution(mesh):
    in_specs = (
        P("stream", "cross", None),
        P("stream", "cross", None),
        P(None, "stream", "cross", None),
        P("stream", "cross", None, None),
        P("stream", "cross", None, None, None),
        P("stream", "cross", None, None, None),
        P("stream", "cross", None, None, None),
        P("stream", "cross", None),
    )
    out_specs = (
        P("stream", "cross", None),
        P(None, "stream", "cross", None),
        P("stream", "cross", None, None, None),
    )
    return jax.shard_map(step, mesh=mesh, in_specs=in_specs, out_specs=out_specs, check_vma=False)
```
